32 devices in a mesh: ctx: 4 (over y, x), shard: 8 (over z, core).
Axes of the slice: x: 2, y: 2, z: 4, core: 2. Of those that a mesh axis runs over, the one named last changes fastest.
Arguments:
- tokens: bfloat16 [4096, 1024], P(('ctx', 'shard')), may hold values from -6 to 6
- w_query: bfloat16 [1024, 1024], P('shard'), may hold values from -0.625 to 0.625
- key_weight: bfloat16 [1024, 512], P('shard'), may hold values from -0.625 to 0.625
- value_weight: bfloat16 [1024, 512], P('shard'), may hold values from -0.1875 to 0.1875
- w_out: bfloat16 [1024, 1024], P('shard'), may hold values from -6 to 6
- norm_attn: bfloat16 [1024], P('shard'), may hold values from 0.5 to 1.5
- norm_ffn: bfloat16 [1024], P('shard'), may hold values from 0.5 to 1.5
- w_router: bfloat16 [1024, 16], P('shard'), may hold values from -0.09375 to 0.09375
- w_gate: bfloat16 [1024, 16, 512], P('shard', 'ctx'), may hold values from -0.1875 to 0.1875
- w_up: bfloat16 [1024, 16, 512], P('shard', 'ctx'), may hold values from -0.1875 to 0.1875
- w_down: bfloat16 [512, 16, 1024], P('shard', 'ctx'), may hold values from -6 to 6
- cotangent: bfloat16 [4096, 1024], P(('ctx', 'shard')), may hold values from -6 to 6
- choices: int32 [4096, 8], P(('ctx', 'shard')), may hold values from 0 to 15, all different within a row
- priority: int32 [4096, 8], P(('ctx', 'shard')), may hold values from 0 to 1023, as said below
Outputs:
- block_out: bfloat16 [4096, 1024], P(('ctx', 'shard'))
- grad_tokens: float32 [4096, 1024], P(('ctx', 'shard'))
- grad_query: float32 [1024, 1024], P(('ctx', 'shard'))
- grad_key: float32 [1024, 512], P(('ctx', 'shard'))
- grad_value: float32 [1024, 512], P(('ctx', 'shard'))
- grad_out: float32 [1024, 1024], P(('ctx', 'shard'))
- grad_norm_attn: float32 [1024], P(('ctx', 'shard'))
- grad_norm_ffn: float32 [1024], P(('ctx', 'shard'))
- grad_router: float32 [1024, 16], P(('ctx', 'shard'))
- grad_gate: float32 [1024, 16, 512], P('shard', 'ctx')
- grad_up: float32 [1024, 16, 512], P('shard', 'ctx')
- grad_down: float32 [512, 16, 1024], P('shard', 'ctx')
The draws below stay inside these ranges and needn't reach their ends.
Inputs may be any that keep to these rules, and one draw needn't show every extreme that they name: `choices`: each row names 8 different experts, and every expert is named by some row. `priority`: within each group of 128 consecutive rows the 1024 entries are 0 to 1023, each once.
All inputs are finite; a program needn't handle non-finite values.
Results may differ from the reference program's by a relative error of at most 0.025.
Values may be sent and summed in bfloat16 or wider, within the bound.
No kernel may reach another device: no remote copies, remote signals or barrier semaphores. Data moves between devices by JAX's collectives and lax.ppermute only.
A program may use at most 192 MiB of HBM per device.

```python
import math
import jax
import jax.numpy as jnp
from jax import lax

MODEL_WIDTH = 1024
QUERY_HEADS = 16
KEY_VALUE_HEADS = 8
HEAD_SIZE = 64
FF = 512
TOPK = 8
TOK_DEV = 128
EXPERTS = 16
SEQUENCE_TOKENS = 4096
CAP = 80


def draw_priority(key, part):
    group_count = SEQUENCE_TOKENS // TOK_DEV
    pair_count = TOK_DEV * TOPK
    group_keys = jax.random.split(jax.random.fold_in(key, 17), group_count)

    def one_order(one_key):
        return jax.random.permutation(one_key, pair_count)
    orders = jax.vmap(one_order)(group_keys)
    return orders.reshape(SEQUENCE_TOKENS, TOPK).astype(jnp.int32)


def raised(entries, stream_key, source, target, parts, factor):
    def block_of(axis_at):
        return (jnp.arange(entries.shape[axis_at]) // (entries.shape[axis_at] // parts)).reshape((-1,) + (1,) * (entries.ndim - 1 - axis_at))

    near = jax.random.permutation(stream_key, parts)[block_of(target)]
    second = (block_of(target) + parts // 2) % parts
    return jnp.where((block_of(source) == near) | (block_of(source) == second), factor * entries, entries)


def levels(key, shape, shards, least, top_value):
    gain = 1.0
    for dim, blocks in shards:
        steps = jax.random.uniform(jax.random.fold_in(jax.random.fold_in(key, 6), dim), (blocks,), jnp.float32, least / len(shards), top_value / len(shards))
        gain = gain * jnp.repeat(jnp.exp(steps), shape[dim] // blocks).reshape((-1,) + (1,) * (len(shape) - 1 - dim))
    return gain


def distinct(stream_key, rows, count, top, lift):
    ranking = jax.random.permutation(jax.random.fold_in(stream_key, 1), count)
    pull = ranking
    for power in range(3):
        pull = pull * pull // count
    pull = pull * lift // count
    chance = jax.random.randint(jax.random.fold_in(stream_key, 2), (rows, count), 0, 4096) + pull
    sure = jax.random.permutation(jax.random.fold_in(stream_key, 3), rows)[jnp.arange(count) % rows]
    chance = jnp.where(jnp.arange(rows)[:, None] == sure[None, :], 1 << 14, chance)
    score = chance * count + jnp.arange(count)
    return lax.top_k(score.astype(jnp.int32), top)[1].astype(jnp.int32)


def centred(key, extent, spread, bound, cuts=(), kind=jnp.bfloat16):
    gain = levels(key, extent, cuts, -0.22, 0.18) if cuts else 1.0
    array = jax.random.normal(key, extent, jnp.float32) * spread * gain
    return jnp.minimum(jnp.maximum(array, -bound), bound).astype(kind)


def noise_with(key, dims, deviation, limit, pieces, heavy, kind=jnp.bfloat16):
    result = deviation * jax.random.normal(key, dims, jnp.float32)
    if pieces:
        result = result * levels(key, dims, pieces, -0.22, 0.18)
    return jnp.clip(raised(result, jax.random.fold_in(key, 3), *heavy), -limit, limit).astype(kind)


def setup_inputs(seed: int = 0) -> dict:
    splits = jax.random.split(jax.random.key(seed), 15)
    return {
        "tokens": noise_with(splits[0], (SEQUENCE_TOKENS, MODEL_WIDTH), 1.0, 6.0, ((0, 32),), (0, 1, 32, 2.75)),
        "w_query": centred(splits[1], (MODEL_WIDTH, QUERY_HEADS * HEAD_SIZE), (MODEL_WIDTH // 10) ** -0.5, 0.625, ((0, 8),)),
        "key_weight": centred(splits[2], (MODEL_WIDTH, KEY_VALUE_HEADS * HEAD_SIZE), (MODEL_WIDTH // 10) ** -0.5, 0.625, ((0, 8),)),
        "value_weight": centred(splits[3], (MODEL_WIDTH, KEY_VALUE_HEADS * HEAD_SIZE), MODEL_WIDTH ** -0.5, 0.1875, ((0, 8),)),
        "w_out": centred(splits[4], (QUERY_HEADS * HEAD_SIZE, MODEL_WIDTH), 1.0, 6.0, ((0, 8),)),
        "norm_attn": jnp.clip(1.0 + 0.1 * jax.random.normal(splits[5], (MODEL_WIDTH,), jnp.float32), 0.5, 1.5).astype(jnp.bfloat16),
        "norm_ffn": jnp.clip(1.0 + 0.1 * jax.random.normal(splits[6], (MODEL_WIDTH,), jnp.float32), 0.5, 1.5).astype(jnp.bfloat16),
        "w_router": centred(splits[7], (MODEL_WIDTH, EXPERTS), (4 * MODEL_WIDTH) ** -0.5, 0.09375, ((0, 8),)),
        "w_gate": centred(splits[8], (MODEL_WIDTH, EXPERTS, FF), MODEL_WIDTH ** -0.5, 0.1875, ((0, 8), (1, 4))),
        "w_up": centred(splits[9], (MODEL_WIDTH, EXPERTS, FF), MODEL_WIDTH ** -0.5, 0.1875, ((0, 8), (1, 4))),
        "w_down": centred(splits[10], (FF, EXPERTS, MODEL_WIDTH), 1.0, 6.0, ((0, 8), (1, 4))),
        "cotangent": centred(splits[11], (SEQUENCE_TOKENS, MODEL_WIDTH), 1.0, 6.0, ((0, 32),)),
        "choices": distinct(splits[12], SEQUENCE_TOKENS, EXPERTS, TOPK, 4096),
        "priority": draw_priority(jax.random.fold_in(splits[14], 71), 0),
    }


NORM_EPS = 1e-06
RESIDUAL_SCALE = 0.22
SCORE_SCALE = 0.015625
ROPE_BASE = 10000.0
PRECISE = lax.Precision.HIGHEST
MASKED = -1e+30

@jax.custom_vjp
def lowered_precision(v):
    return lax.optimization_barrier(v.astype(jnp.bfloat16)).astype(jnp.float32)

@jax.custom_vjp
def lowered_backward(v):
    return v

def low_keep(v):
    return (lowered_precision(v), None)

def low_pass(kept, grad):
    return (grad,)

def back_keep(v):
    return (v, None)

def back_low(kept, grad):
    return (lowered_precision(grad),)
lowered_precision.defvjp(low_keep, low_pass)
lowered_backward.defvjp(back_keep, back_low)

def rotary_tables(total):
    halfway = HEAD_SIZE // 2
    frequency = jnp.exp(jnp.arange(halfway, dtype=jnp.float32) * (-2.0 * math.log(ROPE_BASE) / HEAD_SIZE))
    angles = jnp.arange(total, dtype=jnp.float32)[:, None] * frequency[None, :]
    return (jnp.cos(angles), jnp.sin(angles))

def apply_rotation(vectors, cosine_table, sine_lookup, head_count):
    row_count = vectors.shape[0]
    halfway = HEAD_SIZE // 2
    shaped = vectors.reshape(row_count, head_count, HEAD_SIZE)
    front_half = shaped[:, :, :halfway]
    behind = shaped[:, :, halfway:]
    cosine_wide = cosine_table[:, None, :]
    sine_wide = sine_lookup[:, None, :]
    turned = jnp.concatenate([front_half * cosine_wide - behind * sine_wide, behind * cosine_wide + front_half * sine_wide], axis=2)
    return turned.reshape(row_count, head_count * HEAD_SIZE)

def rms_scale(value_rows):
    return lax.rsqrt(lax.optimization_barrier(jnp.mean(value_rows * value_rows, axis=1, keepdims=True)) + NORM_EPS)

def slot_targets(choices, priority):
    group_count = SEQUENCE_TOKENS // TOK_DEV
    pair_count = TOK_DEV * TOPK
    expert_rows = choices.reshape(group_count, pair_count)
    rank_rows = priority.reshape(group_count, pair_count)

    def one_group(expert_row, rank_row):
        by_rank = jnp.zeros((pair_count,), jnp.int32).at[rank_row].set(expert_row)
        choice_table = (by_rank[:, None] == jnp.arange(EXPERTS, dtype=jnp.int32)[None, :]).astype(jnp.int32)
        earlier = jnp.cumsum(choice_table, axis=0) - choice_table
        slot_taken = earlier[rank_row, expert_row]
        return jnp.where(slot_taken < CAP, expert_row * CAP + slot_taken, EXPERTS * CAP).astype(jnp.int32)
    return jax.vmap(one_group)(expert_rows, rank_rows)

def reference(tokens, w_query, key_weight, value_weight, w_out, norm_attn, norm_ffn, w_router, w_gate, w_up, w_down, cotangent, choices, priority):
    destination = slot_targets(choices, priority)
    cosine_table, sine_lookup = rotary_tables(SEQUENCE_TOKENS)
    choice_table = (choices[:, :, None] == jnp.arange(EXPERTS, dtype=jnp.int32)[None, None, :]).astype(jnp.float32)
    group_count = SEQUENCE_TOKENS // TOK_DEV
    block_rows = 512
    block_count = SEQUENCE_TOKENS // block_rows
    repeat_factor = QUERY_HEADS // KEY_VALUE_HEADS

    def forward(inputs, query_w, key_w, value_w, out_w, gain_attn, gain_ffn, router_w, gate_w, up_w, down_w):
        normed = lowered_precision(inputs * rms_scale(inputs) * gain_attn[None, :])
        query_lin = lowered_backward(jnp.dot(normed, query_w, precision=PRECISE))
        key_linear = lowered_backward(jnp.dot(normed, key_w, precision=PRECISE))
        value_rows = lowered_backward(lowered_precision(jnp.dot(normed, value_w, precision=PRECISE)))
        queries = lowered_backward(lowered_precision(apply_rotation(query_lin, cosine_table, sine_lookup, QUERY_HEADS)))
        key_rotated = lowered_precision(apply_rotation(key_linear, cosine_table, sine_lookup, KEY_VALUE_HEADS))
        keys_repeated = lowered_backward(jnp.repeat(key_rotated.reshape(SEQUENCE_TOKENS, KEY_VALUE_HEADS, HEAD_SIZE), repeat_factor, axis=1))
        values_repeated = lowered_backward(jnp.repeat(value_rows.reshape(SEQUENCE_TOKENS, KEY_VALUE_HEADS, HEAD_SIZE), repeat_factor, axis=1))
        key_place = jnp.arange(SEQUENCE_TOKENS, dtype=jnp.int32)

        def attention_block(packed):
            query_part, block_start = packed
            scores = SCORE_SCALE * jnp.einsum('qhd,khd->hqk', query_part, keys_repeated, precision=PRECISE)
            query_place = block_start + jnp.arange(block_rows, dtype=jnp.int32)
            visible = key_place[None, None, :] <= query_place[None, :, None]
            scores = lowered_backward(jnp.where(visible, scores, MASKED))
            probability = lowered_precision(jax.nn.softmax(scores, axis=2))
            return jnp.einsum('hqk,khd->qhd', probability, values_repeated, precision=PRECISE)
        query_blocks = queries.reshape(block_count, block_rows, QUERY_HEADS, HEAD_SIZE)
        block_starts = jnp.arange(block_count, dtype=jnp.int32) * block_rows
        attended = lax.map(jax.checkpoint(attention_block), (query_blocks, block_starts))
        attended = lowered_backward(lowered_precision(attended.reshape(SEQUENCE_TOKENS, QUERY_HEADS * HEAD_SIZE)))
        branch = lowered_backward(jnp.dot(attended, out_w, precision=PRECISE))
        middle = inputs + RESIDUAL_SCALE * branch
        normed_ffn = middle * rms_scale(middle) * gain_ffn[None, :]
        logits = jnp.dot(normed_ffn, router_w, precision=PRECISE)
        chosen = jnp.einsum('tke,te->tk', choice_table, logits, precision=PRECISE)
        gate_weights = jax.nn.softmax(chosen, axis=1)

        def expert_group(packed):
            normed_rows, gate_rows, target = packed
            pair_rows = lowered_backward(lowered_precision(jnp.repeat(normed_rows, TOPK, axis=0)))
            buffer = jnp.zeros((EXPERTS * CAP + 1, MODEL_WIDTH), jnp.float32).at[target].add(pair_rows)
            buffer = buffer[:EXPERTS * CAP].reshape(EXPERTS, CAP, MODEL_WIDTH)
            gate_act = lowered_backward(jnp.einsum('ecd,def->ecf', buffer, gate_w, precision=PRECISE))
            up_act = lowered_backward(jnp.einsum('ecd,def->ecf', buffer, up_w, precision=PRECISE))
            hidden = lowered_precision(jax.nn.silu(gate_act) * up_act)
            expert_out = lowered_backward(lowered_precision(jnp.einsum('ecf,fed->ecd', hidden, down_w, precision=PRECISE)))
            padded = jnp.concatenate([expert_out.reshape(EXPERTS * CAP, MODEL_WIDTH), jnp.zeros((1, MODEL_WIDTH), jnp.float32)], axis=0)
            returned = padded[target].reshape(TOK_DEV, TOPK, MODEL_WIDTH)
            return lax.optimization_barrier(jnp.sum(gate_rows[:, :, None] * returned, axis=1))
        expert_mix = lax.map(jax.checkpoint(expert_group), (normed_ffn.reshape(group_count, TOK_DEV, MODEL_WIDTH), gate_weights.reshape(group_count, TOK_DEV, TOPK), destination))
        return middle + RESIDUAL_SCALE * expert_mix.reshape(SEQUENCE_TOKENS, MODEL_WIDTH)
    output, pullback = jax.vjp(forward, tokens.astype(jnp.float32), w_query.astype(jnp.float32), key_weight.astype(jnp.float32), value_weight.astype(jnp.float32), w_out.astype(jnp.float32), norm_attn.astype(jnp.float32), norm_ffn.astype(jnp.float32), w_router.astype(jnp.float32), w_gate.astype(jnp.float32), w_up.astype(jnp.float32), w_down.astype(jnp.float32))
    grads = pullback(cotangent.astype(jnp.float32))
    return (output.astype(jnp.bfloat16), grads[0], grads[1], grads[2], grads[3], grads[4], grads[5], grads[6], grads[7], grads[8], grads[9], grads[10])
```

```python
import functools
import math

import jax
import jax.numpy as jnp
from jax import lax
from jax.experimental import pallas as pl
from jax.experimental.pallas import tpu as pltpu
from jax.sharding import PartitionSpec as P

MODEL_WIDTH = 1024
QUERY_HEADS = 16
KEY_VALUE_HEADS = 8
HEAD_SIZE = 64
FF = 512
TOPK = 8

NORM_EPS = 1e-06
RESIDUAL_SCALE = 0.22
SCORE_SCALE = 0.015625
ROPE_BASE = 10000.0
PRECISE = lax.Precision.HIGHEST
MASKED = -1e30
UNCHOSEN = 1 << 20
LANES = 128

F32 = jnp.float32
BF16 = jnp.bfloat16


def dot(a, b, dims=((1,), (0,))):
    return lax.dot_general(a, b, (dims, ((), ())), preferred_element_type=F32)


def rotary_tables(positions):
    halfway = HEAD_SIZE // 2
    frequency = jnp.exp(
        jnp.arange(halfway, dtype=F32) * (-2.0 * math.log(ROPE_BASE) / HEAD_SIZE)
    )
    angles = frequency[:, None] * positions.astype(F32)[None, :]
    return (jnp.cos(angles), jnp.sin(angles))


def rotate(vectors, cosine, sine):
    rows, count = vectors.shape
    shaped = vectors.reshape(rows // HEAD_SIZE, 2, HEAD_SIZE // 2, count)
    front, behind = shaped[:, 0], shaped[:, 1]
    turned = jnp.stack(
        [front * cosine - behind * sine, behind * cosine + front * sine], axis=1
    )
    return turned.reshape(rows, count)


def rms_scale(value_rows):
    return lax.rsqrt(jnp.mean(value_rows * value_rows, axis=1, keepdims=True) + NORM_EPS)


def norm_back(upward, inputs, inverse_rms, gain_vector):
    weighted = upward * gain_vector[None, :]
    cubed = inverse_rms * inverse_rms * inverse_rms
    return inverse_rms * weighted - inputs * cubed * jnp.mean(
        weighted * inputs, axis=1, keepdims=True
    )


def attention_blocks(rows):
    return min(512, rows)


def attend_kernel(c_ref, q_ref, *refs, ctx_count, heads, rows, block, tile):
    kv_refs = refs[:ctx_count]
    out_ref, wide_ref, log_ref = refs[ctx_count : ctx_count + 3]
    natural, peak, total, acc = refs[ctx_count + 3 :]
    step = pl.program_id(0)
    mine = c_ref[0]

    @pl.when(step == 0)
    def _():
        for k in range(ctx_count):

            @pl.when(mine >= k)
            def _(k=k):
                natural[k] = kv_refs[k][...].T

    zeros = jnp.zeros((HEAD_SIZE, block), BF16)
    wide_q = [
        jnp.concatenate([q_ref[h * HEAD_SIZE : (h + 1) * HEAD_SIZE, :], zeros], axis=0)
        for h in range(heads)
    ]
    for h in range(heads):
        peak[h] = jnp.full((1, block), MASKED, F32)
        total[h] = jnp.zeros((1, block), F32)
        acc[h] = jnp.zeros((HEAD_SIZE, block), F32)

    def visit(k, start, masked):
        keys = natural[k, pl.ds(start, block), :]
        values = kv_refs[k][HEAD_SIZE:, pl.ds(start, block)]
        for h in range(heads):
            scores = dot(keys, wide_q[h])
            if masked:
                place = lax.broadcasted_iota(jnp.int32, (block, block), 0)
                query = lax.broadcasted_iota(jnp.int32, (block, block), 1)
                scores = jnp.where(place <= query, scores, MASKED)
            old = peak[h]
            new = jnp.maximum(old, jnp.max(scores, axis=0, keepdims=True))
            shrink = jnp.exp(old - new)
            weights = jnp.exp(scores - new)
            peak[h] = new
            total[h] = total[h] * shrink + jnp.sum(weights, axis=0, keepdims=True)
            acc[h] = acc[h] * shrink + dot(values, weights.astype(BF16))

    def full(k):
        def body(j, carry):
            visit(k, pl.multiple_of(j * block, block), False)
            return carry

        return body

    for k in range(1, ctx_count):

        @pl.when(mine >= k)
        def _(k=k):
            lax.fori_loop(0, rows // block, full(k), 0)

    lax.fori_loop(0, step, full(0), 0)
    visit(0, pl.multiple_of(step * block, block), True)
    for h in range(heads):
        result = acc[h] / total[h]
        at = slice(h * HEAD_SIZE, (h + 1) * HEAD_SIZE)
        wide_ref[at, :] = result
        log_ref[h : h + 1, :] = peak[h] + jnp.log(total[h])
        for j in range(block // tile):
            out_ref[j, at, :] = result[:, j * tile : (j + 1) * tile].astype(BF16)


def attend(queries, key_values, ctx_index, tile):
    width, rows = queries.shape
    heads = width // HEAD_SIZE
    ctx_count = len(key_values)
    block = attention_blocks(rows)
    kv_width = key_values[0].shape[0]
    whole = pl.BlockSpec((kv_width, rows), lambda i, c: (0, 0))
    return pl.pallas_call(
        functools.partial(
            attend_kernel, ctx_count=ctx_count, heads=heads, rows=rows, block=block, tile=tile
        ),
        grid_spec=pltpu.PrefetchScalarGridSpec(
            num_scalar_prefetch=1,
            grid=(rows // block,),
            in_specs=[pl.BlockSpec((width, block), lambda i, c: (0, i))] + [whole] * ctx_count,
            out_specs=[
                pl.BlockSpec((block // tile, width, tile), lambda i, c: (i, 0, 0)),
                pl.BlockSpec((width, block), lambda i, c: (0, i)),
                pl.BlockSpec((heads, block), lambda i, c: (0, i)),
            ],
            scratch_shapes=[
                pltpu.VMEM((ctx_count, rows, kv_width), BF16),
                pltpu.VMEM((heads, 1, block), F32),
                pltpu.VMEM((heads, 1, block), F32),
                pltpu.VMEM((heads, HEAD_SIZE, block), F32),
            ],
        ),
        out_shape=[
            jax.ShapeDtypeStruct((rows // tile, width, tile), BF16),
            jax.ShapeDtypeStruct((width, rows), F32),
            jax.ShapeDtypeStruct((heads, rows), F32),
        ],
        compiler_params=pltpu.CompilerParams(
            dimension_semantics=("arbitrary",), vmem_limit_bytes=48 << 20
        ),
        cost_estimate=pl.CostEstimate(
            flops=4 * width * rows * rows * ctx_count // 2,
            transcendentals=heads * rows * rows * ctx_count // 2,
            bytes_accessed=2 * ctx_count * rows * kv_width,
        ),
        name="attend",
    )(ctx_index, queries, *key_values)


def attend_back_kernel(
    c_ref, q_ref, grad_ref, wide_ref, log_ref, *refs, ctx_count, heads, rows, block, tile
):
    kv_refs = refs[:ctx_count]
    gq_ref = refs[ctx_count]
    gkv_refs = refs[ctx_count + 1 : 2 * ctx_count + 1]
    natural, sums, gq_acc = refs[2 * ctx_count + 1 :]
    step = pl.program_id(0)
    last = pl.num_programs(0) - 1
    mine = c_ref[0]

    @pl.when(step == 0)
    def _():
        for k in range(ctx_count):

            @pl.when(mine >= k)
            def _(k=k):
                natural[k] = kv_refs[k][...].T
                sums[k] = jnp.zeros_like(sums[k])

    zeros = jnp.zeros((HEAD_SIZE, block), BF16)
    wide_q, wide_g, tall_q, tall_g, delta, level = [], [], [], [], [], []
    for h in range(heads):
        at = slice(h * HEAD_SIZE, (h + 1) * HEAD_SIZE)
        grad = jnp.concatenate([grad_ref[j, at, :] for j in range(block // tile)], axis=1)
        q_part = jnp.concatenate([q_ref[at, :], zeros], axis=0)
        g_part = jnp.concatenate([zeros, grad], axis=0)
        wide_q.append(q_part)
        wide_g.append(g_part)
        tall_q.append(q_part.T)
        tall_g.append(g_part.T)
        delta.append(jnp.sum(grad.astype(F32) * wide_ref[at, :], axis=0, keepdims=True))
        level.append(log_ref[h : h + 1, :])
        gq_acc[h] = jnp.zeros((HEAD_SIZE, block), F32)

    def visit(k, start, masked):
        both = natural[k, pl.ds(start, block), :]
        keys = kv_refs[k][:HEAD_SIZE, pl.ds(start, block)]
        add = None
        for h in range(heads):
            scores = dot(both, wide_q[h])
            if masked:
                place = lax.broadcasted_iota(jnp.int32, (block, block), 0)
                query = lax.broadcasted_iota(jnp.int32, (block, block), 1)
                scores = jnp.where(place <= query, scores, MASKED)
            weights = jnp.exp(scores - level[h])
            grad_probs = dot(both, wide_g[h])
            grad_scores = (weights * (grad_probs - delta[h])).astype(BF16)
            part = dot(grad_scores, tall_q[h]) + dot(weights.astype(BF16), tall_g[h])
            add = part if add is None else add + part
            gq_acc[h] += dot(keys, grad_scores)
        sums[k, pl.ds(start, block), :] += add

    def full(k):
        def body(j, carry):
            visit(k, pl.multiple_of(j * block, block), False)
            return carry

        return body

    for k in range(1, ctx_count):

        @pl.when(mine >= k)
        def _(k=k):
            lax.fori_loop(0, rows // block, full(k), 0)

    lax.fori_loop(0, step, full(0), 0)
    visit(0, pl.multiple_of(step * block, block), True)
    for h in range(heads):
        gq_ref[h * HEAD_SIZE : (h + 1) * HEAD_SIZE, :] = SCORE_SCALE * gq_acc[h]

    @pl.when(step == last)
    def _():
        gkv_refs[0][...] = sums[0]
        for k in range(1, ctx_count):

            @pl.when(mine >= k)
            def _(k=k):
                gkv_refs[k][...] = sums[k].astype(BF16)

            @pl.when(mine < k)
            def _(k=k):
                gkv_refs[k][...] = jnp.zeros((rows, sums.shape[2]), BF16)


def attend_back(queries, grads, wide, level, key_values, ctx_index):
    width, rows = queries.shape
    heads = width // HEAD_SIZE
    ctx_count = len(key_values)
    block = attention_blocks(rows)
    tile = grads.shape[2]
    kv_width = key_values[0].shape[0]
    whole = pl.BlockSpec((kv_width, rows), lambda i, c: (0, 0))
    tall = pl.BlockSpec((rows, kv_width), lambda i, c: (0, 0))
    return pl.pallas_call(
        functools.partial(
            attend_back_kernel, ctx_count=ctx_count, heads=heads, rows=rows, block=block, tile=tile
        ),
        grid_spec=pltpu.PrefetchScalarGridSpec(
            num_scalar_prefetch=1,
            grid=(rows // block,),
            in_specs=[
                pl.BlockSpec((width, block), lambda i, c: (0, i)),
                pl.BlockSpec((block // tile, width, tile), lambda i, c: (i, 0, 0)),
                pl.BlockSpec((width, block), lambda i, c: (0, i)),
                pl.BlockSpec((heads, block), lambda i, c: (0, i)),
            ]
            + [whole] * ctx_count,
            out_specs=[pl.BlockSpec((width, block), lambda i, c: (0, i))] + [tall] * ctx_count,
            scratch_shapes=[
                pltpu.VMEM((ctx_count, rows, kv_width), BF16),
                pltpu.VMEM((ctx_count, rows, kv_width), F32),
                pltpu.VMEM((heads, HEAD_SIZE, block), F32),
            ],
        ),
        out_shape=[jax.ShapeDtypeStruct((width, rows), F32)]
        + [
            jax.ShapeDtypeStruct((rows, kv_width), F32 if k == 0 else BF16)
            for k in range(ctx_count)
        ],
        compiler_params=pltpu.CompilerParams(
            dimension_semantics=("arbitrary",), vmem_limit_bytes=56 << 20
        ),
        cost_estimate=pl.CostEstimate(
            flops=10 * width * rows * rows * ctx_count // 2,
            transcendentals=heads * rows * rows * ctx_count // 2,
            bytes_accessed=4 * ctx_count * rows * kv_width,
        ),
        name="attend_back",
    )(ctx_index, queries, grads, wide, level, *key_values)


def expert_kernel(c_ref, *refs, ctx_count, experts, tile, rows, down_rows):
    shards = refs[2 * ctx_count].shape[0]
    x_refs, u_refs = refs[:ctx_count], refs[ctx_count : 2 * ctx_count]
    w_ref = refs[2 * ctx_count]
    gin_refs = refs[2 * ctx_count + 1 : 3 * ctx_count + 1]
    mix_refs = refs[3 * ctx_count + 1 : 4 * ctx_count + 1]
    grad_ref = refs[4 * ctx_count + 1]
    (x_all, x_turned, u_all, share, gin_acc, mix_acc, dots, hid, g_out, g_gate, g_up) = refs[
        4 * ctx_count + 2 :
    ]
    e = pl.program_id(0)
    last = pl.num_programs(0) - 1
    width = u_all.shape[1]
    count = ctx_count * tile
    chunk = min(2 * tile, count)
    column = c_ref[0] * experts + e

    @pl.when(e == 0)
    def _():
        for k in range(ctx_count):
            at = slice(k * tile, (k + 1) * tile)
            part = x_refs[k][:, :width]
            x_all[at, :] = part
            x_turned[:, at] = part.T
            u_all[at, :] = u_refs[k][...]
            share[at, :] = x_refs[k][:, width:].astype(F32)
        gin_acc[...] = jnp.zeros_like(gin_acc)
        mix_acc[...] = jnp.zeros_like(mix_acc)
        dots[...] = jnp.zeros_like(dots)

    lane = lax.broadcasted_iota(jnp.int32, (chunk, LANES), 1)
    picked = (lane == column) | (lane == column + LANES // 2)
    down = 2 * rows

    def gate_matrix():
        return w_ref[:, 0, 0:rows, :].reshape(shards * rows, FF)

    def up_matrix():
        return w_ref[:, 0, rows : 2 * rows, :].reshape(shards * rows, FF)

    def down_matrix(half):
        at = down + half * down_rows
        return w_ref[:, 0, at : at + down_rows, :].reshape(FF, FF)

    def one_chunk(j, carry):
        at = pl.ds(pl.multiple_of(j * chunk, chunk), chunk)
        x = x_all[at, :]
        gate = dot(x, gate_matrix())
        up = dot(x, up_matrix())
        sig = jax.nn.sigmoid(gate)
        silu = gate * sig
        hidden = (silu * up).astype(BF16)
        hid[at, :] = hidden
        weight = jnp.sum(jnp.where(picked, share[at, :], 0.0), axis=1, keepdims=True)
        upstream = u_all[at, :].astype(F32) * RESIDUAL_SCALE
        down_grad = (upstream * weight).astype(BF16)
        g_out[at, :] = down_grad
        gathered = jnp.zeros((chunk, 1), F32)
        grad_hidden = jnp.zeros((chunk, FF), F32)
        for half in range(width // FF):
            cols = slice(half * FF, (half + 1) * FF)
            matrix = down_matrix(half)
            made = dot(hidden, matrix).astype(BF16).astype(F32)
            mix_acc[at, cols] += weight * made
            gathered += jnp.sum(upstream[:, cols] * made, axis=1, keepdims=True)
            grad_hidden += dot(down_grad[:, cols], matrix, ((1,), (1,)))
        dots[at, :] += jnp.where(lane == column, gathered, 0.0)
        grad_gate = (grad_hidden * up * sig * (1.0 + gate * (1.0 - sig))).astype(BF16)
        grad_up = (grad_hidden * silu).astype(BF16)
        g_gate[at, :] = grad_gate
        g_up[at, :] = grad_up
        gin_acc[at, :] += dot(grad_gate, gate_matrix(), ((1,), (1,))) + dot(
            grad_up, up_matrix(), ((1,), (1,))
        )
        return carry

    lax.fori_loop(0, count // chunk, one_chunk, 0)
    grad_ref[:, 0, 0:rows, :] = (
        dot(x_turned[...], g_gate[...]).astype(BF16).reshape(shards, rows, FF)
    )
    grad_ref[:, 0, rows : 2 * rows, :] = (
        dot(x_turned[...], g_up[...]).astype(BF16).reshape(shards, rows, FF)
    )
    hid_turned = hid[...].T
    for half in range(width // FF):
        at = down + half * down_rows
        grad_ref[:, 0, at : at + down_rows, :] = (
            dot(hid_turned, g_out[:, half * FF : (half + 1) * FF])
            .astype(BF16)
            .reshape(shards, down_rows, FF)
        )

    @pl.when(e == last)
    def _():
        for k in range(ctx_count):
            at = slice(k * tile, (k + 1) * tile)
            gin_refs[k][:, :width] = gin_acc[at, :].astype(BF16)
            high = dots[at, :].astype(BF16)
            gin_refs[k][:, width : width + LANES] = high
            gin_refs[k][:, width + LANES :] = (dots[at, :] - high.astype(F32)).astype(BF16)
            mix_refs[k][...] = mix_acc[at, :].astype(BF16)


def run_experts(x_parts, u_parts, weights, ctx_index):
    ctx_count = len(x_parts)
    tile, width = u_parts[0].shape
    shards, experts, all_rows, _ = weights.shape
    rows = width // shards
    down_rows = FF // shards
    count = ctx_count * tile
    flat = lambda *shape: pl.BlockSpec(shape, lambda e, c: (0,) * len(shape))
    by_expert = pl.BlockSpec((shards, 1, all_rows, FF), lambda e, c: (0, e, 0, 0))
    out = pl.pallas_call(
        functools.partial(
            expert_kernel,
            ctx_count=ctx_count,
            experts=experts,
            tile=tile,
            rows=rows,
            down_rows=down_rows,
        ),
        grid_spec=pltpu.PrefetchScalarGridSpec(
            num_scalar_prefetch=1,
            grid=(experts,),
            in_specs=[flat(tile, width + LANES)] * ctx_count
            + [flat(tile, width)] * ctx_count
            + [by_expert],
            out_specs=[flat(tile, width + 2 * LANES)] * ctx_count
            + [flat(tile, width)] * ctx_count
            + [by_expert],
            scratch_shapes=[
                pltpu.VMEM((count, width), BF16),
                pltpu.VMEM((width, count), BF16),
                pltpu.VMEM((count, width), BF16),
                pltpu.VMEM((count, LANES), F32),
                pltpu.VMEM((count, width), F32),
                pltpu.VMEM((count, width), F32),
                pltpu.VMEM((count, LANES), F32),
                pltpu.VMEM((count, FF), BF16),
                pltpu.VMEM((count, width), BF16),
                pltpu.VMEM((count, FF), BF16),
                pltpu.VMEM((count, FF), BF16),
            ],
        ),
        out_shape=[jax.ShapeDtypeStruct((tile, width + 2 * LANES), BF16)] * ctx_count
        + [jax.ShapeDtypeStruct((tile, width), BF16)] * ctx_count
        + [jax.ShapeDtypeStruct(weights.shape, BF16)],
        compiler_params=pltpu.CompilerParams(
            dimension_semantics=("arbitrary",), vmem_limit_bytes=60 << 20
        ),
        cost_estimate=pl.CostEstimate(
            flops=18 * experts * count * width * FF,
            transcendentals=experts * count * FF,
            bytes_accessed=4 * shards * experts * all_rows * FF,
        ),
        name="experts",
    )(ctx_index, *x_parts, *u_parts, weights)
    return out[:ctx_count], out[ctx_count : 2 * ctx_count], out[2 * ctx_count]


def send_ctx(value, by):
    count = lax.axis_size("ctx")
    return lax.ppermute(value, "ctx", [(i, (i + by) % count) for i in range(count)])


def from_ctx(value):
    return [value] + [send_ctx(value, k) for k in range(1, lax.axis_size("ctx"))]


def to_ctx(parts):
    total = parts[0].astype(F32)
    for k in range(1, len(parts)):
        total = total + send_ctx(parts[k], -k).astype(F32)
    return total


def scatter_ctx(value):
    count = lax.axis_size("ctx")
    mine = lax.axis_index("ctx")
    rows = value.shape[0] // count
    parts = [
        lax.dynamic_slice_in_dim(value, ((mine - k) % count) * rows, rows, 0) for k in range(count)
    ]
    return to_ctx(parts)


def gather_shard(value):
    count = lax.axis_size("shard")
    chips = count // 2
    mine = lax.axis_index("shard")
    chip, core = mine // 2, mine % 2
    shape = (chips,) + value.shape
    own = jnp.zeros(shape, value.dtype)
    for k in range(chips):
        part = value
        if k:
            part = lax.ppermute(
                value,
                "shard",
                [(2 * i + j, 2 * ((i + k) % chips) + j) for i in range(chips) for j in range(2)],
            )
        own = lax.dynamic_update_index_in_dim(own, part, (chip - k) % chips, 0)
    other = lax.ppermute(own, "shard", [(i, i ^ 1) for i in range(count)])
    first = jnp.where(core == 0, own, other)
    second = jnp.where(core == 0, other, own)
    return jnp.stack([first, second], axis=1).reshape((count,) + value.shape)


def all_to_all(value):
    return lax.all_to_all(value, "shard", split_axis=0, concat_axis=0, tiled=True)


def local(
    tokens,
    w_query,
    key_weight,
    value_weight,
    w_out,
    norm_attn,
    norm_ffn,
    w_router,
    w_gate,
    w_up,
    w_down,
    cotangent,
    choices,
    priority,
):
    shards = lax.axis_size("shard")
    ctx_count = lax.axis_size("ctx")
    ctx = lax.axis_index("ctx")
    shard = lax.axis_index("shard")
    ctx_index = ctx.astype(jnp.int32).reshape(1)
    tile = tokens.shape[0]
    rows = tile * shards
    expert_count = w_router.shape[1]
    experts = w_gate.shape[1]
    depth = w_query.shape[0]
    down_depth = w_down.shape[0]
    capacity = tile * TOPK * 5 // (4 * expert_count)
    heads = QUERY_HEADS // shards
    copies = max(1, shards // KEY_VALUE_HEADS)
    q_width = heads * HEAD_SIZE
    width = q_width + 2 * HEAD_SIZE

    halves = w_down.reshape(down_depth, experts, MODEL_WIDTH // FF, FF)
    expert_rows = jnp.concatenate(
        [
            jnp.transpose(w_gate, (1, 0, 2)),
            jnp.transpose(w_up, (1, 0, 2)),
            jnp.transpose(halves, (1, 2, 0, 3)).reshape(experts, -1, FF),
        ],
        axis=1,
    )
    expert_weights = lax.all_gather(expert_rows, "shard", axis=0, tiled=False)
    grouped = jnp.concatenate(
        [
            w_query.reshape(depth, shards, q_width),
            jnp.repeat(key_weight.reshape(depth, KEY_VALUE_HEADS, HEAD_SIZE), copies, axis=1),
            jnp.repeat(value_weight.reshape(depth, KEY_VALUE_HEADS, HEAD_SIZE), copies, axis=1),
        ],
        axis=2,
    )
    gains = jnp.concatenate([norm_attn, norm_ffn])
    gains = jnp.pad(gains[None, :], ((0, 15), (0, width - 2 * depth)))
    sent = jnp.concatenate(
        [
            jnp.transpose(grouped, (1, 0, 2)),
            jnp.broadcast_to(gains[None], (shards, 16, width)),
        ],
        axis=1,
    )
    arrived = all_to_all(sent)
    columns = arrived[:, :depth].reshape(MODEL_WIDTH, width)
    gain_attn = arrived[:, depth, :depth].reshape(MODEL_WIDTH).astype(F32)
    gain_ffn = arrived[:, depth, depth : 2 * depth].reshape(MODEL_WIDTH).astype(F32)
    out_rows = jnp.concatenate(
        [w_out, jnp.pad(w_router, ((0, 0), (0, LANES - expert_count)))], axis=1
    )
    gathered_out = lax.all_gather(out_rows, "shard", axis=0, tiled=True)
    out_full = gathered_out[:, :MODEL_WIDTH]
    router_wide = gathered_out[:, MODEL_WIDTH : MODEL_WIDTH + expert_count].astype(F32)
    grouped_full = lax.all_gather(
        grouped.reshape(depth, shards * width), "shard", axis=0, tiled=True
    )
    cot_parts = from_ctx(cotangent)

    x_block = gather_shard(tokens).reshape(rows, MODEL_WIDTH).astype(F32)
    normed = (x_block * rms_scale(x_block) * gain_attn[None, :]).astype(BF16)
    positions = ctx * rows + jnp.arange(rows, dtype=jnp.int32)
    cosine, sine = rotary_tables(positions)
    lin = dot(columns, normed, ((0,), (1,)))
    queries = rotate(lin[:q_width], cosine, sine).astype(BF16) * jnp.asarray(SCORE_SCALE, BF16)
    keys = rotate(lin[q_width : q_width + HEAD_SIZE], cosine, sine).astype(BF16)
    key_values = jnp.concatenate([keys, lin[q_width + HEAD_SIZE :].astype(BF16)], axis=0)
    kv_parts = from_ctx(key_values)
    outcome, outcome_wide, level = attend(queries, kv_parts, ctx_index, tile)

    chosen = choices[:, :, None] == jnp.arange(expert_count, dtype=jnp.int32)[None, None, :]
    rank = jnp.min(jnp.where(chosen, priority[:, :, None], UNCHOSEN), axis=1)
    earlier = jnp.sum((rank.T[:, None, :] < rank.T[:, :, None]).astype(F32), axis=2).T
    named = rank < UNCHOSEN
    kept = named & (earlier < capacity)

    attended = all_to_all(outcome).reshape(MODEL_WIDTH, tile)
    inputs = tokens.astype(F32)
    inverse_attn = rms_scale(inputs)
    branch = dot(attended, out_full, ((0,), (0,)))
    middle = inputs + RESIDUAL_SCALE * branch
    inverse_ffn = rms_scale(middle)
    normed_ffn = middle * inverse_ffn * gain_ffn[None, :]
    logits = jnp.dot(normed_ffn, router_wide, precision=PRECISE)
    masked_logits = jnp.where(named, logits, MASKED)
    raised = jnp.where(
        named, jnp.exp(masked_logits - jnp.max(masked_logits, axis=1, keepdims=True)), 0.0
    )
    gate_weights = raised / jnp.sum(raised, axis=1, keepdims=True)
    kept_weights = jnp.where(kept, gate_weights, 0.0)
    high = kept_weights.astype(BF16)
    low = (kept_weights - high.astype(F32)).astype(BF16)
    spare = ((0, 0), (0, LANES // 2 - expert_count))
    packet = jnp.concatenate([normed_ffn.astype(BF16), jnp.pad(high, spare), jnp.pad(low, spare)], 1)
    x_parts = from_ctx(packet)
    gin_parts, mix_parts, expert_grads = run_experts(x_parts, cot_parts, expert_weights, ctx_index)
    back = to_ctx(gin_parts)
    expert_mix = to_ctx(mix_parts)
    expert_share = lax.psum_scatter(expert_grads, "shard", scatter_dimension=0, tiled=False)
    block_out = (middle + RESIDUAL_SCALE * expert_mix).astype(BF16)

    upstream = cotangent.astype(F32)
    grad_gates = jnp.where(
        kept,
        back[:, MODEL_WIDTH : MODEL_WIDTH + expert_count]
        + back[:, MODEL_WIDTH + LANES : MODEL_WIDTH + LANES + expert_count],
        0.0,
    )
    grad_logits = gate_weights * (
        grad_gates - jnp.sum(gate_weights * grad_gates, axis=1, keepdims=True)
    )
    grad_normed_ffn = back[:, :MODEL_WIDTH] + jnp.einsum(
        "te,de->td", grad_logits, router_wide, precision=PRECISE
    )
    grad_middle = upstream + norm_back(grad_normed_ffn, middle, inverse_ffn, gain_ffn)
    grad_branch = (RESIDUAL_SCALE * grad_middle).astype(BF16)
    grad_attended = dot(out_full, grad_branch, ((1,), (1,))).astype(BF16)
    grad_heads = all_to_all(grad_attended.reshape(shards, q_width, tile))

    grad_router = jnp.einsum("td,te->de", normed_ffn, grad_logits, precision=PRECISE)
    grad_norm_ffn = jnp.sum(grad_normed_ffn * middle * inverse_ffn, axis=0)[:, None]
    fine = jnp.concatenate([grad_router, grad_norm_ffn], axis=1)
    fine_high = fine.astype(BF16)
    fine_low = (fine - fine_high.astype(F32)).astype(BF16)
    fine_width = expert_count + 1
    early = jnp.concatenate(
        [
            dot(attended, grad_branch).astype(BF16),
            fine_high,
            fine_low,
            jnp.zeros((MODEL_WIDTH, LANES - 2 * fine_width), BF16),
        ],
        axis=1,
    )
    early = scatter_ctx(early).astype(BF16)
    early = jnp.sum(
        all_to_all(early.reshape(shards, -1, MODEL_WIDTH + LANES)).astype(F32), axis=0
    )

    out = attend_back(queries, grad_heads, outcome_wide, level, kv_parts, ctx_index)
    grad_kv = to_ctx(out[1:]).T
    grad_lin = jnp.concatenate(
        [
            rotate(out[0], cosine, -sine),
            rotate(grad_kv[:HEAD_SIZE], cosine, -sine),
            grad_kv[HEAD_SIZE:],
        ],
        axis=0,
    ).astype(BF16)
    token_grads = all_to_all(
        jnp.transpose(grad_lin.reshape(width, shards, tile), (1, 0, 2))
    ).reshape(shards * width, tile)
    late = dot(normed, grad_lin, ((0,), (1,))).astype(BF16)
    late = scatter_ctx(late).astype(BF16)
    late = all_to_all(late.reshape(shards, -1, width)).astype(F32)
    share_rows = late.shape[1]

    grad_normed = dot(token_grads, grouped_full, ((0,), (1,)))
    grad_tokens = grad_middle + norm_back(grad_normed, inputs, inverse_attn, gain_attn)
    grad_query = jnp.transpose(late[:, :, :q_width], (1, 0, 2)).reshape(share_rows, -1)

    def kv_grad(part):
        part = part.reshape(KEY_VALUE_HEADS, copies, share_rows, HEAD_SIZE)
        return jnp.transpose(jnp.sum(part, axis=1), (1, 0, 2)).reshape(share_rows, -1)

    grad_key = kv_grad(late[:, :, q_width : q_width + HEAD_SIZE])
    grad_value = kv_grad(late[:, :, q_width + HEAD_SIZE :])
    first_row = (ctx * shards + shard) * share_rows
    own_weights = lax.dynamic_slice_in_dim(grouped_full, first_row, share_rows, 0).astype(F32)
    flat_late = jnp.transpose(late, (1, 0, 2)).reshape(share_rows, -1)
    own_gain = lax.dynamic_slice_in_dim(gain_attn, first_row, share_rows, 0)
    grad_norm_attn = jnp.sum(own_weights * flat_late, axis=1) / own_gain

    grad_router_sum = (
        early[:, MODEL_WIDTH : MODEL_WIDTH + fine_width]
        + early[:, MODEL_WIDTH + fine_width : MODEL_WIDTH + 2 * fine_width]
    )
    down_at = 2 * depth
    grad_down = expert_share[:, down_at:].reshape(experts, MODEL_WIDTH // FF, down_depth, FF)
    return (
        block_out,
        grad_tokens,
        grad_query,
        grad_key,
        grad_value,
        early[:, :MODEL_WIDTH],
        grad_norm_attn,
        grad_router_sum[:, expert_count],
        grad_router_sum[:, :expert_count],
        jnp.transpose(expert_share[:, :depth], (1, 0, 2)).astype(F32),
        jnp.transpose(expert_share[:, depth : 2 * depth], (1, 0, 2)).astype(F32),
        jnp.transpose(grad_down, (2, 0, 1, 3)).reshape(down_depth, experts, -1).astype(F32),
    )


def solution(mesh):
    placed = (
        P(("ctx", "shard"), None),
        P("shard", None),
        P("shard", None),
        P("shard", None),
        P("shard", None),
        P("shard"),
        P("shard"),
        P("shard", None),
        P("shard", "ctx", None),
        P("shard", "ctx", None),
        P("shard", "ctx", None),
        P(("ctx", "shard"), None),
        P(("ctx", "shard"), None),
        P(("ctx", "shard"), None),
    )
    return jax.shard_map(
        local,
        mesh=mesh,
        in_specs=placed,
        out_specs=(
            P(("ctx", "shard"), None),
            P(("ctx", "shard"), None),
            P(("ctx", "shard"), None),
            P(("ctx", "shard"), None),
            P(("ctx", "shard"), None),
            P(("ctx", "shard"), None),
            P(("ctx", "shard")),
            P(("ctx", "shard")),
            P(("ctx", "shard"), None),
            P("shard", "ctx", None),
            P("shard", "ctx", None),
            P("shard", "ctx", None),
        ),
        check_vma=False,
    )
```

```python
import functools
import math

import jax
import jax.numpy as jnp
from jax import lax
from jax.experimental import pallas as pl
from jax.experimental.pallas import tpu as pltpu
from jax.sharding import PartitionSpec as P

MODEL_WIDTH = 1024
QUERY_HEADS = 16
KEY_VALUE_HEADS = 8
HEAD_SIZE = 64
FF = 512
TOPK = 8

NORM_EPS = 1e-06
RESIDUAL_SCALE = 0.22
SCORE_SCALE = 0.015625
ROPE_BASE = 10000.0
PRECISE = lax.Precision.HIGHEST
MASKED = -1e30
UNCHOSEN = 1 << 20
LANES = 128

F32 = jnp.float32
BF16 = jnp.bfloat16


def whole(shape):
    return pl.BlockSpec(tuple(shape), lambda i: (0,) * len(shape))


def dot(a, b, dims=((1,), (0,))):
    return lax.dot_general(a, b, (dims, ((), ())), preferred_element_type=F32)


def rotary_tables(positions):
    halfway = HEAD_SIZE // 2
    frequency = jnp.exp(
        jnp.arange(halfway, dtype=F32) * (-2.0 * math.log(ROPE_BASE) / HEAD_SIZE)
    )
    angles = frequency[:, None] * positions.astype(F32)[None, :]
    return (jnp.cos(angles), jnp.sin(angles))


def rotate(vectors, cosine, sine):
    rows, count = vectors.shape
    shaped = vectors.reshape(rows // HEAD_SIZE, 2, HEAD_SIZE // 2, count)
    front, behind = shaped[:, 0], shaped[:, 1]
    turned = jnp.stack(
        [front * cosine - behind * sine, behind * cosine + front * sine], axis=1
    )
    return turned.reshape(rows, count)


def rms_scale(value_rows):
    return lax.rsqrt(jnp.mean(value_rows * value_rows, axis=1, keepdims=True) + NORM_EPS)


def norm_back(upward, inputs, inverse_rms, gain_vector):
    weighted = upward * gain_vector[None, :]
    cubed = inverse_rms * inverse_rms * inverse_rms
    return inverse_rms * weighted - inputs * cubed * jnp.mean(
        weighted * inputs, axis=1, keepdims=True
    )


def attention_blocks(rows):
    return min(512, rows)


def attend_kernel(c_ref, q_ref, *refs, ctx_count, heads, rows, block, tile):
    kv_refs = refs[:ctx_count]
    out_ref, wide_ref, log_ref = refs[ctx_count : ctx_count + 3]
    natural, peak, total, acc = refs[ctx_count + 3 :]
    step = pl.program_id(0)
    mine = c_ref[0]

    @pl.when(step == 0)
    def _():
        for k in range(ctx_count):

            @pl.when(mine >= k)
            def _(k=k):
                natural[k] = kv_refs[k][...].T

    zeros = jnp.zeros((HEAD_SIZE, block), BF16)
    wide_q = [
        jnp.concatenate([q_ref[h * HEAD_SIZE : (h + 1) * HEAD_SIZE, :], zeros], axis=0)
        for h in range(heads)
    ]
    for h in range(heads):
        peak[h] = jnp.full((1, block), MASKED, F32)
        total[h] = jnp.zeros((1, block), F32)
        acc[h] = jnp.zeros((HEAD_SIZE, block), F32)

    def visit(k, start, masked):
        keys = natural[k, pl.ds(start, block), :]
        values = kv_refs[k][HEAD_SIZE:, pl.ds(start, block)]
        for h in range(heads):
            scores = dot(keys, wide_q[h])
            if masked:
                place = lax.broadcasted_iota(jnp.int32, (block, block), 0)
                query = lax.broadcasted_iota(jnp.int32, (block, block), 1)
                scores = jnp.where(place <= query, scores, MASKED)
            old = peak[h]
            new = jnp.maximum(old, jnp.max(scores, axis=0, keepdims=True))
            shrink = jnp.exp(old - new)
            weights = jnp.exp(scores - new)
            peak[h] = new
            total[h] = total[h] * shrink + jnp.sum(weights, axis=0, keepdims=True)
            acc[h] = acc[h] * shrink + dot(values, weights.astype(BF16))

    def full(k):
        def body(j, carry):
            visit(k, pl.multiple_of(j * block, block), False)
            return carry

        return body

    for k in range(1, ctx_count):

        @pl.when(mine >= k)
        def _(k=k):
            lax.fori_loop(0, rows // block, full(k), 0)

    lax.fori_loop(0, step, full(0), 0)
    visit(0, pl.multiple_of(step * block, block), True)
    for h in range(heads):
        result = acc[h] / total[h]
        at = slice(h * HEAD_SIZE, (h + 1) * HEAD_SIZE)
        wide_ref[at, :] = result
        log_ref[h : h + 1, :] = peak[h] + jnp.log(total[h])
        for j in range(block // tile):
            out_ref[j, at, :] = result[:, j * tile : (j + 1) * tile].astype(BF16)


def attend(queries, key_values, ctx_index, tile):
    width, rows = queries.shape
    heads = width // HEAD_SIZE
    ctx_count = len(key_values)
    block = attention_blocks(rows)
    kv_width = key_values[0].shape[0]
    whole = pl.BlockSpec((kv_width, rows), lambda i, c: (0, 0))
    return pl.pallas_call(
        functools.partial(
            attend_kernel, ctx_count=ctx_count, heads=heads, rows=rows, block=block, tile=tile
        ),
        grid_spec=pltpu.PrefetchScalarGridSpec(
            num_scalar_prefetch=1,
            grid=(rows // block,),
            in_specs=[pl.BlockSpec((width, block), lambda i, c: (0, i))] + [whole] * ctx_count,
            out_specs=[
                pl.BlockSpec((block // tile, width, tile), lambda i, c: (i, 0, 0)),
                pl.BlockSpec((width, block), lambda i, c: (0, i)),
                pl.BlockSpec((heads, block), lambda i, c: (0, i)),
            ],
            scratch_shapes=[
                pltpu.VMEM((ctx_count, rows, kv_width), BF16),
                pltpu.VMEM((heads, 1, block), F32),
                pltpu.VMEM((heads, 1, block), F32),
                pltpu.VMEM((heads, HEAD_SIZE, block), F32),
            ],
        ),
        out_shape=[
            jax.ShapeDtypeStruct((rows // tile, width, tile), BF16),
            jax.ShapeDtypeStruct((width, rows), F32),
            jax.ShapeDtypeStruct((heads, rows), F32),
        ],
        compiler_params=pltpu.CompilerParams(
            dimension_semantics=("arbitrary",), vmem_limit_bytes=48 << 20
        ),
        cost_estimate=pl.CostEstimate(
            flops=64 * width * rows * rows * ctx_count // 2,
            transcendentals=heads * rows * rows * ctx_count // 2,
            bytes_accessed=2 * ctx_count * rows * kv_width,
        ),
        name="attend",
    )(ctx_index, queries, *key_values)


def attend_back_kernel(
    c_ref, q_ref, grad_ref, wide_ref, log_ref, *refs, ctx_count, heads, rows, block, tile
):
    kv_refs = refs[:ctx_count]
    gq_ref = refs[ctx_count]
    gkv_refs = refs[ctx_count + 1 : 2 * ctx_count + 1]
    natural, sums, gq_acc = refs[2 * ctx_count + 1 :]
    step = pl.program_id(0)
    last = pl.num_programs(0) - 1
    mine = c_ref[0]

    @pl.when(step == 0)
    def _():
        for k in range(ctx_count):

            @pl.when(mine >= k)
            def _(k=k):
                natural[k] = kv_refs[k][...].T
                sums[k] = jnp.zeros_like(sums[k])

    zeros = jnp.zeros((HEAD_SIZE, block), BF16)
    wide_q, wide_g, tall_q, tall_g, delta, level = [], [], [], [], [], []
    for h in range(heads):
        at = slice(h * HEAD_SIZE, (h + 1) * HEAD_SIZE)
        grad = jnp.concatenate([grad_ref[j, at, :] for j in range(block // tile)], axis=1)
        q_part = jnp.concatenate([q_ref[at, :], zeros], axis=0)
        g_part = jnp.concatenate([zeros, grad], axis=0)
        wide_q.append(q_part)
        wide_g.append(g_part)
        tall_q.append(q_part.T)
        tall_g.append(g_part.T)
        delta.append(jnp.sum(grad.astype(F32) * wide_ref[at, :], axis=0, keepdims=True))
        level.append(log_ref[h : h + 1, :])
        gq_acc[h] = jnp.zeros((HEAD_SIZE, block), F32)

    def visit(k, start, masked):
        both = natural[k, pl.ds(start, block), :]
        keys = kv_refs[k][:HEAD_SIZE, pl.ds(start, block)]
        add = None
        for h in range(heads):
            scores = dot(both, wide_q[h])
            if masked:
                place = lax.broadcasted_iota(jnp.int32, (block, block), 0)
                query = lax.broadcasted_iota(jnp.int32, (block, block), 1)
                scores = jnp.where(place <= query, scores, MASKED)
            weights = jnp.exp(scores - level[h])
            grad_probs = dot(both, wide_g[h])
            grad_scores = (weights * (grad_probs - delta[h])).astype(BF16)
            part = dot(grad_scores, tall_q[h]) + dot(weights.astype(BF16), tall_g[h])
            add = part if add is None else add + part
            gq_acc[h] += dot(keys, grad_scores)
        sums[k, pl.ds(start, block), :] += add

    def full(k):
        def body(j, carry):
            visit(k, pl.multiple_of(j * block, block), False)
            return carry

        return body

    for k in range(1, ctx_count):

        @pl.when(mine >= k)
        def _(k=k):
            lax.fori_loop(0, rows // block, full(k), 0)

    lax.fori_loop(0, step, full(0), 0)
    visit(0, pl.multiple_of(step * block, block), True)
    for h in range(heads):
        gq_ref[h * HEAD_SIZE : (h + 1) * HEAD_SIZE, :] = SCORE_SCALE * gq_acc[h]

    @pl.when(step == last)
    def _():
        gkv_refs[0][...] = sums[0]
        for k in range(1, ctx_count):

            @pl.when(mine >= k)
            def _(k=k):
                gkv_refs[k][...] = sums[k].astype(BF16)

            @pl.when(mine < k)
            def _(k=k):
                gkv_refs[k][...] = jnp.zeros((rows, sums.shape[2]), BF16)


def attend_back(queries, grads, wide, level, key_values, ctx_index):
    width, rows = queries.shape
    heads = width // HEAD_SIZE
    ctx_count = len(key_values)
    block = attention_blocks(rows)
    tile = grads.shape[2]
    kv_width = key_values[0].shape[0]
    whole = pl.BlockSpec((kv_width, rows), lambda i, c: (0, 0))
    tall = pl.BlockSpec((rows, kv_width), lambda i, c: (0, 0))
    return pl.pallas_call(
        functools.partial(
            attend_back_kernel, ctx_count=ctx_count, heads=heads, rows=rows, block=block, tile=tile
        ),
        grid_spec=pltpu.PrefetchScalarGridSpec(
            num_scalar_prefetch=1,
            grid=(rows // block,),
            in_specs=[
                pl.BlockSpec((width, block), lambda i, c: (0, i)),
                pl.BlockSpec((block // tile, width, tile), lambda i, c: (i, 0, 0)),
                pl.BlockSpec((width, block), lambda i, c: (0, i)),
                pl.BlockSpec((heads, block), lambda i, c: (0, i)),
            ]
            + [whole] * ctx_count,
            out_specs=[pl.BlockSpec((width, block), lambda i, c: (0, i))] + [tall] * ctx_count,
            scratch_shapes=[
                pltpu.VMEM((ctx_count, rows, kv_width), BF16),
                pltpu.VMEM((ctx_count, rows, kv_width), F32),
                pltpu.VMEM((heads, HEAD_SIZE, block), F32),
            ],
        ),
        out_shape=[jax.ShapeDtypeStruct((width, rows), F32)]
        + [
            jax.ShapeDtypeStruct((rows, kv_width), F32 if k == 0 else BF16)
            for k in range(ctx_count)
        ],
        compiler_params=pltpu.CompilerParams(
            dimension_semantics=("arbitrary",), vmem_limit_bytes=56 << 20
        ),
        cost_estimate=pl.CostEstimate(
            flops=96 * width * rows * rows * ctx_count // 2,
            transcendentals=heads * rows * rows * ctx_count // 2,
            bytes_accessed=4 * ctx_count * rows * kv_width,
        ),
        name="attend_back",
    )(ctx_index, queries, grads, wide, level, *key_values)


def tail_kernel(at_ref, gq_ref, cos_ref, sin_ref, normed_ref, columns_ref, *refs, ctx_count, tile):
    kv_refs, early_refs = refs[:ctx_count], refs[ctx_count : 2 * ctx_count]
    own_ref, other_ref, early_own_ref, early_other_ref = refs[2 * ctx_count : 2 * ctx_count + 4]
    late_refs = refs[2 * ctx_count + 4 : 3 * ctx_count + 4]
    tall, late = refs[3 * ctx_count + 4 :]
    ctx, core = at_ref[0], at_ref[1]
    q_width = gq_ref.shape[0]
    half = HEAD_SIZE // 2
    cosine, sine = cos_ref[...], sin_ref[...]

    def turn_back(vectors):
        front, behind = vectors[:half], vectors[half:]
        return [front * cosine + behind * sine, behind * cosine - front * sine]

    grad_kv = add_up([ref[...] for ref in kv_refs]).T
    pieces = []
    for h in range(q_width // HEAD_SIZE):
        pieces += turn_back(gq_ref[h * HEAD_SIZE : (h + 1) * HEAD_SIZE, :])
    pieces += turn_back(grad_kv[:HEAD_SIZE]) + [grad_kv[HEAD_SIZE:]]
    grad_lin = jnp.concatenate(pieces, axis=0).astype(BF16)
    tall[...] = grad_lin.T
    late[...] = dot(grad_lin, normed_ref[...]).astype(BF16).T
    block = late.shape[0] // ctx_count
    for k in range(ctx_count):
        first = pl.multiple_of(lax.rem(ctx - k + ctx_count, ctx_count) * block, block)
        late_refs[k][...] = late[pl.ds(first, block), :]
    early = add_up([ref[...] for ref in early_refs]).astype(BF16)
    chips, small = early_own_ref.shape[0], early_own_ref.shape[1]
    for chip in range(chips):
        at = [slice((2 * chip + j) * small, (2 * chip + j + 1) * small) for j in range(2)]
        swap = core == 1
        early_own_ref[chip] = jnp.where(swap, early[at[1]], early[at[0]])
        early_other_ref[chip] = jnp.where(swap, early[at[0]], early[at[1]])
        for side, ref in ((core, own_ref), (1 - core, other_ref)):
            first = pl.multiple_of((2 * chip + side) * tile, tile)
            ref[chip] = dot(
                tall[pl.ds(first, tile), :], columns_ref[...], ((1,), (1,))
            ).astype(BF16)


def tail(gq, cosine, sine, normed, columns, kv_back, early_back, at, tile):
    ctx_count = len(kv_back)
    rows, width = normed.shape
    lin_width = columns.shape[1]
    chips = rows // (2 * tile)
    small = early_back[0].shape[0] // (2 * chips)
    early_width = early_back[0].shape[1]
    block = width // ctx_count
    args = [at, gq, cosine, sine, normed, columns, *kv_back, *early_back]
    shapes = (
        [((chips, tile, width), BF16)] * 2
        + [((chips, small, early_width), BF16)] * 2
        + [((block, lin_width), BF16)] * ctx_count
    )
    out = pl.pallas_call(
        functools.partial(tail_kernel, ctx_count=ctx_count, tile=tile),
        grid=(1,),
        in_specs=[pl.BlockSpec(memory_space=pltpu.SMEM)] + [whole(v.shape) for v in args[1:]],
        out_specs=[whole(shape) for shape, _ in shapes],
        out_shape=[jax.ShapeDtypeStruct(*shape) for shape in shapes],
        scratch_shapes=[pltpu.VMEM((rows, lin_width), BF16), pltpu.VMEM((width, lin_width), BF16)],
        compiler_params=pltpu.CompilerParams(vmem_limit_bytes=48 << 20),
        cost_estimate=pl.CostEstimate(
            flops=4 * rows * width * lin_width, transcendentals=0, bytes_accessed=12 * rows * width
        ),
        name="tail",
    )(*args)
    return out[0], out[1], out[2], out[3], out[4:]


def finish_kernel(late_ref, weight_ref, gain_ref, *refs, q_width, copies, fine_rows):
    parts, (q_ref, k_ref, v_ref, out_ref, fine_ref) = refs[:-5], refs[-5:]
    shards, rows, width = late_ref.shape
    model = out_ref.shape[1]
    gain_grad = jnp.zeros((rows, 1), F32)
    values = [late_ref[s].astype(F32) for s in range(shards)]
    for s in range(shards):
        weights = weight_ref[:, s * width : (s + 1) * width].astype(F32)
        gain_grad += jnp.sum(values[s] * weights, axis=1, keepdims=True)
    q_ref[...] = jnp.concatenate([v[:, :q_width] for v in values], axis=1)
    for ref, first in ((k_ref, q_width), (v_ref, q_width + HEAD_SIZE)):
        heads = [v[:, first : first + HEAD_SIZE] for v in values]
        ref[...] = jnp.concatenate(
            [sum(heads[i * copies + 1 : (i + 1) * copies], heads[i * copies])
             for i in range(len(heads) // copies)],
            axis=1,
        )
    early = add_up([ref[...] for ref in parts])
    out_ref[...] = early[:, :model]
    fine = early[:, model:]
    lane = lax.broadcasted_iota(jnp.int32, (rows, LANES), 1)
    low = jnp.concatenate([fine[:, fine_rows:], fine[:, :fine_rows]], axis=1)
    fine_ref[...] = jnp.where(lane == fine_rows, gain_grad / gain_ref[...], fine + low)


def finish(late, own_weights, own_gain, early_back, q_width, copies, fine_rows):
    shards, rows, _ = late.shape
    model = early_back[0].shape[1] - LANES
    args = [late, own_weights, own_gain, *early_back]
    kv_width = shards // copies * HEAD_SIZE
    widths = [shards * q_width, kv_width, kv_width, model, LANES]
    return pl.pallas_call(
        functools.partial(finish_kernel, q_width=q_width, copies=copies, fine_rows=fine_rows),
        grid=(1,),
        in_specs=[whole(v.shape) for v in args],
        out_specs=[whole((rows, w)) for w in widths],
        out_shape=[jax.ShapeDtypeStruct((rows, w), F32) for w in widths],
        cost_estimate=pl.CostEstimate(
            flops=0, transcendentals=0, bytes_accessed=16 * rows * sum(widths)
        ),
        name="finish",
    )(*args)


def expert_kernel(
    c_ref, *refs, ctx_count, experts, first, carried, final, tile, rows, down_rows
):
    refs = list(refs)

    def take(count):
        taken = refs[:count]
        del refs[:count]
        return taken

    x_refs, u_refs, (w_ref,) = take(ctx_count), take(ctx_count), take(1)
    carry_refs = take(3 if carried else 0)
    if final:
        gin_refs, mix_refs = take(ctx_count), take(ctx_count)
    else:
        sums = take(3)
    (grad_ref,) = take(1)
    if final:
        sums = take(3)
    gin_acc, mix_acc, dots = sums
    x_all, x_turned, u_all, share, hid, g_out, g_gate, g_up = refs
    shards = w_ref.shape[0]
    e = pl.program_id(0)
    last = pl.num_programs(0) - 1
    width = u_all.shape[1]
    count = ctx_count * tile
    chunk = min(2 * tile, count)
    column = c_ref[0] * experts + first + e

    @pl.when(e == 0)
    def _():
        for k in range(ctx_count):
            at = slice(k * tile, (k + 1) * tile)
            part = x_refs[k][:, :width]
            x_all[at, :] = part
            x_turned[:, at] = part.T
            u_all[at, :] = u_refs[k][...]
            share[at, :] = x_refs[k][:, width:].astype(F32)
        for i, ref in enumerate(sums):
            ref[...] = carry_refs[i][...] if carried else jnp.zeros_like(ref)

    lane = lax.broadcasted_iota(jnp.int32, (chunk, LANES), 1)
    picked = (lane == column) | (lane == column + LANES // 2)
    down = 2 * rows

    def gate_matrix():
        return w_ref[:, 0, 0:rows, :].reshape(shards * rows, FF)

    def up_matrix():
        return w_ref[:, 0, rows : 2 * rows, :].reshape(shards * rows, FF)

    def down_matrix(half):
        at = down + half * down_rows
        return w_ref[:, 0, at : at + down_rows, :].reshape(FF, FF)

    def one_chunk(j, carry):
        at = pl.ds(pl.multiple_of(j * chunk, chunk), chunk)
        x = x_all[at, :]
        gate = dot(x, gate_matrix())
        up = dot(x, up_matrix())
        sig = jax.nn.sigmoid(gate)
        silu = gate * sig
        hidden = (silu * up).astype(BF16)
        hid[at, :] = hidden
        weight = jnp.sum(jnp.where(picked, share[at, :], 0.0), axis=1, keepdims=True)
        upstream = u_all[at, :].astype(F32) * RESIDUAL_SCALE
        down_grad = (upstream * weight).astype(BF16)
        g_out[at, :] = down_grad
        gathered = jnp.zeros((chunk, 1), F32)
        grad_hidden = jnp.zeros((chunk, FF), F32)
        for half in range(width // FF):
            cols = slice(half * FF, (half + 1) * FF)
            matrix = down_matrix(half)
            made = dot(hidden, matrix).astype(BF16).astype(F32)
            mix_acc[at, cols] += weight * made
            gathered += jnp.sum(upstream[:, cols] * made, axis=1, keepdims=True)
            grad_hidden += dot(down_grad[:, cols], matrix, ((1,), (1,)))
        dots[at, :] += jnp.where(picked, gathered, 0.0)
        grad_gate = (grad_hidden * up * sig * (1.0 + gate * (1.0 - sig))).astype(BF16)
        grad_up = (grad_hidden * silu).astype(BF16)
        g_gate[at, :] = grad_gate
        g_up[at, :] = grad_up
        gin_acc[at, :] += dot(grad_gate, gate_matrix(), ((1,), (1,))) + dot(
            grad_up, up_matrix(), ((1,), (1,))
        )
        return carry

    lax.fori_loop(0, count // chunk, one_chunk, 0)
    grad_ref[:, 0, 0:rows, :] = (
        dot(x_turned[...], g_gate[...]).astype(BF16).reshape(shards, rows, FF)
    )
    grad_ref[:, 0, rows : 2 * rows, :] = (
        dot(x_turned[...], g_up[...]).astype(BF16).reshape(shards, rows, FF)
    )
    hid_turned = hid[...].T
    for half in range(width // FF):
        at = down + half * down_rows
        grad_ref[:, 0, at : at + down_rows, :] = (
            dot(hid_turned, g_out[:, half * FF : (half + 1) * FF])
            .astype(BF16)
            .reshape(shards, down_rows, FF)
        )

    if not final:
        return

    @pl.when(e == last)
    def _():
        for k in range(ctx_count):
            at = slice(k * tile, (k + 1) * tile)
            gin_refs[k][:, :width] = gin_acc[at, :].astype(BF16)
            high = dots[at, :].astype(BF16)
            gin_refs[k][:, width : width + LANES // 2] = high[:, : LANES // 2]
            low = (dots[at, :] - high.astype(F32)).astype(BF16)
            gin_refs[k][:, width + LANES // 2 :] = low[:, LANES // 2 :]
            mix_refs[k][...] = mix_acc[at, :].astype(BF16)


def run_experts(x_parts, u_parts, weights, ctx_index, experts, first, carry, final):
    ctx_count = len(x_parts)
    tile, width = u_parts[0].shape
    shards, group, all_rows, _ = weights.shape
    rows = width // shards
    down_rows = FF // shards
    count = ctx_count * tile

    def flat(*shape, **options):
        return pl.BlockSpec(shape, lambda e, c: (0,) * len(shape), **options)

    by_expert = pl.BlockSpec((shards, 1, all_rows, FF), lambda e, c: (0, e, 0, 0))
    sum_shapes = [(count, width), (count, width), (count, LANES)]
    if final:
        out_specs = [flat(tile, width + LANES)] * ctx_count + [flat(tile, width)] * ctx_count
        out_shape = [jax.ShapeDtypeStruct((tile, width + LANES), BF16)] * ctx_count + [
            jax.ShapeDtypeStruct((tile, width), BF16)
        ] * ctx_count
        sum_scratch = [pltpu.VMEM(shape, F32) for shape in sum_shapes]
    else:
        out_specs = [flat(*shape) for shape in sum_shapes]
        out_shape = [jax.ShapeDtypeStruct(shape, F32) for shape in sum_shapes]
        sum_scratch = []
    once = pl.Buffered(1)
    out = pl.pallas_call(
        functools.partial(
            expert_kernel,
            ctx_count=ctx_count,
            experts=experts,
            first=first,
            carried=bool(carry),
            final=final,
            tile=tile,
            rows=rows,
            down_rows=down_rows,
        ),
        grid_spec=pltpu.PrefetchScalarGridSpec(
            num_scalar_prefetch=1,
            grid=(group,),
            in_specs=[flat(tile, width + LANES)] * ctx_count
            + [flat(tile, width)] * ctx_count
            + [by_expert]
            + [flat(*shape, pipeline_mode=once) for shape in sum_shapes[: len(carry)]],
            out_specs=out_specs + [by_expert],
            scratch_shapes=sum_scratch
            + [
                pltpu.VMEM((count, width), BF16),
                pltpu.VMEM((width, count), BF16),
                pltpu.VMEM((count, width), BF16),
                pltpu.VMEM((count, LANES), F32),
                pltpu.VMEM((count, FF), BF16),
                pltpu.VMEM((count, width), BF16),
                pltpu.VMEM((count, FF), BF16),
                pltpu.VMEM((count, FF), BF16),
            ],
        ),
        out_shape=out_shape + [jax.ShapeDtypeStruct(weights.shape, BF16)],
        compiler_params=pltpu.CompilerParams(
            dimension_semantics=("arbitrary",), vmem_limit_bytes=60 << 20
        ),
        cost_estimate=pl.CostEstimate(
            flops=24 * group * count * width * FF,
            transcendentals=group * count * FF,
            bytes_accessed=4 * shards * group * all_rows * FF,
        ),
        name="experts",
    )(ctx_index, *x_parts, *u_parts, weights, *carry)
    if final:
        return out[:ctx_count], out[ctx_count : 2 * ctx_count], out[2 * ctx_count]
    return out[:3], out[3]


def send_ctx(value, by):
    count = lax.axis_size("ctx")
    return lax.ppermute(value, "ctx", [(i, (i + by) % count) for i in range(count)])


def from_ctx(value):
    return [value] + [send_ctx(value, k) for k in range(1, lax.axis_size("ctx"))]


def from_later(parts):
    return [parts[0]] + [send_ctx(parts[k], -k) for k in range(1, len(parts))]


def add_up(parts):
    total = parts[0].astype(F32)
    for part in parts[1:]:
        total = total + part.astype(F32)
    return total


def to_ctx(parts):
    return add_up(from_later(parts))


def all_to_all(value):
    return lax.all_to_all(value, "shard", split_axis=0, concat_axis=0, tiled=True)


def send_chip(value, by):
    chips = lax.axis_size("shard") // 2
    return lax.ppermute(
        value,
        "shard",
        [(2 * i + j, 2 * ((i + by) % chips) + j) for i in range(chips) for j in range(2)],
    )


def send_core(value):
    return lax.ppermute(value, "shard", [(i, i ^ 1) for i in range(lax.axis_size("shard"))])


def tie(value, *others):
    return lax.optimization_barrier((value, others))[0]


def meet(*values):
    return lax.optimization_barrier(values)


def arrive(own, send, count):
    return [own] + [send(own, k) for k in range(1, count)]


def assemble_kernel(at_ref, *refs, count, lead):
    parts, out_ref = refs[:-1], refs[-1]
    for k in range(count):
        index = lax.rem(at_ref[0] - k + count, count)
        for side in range(2):
            slot = at_ref[1] if side == 0 else 1 - at_ref[1]
            out_ref[(slice(None),) * lead + (index, slot)] = parts[side * count + k][...]


def assemble(parts, others, first, lead):
    count = len(parts)
    shape, dtype = parts[0].shape, parts[0].dtype
    at = jnp.stack([first, lax.axis_index("shard") % 2]).astype(jnp.int32)
    out_shape = shape[:lead] + (count, 2) + shape[lead:]
    return pl.pallas_call(
        functools.partial(assemble_kernel, count=count, lead=lead),
        grid=(1,),
        in_specs=[pl.BlockSpec(memory_space=pltpu.SMEM)] + [whole(shape)] * (2 * count),
        out_specs=whole(out_shape),
        out_shape=jax.ShapeDtypeStruct(out_shape, dtype),
        compiler_params=pltpu.CompilerParams(vmem_limit_bytes=24 << 20),
        cost_estimate=pl.CostEstimate(
            flops=0, transcendentals=0, bytes_accessed=8 * count * parts[0].size
        ),
        name="assemble",
    )(at, *parts, *others)


def spread_start(value):
    shards, ctx_count = lax.axis_size("shard"), lax.axis_size("ctx")
    shard, ctx = lax.axis_index("shard"), lax.axis_index("ctx")
    core, chips = shard % 2, shards // 2
    rows, columns = value.shape
    pieces = lax.dynamic_index_in_dim(
        value.reshape(ctx_count, 2, rows // (2 * ctx_count), columns), ctx, 0, keepdims=False
    )
    mine = lax.dynamic_index_in_dim(pieces, core, 0, keepdims=False)
    theirs = send_core(lax.dynamic_index_in_dim(pieces, 1 - core, 0, keepdims=False))
    pair = jnp.stack([jnp.where(core == 0, mine, theirs), jnp.where(core == 0, theirs, mine)])
    return arrive(pair, send_chip, chips)


def spread_join(parts):
    chips = len(parts)
    chip = lax.axis_index("shard") // 2
    joined = jnp.zeros((chips,) + parts[0].shape, parts[0].dtype)
    for k, part in enumerate(parts):
        joined = lax.dynamic_update_index_in_dim(joined, part, (chip - k) % chips, 0)
    return joined


def spread_ctx(joined):
    return arrive(joined, send_ctx, lax.axis_size("ctx"))


def spread_end(parts, others):
    return assemble(parts, others, lax.axis_index("ctx"), 2).reshape(MODEL_WIDTH, -1)


def to_chips(blocks):
    chips = blocks.shape[0]
    chip = lax.axis_index("shard") // 2
    parts = [lax.dynamic_index_in_dim(blocks, chip, 0, keepdims=False)]
    for k in range(1, chips):
        part = lax.dynamic_index_in_dim(blocks, (chip + k) % chips, 0, keepdims=False)
        parts.append(send_chip(part, k))
    return parts


def local(
    tokens,
    w_query,
    key_weight,
    value_weight,
    w_out,
    norm_attn,
    norm_ffn,
    w_router,
    w_gate,
    w_up,
    w_down,
    cotangent,
    choices,
    priority,
):
    shards = lax.axis_size("shard")
    ctx_count = lax.axis_size("ctx")
    ctx = lax.axis_index("ctx")
    shard = lax.axis_index("shard")
    ctx_index = ctx.astype(jnp.int32).reshape(1)
    tile = tokens.shape[0]
    rows = tile * shards
    expert_count = w_router.shape[1]
    experts = w_gate.shape[1]
    depth = w_query.shape[0]
    down_depth = w_down.shape[0]
    capacity = tile * TOPK * 5 // (4 * expert_count)
    heads = QUERY_HEADS // shards
    copies = max(1, shards // KEY_VALUE_HEADS)
    q_width = heads * HEAD_SIZE
    width = q_width + 2 * HEAD_SIZE

    halves = w_down.reshape(down_depth, experts, MODEL_WIDTH // FF, FF)
    expert_rows = jnp.concatenate(
        [
            jnp.transpose(w_gate, (1, 0, 2)),
            jnp.transpose(w_up, (1, 0, 2)),
            jnp.transpose(halves, (1, 2, 0, 3)).reshape(experts, -1, FF),
        ],
        axis=1,
    )
    grouped = jnp.concatenate(
        [
            w_query.reshape(depth, shards, q_width),
            jnp.repeat(key_weight.reshape(depth, KEY_VALUE_HEADS, HEAD_SIZE), copies, axis=1),
            jnp.repeat(value_weight.reshape(depth, KEY_VALUE_HEADS, HEAD_SIZE), copies, axis=1),
        ],
        axis=2,
    )
    small = jnp.concatenate([norm_attn, norm_ffn])[None, :]
    small = jnp.concatenate(
        [
            jnp.pad(small, ((0, 0), (0, MODEL_WIDTH - 2 * depth))),
            w_router.reshape(-1, MODEL_WIDTH),
        ],
        axis=0,
    )
    small = jnp.pad(small, ((0, 16 - small.shape[0]), (0, 0)))
    chips = shards // 2
    token_parts = arrive(jnp.concatenate([tokens, small], axis=0), send_chip, chips)
    cot_parts = from_ctx(cotangent)
    columns = all_to_all(jnp.transpose(grouped, (1, 0, 2))).reshape(MODEL_WIDTH, width)
    token_parts, columns, cot_parts = meet(token_parts, columns, cot_parts)
    gathered = assemble(token_parts, [send_core(part) for part in token_parts], shard // 2, 0)
    gathered = gathered.reshape((shards,) + token_parts[0].shape)
    split = experts - 1
    weights_first = lax.all_gather(tie(expert_rows[:split], token_parts), "shard", axis=0, tiled=False)
    weights_last = lax.all_gather(
        tie(expert_rows[split:], gathered), "shard", axis=0, tiled=False
    )
    gain_attn = gathered[:, tile, :depth].reshape(MODEL_WIDTH).astype(F32)
    gain_ffn = gathered[:, tile, depth : 2 * depth].reshape(MODEL_WIDTH).astype(F32)
    router_rows = w_router.size // MODEL_WIDTH
    router_wide = gathered[:, tile + 1 : tile + 1 + router_rows].reshape(MODEL_WIDTH, expert_count)
    router_wide = router_wide.astype(F32)
    share_rows = MODEL_WIDTH // (ctx_count * shards)
    own_weights = lax.ppermute(
        lax.dynamic_slice_in_dim(
            tie(grouped.reshape(depth, shards * width), token_parts), ctx * share_rows, share_rows, 0
        ),
        ("ctx", "shard"),
        [(j * shards + i, ctx_count * i + j) for j in range(ctx_count) for i in range(shards)],
    )

    x_block = gathered[:, :tile].reshape(rows, MODEL_WIDTH).astype(F32)
    normed = (x_block * rms_scale(x_block) * gain_attn[None, :]).astype(BF16)
    positions = ctx * rows + jnp.arange(rows, dtype=jnp.int32)
    cosine, sine = rotary_tables(positions)
    lin = dot(columns, normed, ((0,), (1,)))
    queries = rotate(lin[:q_width], cosine, sine).astype(BF16) * jnp.asarray(SCORE_SCALE, BF16)
    keys = rotate(lin[q_width : q_width + HEAD_SIZE], cosine, sine).astype(BF16)
    key_values = jnp.concatenate([keys, lin[q_width + HEAD_SIZE :].astype(BF16)], axis=0)
    kv_parts = from_ctx(key_values)
    out_parts = spread_start(tie(w_out, key_values))
    outcome, outcome_wide, level = attend(queries, kv_parts, ctx_index, tile)
    outcome, out_parts, own_weights = meet(outcome, out_parts, own_weights)
    out_ctx = spread_ctx(spread_join(out_parts))
    out_other = [send_core(part) for part in out_ctx]

    chosen = choices[:, :, None] == jnp.arange(expert_count, dtype=jnp.int32)[None, None, :]
    rank = jnp.min(jnp.where(chosen, priority[:, :, None], UNCHOSEN), axis=1)
    earlier = jnp.sum((rank.T[:, None, :] < rank.T[:, :, None]).astype(F32), axis=2).T
    named = rank < UNCHOSEN
    kept = named & (earlier < capacity)

    attended = all_to_all(outcome).reshape(MODEL_WIDTH, tile)
    attended, out_ctx, out_other = meet(attended, out_ctx, out_other)
    out_full = spread_end(out_ctx, out_other)
    inputs = tokens.astype(F32)
    inverse_attn = rms_scale(inputs)
    branch = dot(attended, out_full, ((0,), (0,)))
    middle = inputs + RESIDUAL_SCALE * branch
    inverse_ffn = rms_scale(middle)
    normed_ffn = middle * inverse_ffn * gain_ffn[None, :]
    logits = jnp.dot(normed_ffn, router_wide, precision=PRECISE)
    masked_logits = jnp.where(named, logits, MASKED)
    raised = jnp.where(
        named, jnp.exp(masked_logits - jnp.max(masked_logits, axis=1, keepdims=True)), 0.0
    )
    gate_weights = raised / jnp.sum(raised, axis=1, keepdims=True)
    kept_weights = jnp.where(kept, gate_weights, 0.0)
    high = kept_weights.astype(BF16)
    low = (kept_weights - high.astype(F32)).astype(BF16)
    spare = ((0, 0), (0, LANES // 2 - expert_count))
    packet = jnp.concatenate([normed_ffn.astype(BF16), jnp.pad(high, spare), jnp.pad(low, spare)], 1)
    x_parts = from_ctx(packet)
    carry, grads_first = run_experts(
        x_parts, cot_parts, weights_first, ctx_index, experts, 0, [], False
    )
    gin_parts, mix_parts, grads_last = run_experts(
        x_parts, cot_parts, weights_last, ctx_index, experts, split, carry, True
    )
    back = to_ctx(gin_parts)
    share_first = lax.psum_scatter(grads_first, "shard", scatter_dimension=0, tiled=False)
    upstream = cotangent.astype(F32)
    grad_gates = jnp.where(
        kept,
        back[:, MODEL_WIDTH : MODEL_WIDTH + expert_count]
        + back[:, MODEL_WIDTH + LANES // 2 : MODEL_WIDTH + LANES // 2 + expert_count],
        0.0,
    )
    grad_logits = gate_weights * (
        grad_gates - jnp.sum(gate_weights * grad_gates, axis=1, keepdims=True)
    )
    grad_normed_ffn = back[:, :MODEL_WIDTH] + jnp.einsum(
        "te,de->td", grad_logits, router_wide, precision=PRECISE
    )
    grad_middle = upstream + norm_back(grad_normed_ffn, middle, inverse_ffn, gain_ffn)
    grad_branch = (RESIDUAL_SCALE * grad_middle).astype(BF16)
    grad_attended = dot(out_full, grad_branch, ((1,), (1,))).astype(BF16)
    grad_heads = all_to_all(grad_attended.reshape(shards, q_width, tile))

    grad_router = jnp.einsum("te,td->ed", grad_logits, normed_ffn, precision=PRECISE)
    grad_norm_ffn = jnp.sum(grad_normed_ffn * middle * inverse_ffn, axis=0)[None, :]
    fine = jnp.concatenate([grad_router, grad_norm_ffn], axis=0)
    fine_high = fine.astype(BF16)
    fine_low = (fine - fine_high.astype(F32)).astype(BF16)
    fine_rows = expert_count + 1
    fine = jnp.concatenate(
        [fine_high, fine_low, jnp.zeros((LANES - 2 * fine_rows, MODEL_WIDTH), BF16)], axis=0
    ).T
    block = MODEL_WIDTH // ctx_count
    early_parts = []
    for k in range(ctx_count):
        first = ((ctx - k) % ctx_count) * block
        part = lax.dynamic_slice_in_dim(attended, first, block, 0)
        early_parts.append(
            jnp.concatenate(
                [
                    dot(part, grad_branch).astype(BF16),
                    lax.dynamic_slice_in_dim(fine, first, block, 0),
                ],
                axis=1,
            )
        )
    grad_heads, early_parts = meet(grad_heads, early_parts)
    early_parts = from_later(early_parts)

    out = attend_back(queries, grad_heads, outcome_wide, level, kv_parts, ctx_index)
    early_parts, gq, kv_out = meet(early_parts, out[0], out[1:])
    kv_back = from_later(kv_out)
    mix_back = from_later(tie(mix_parts, kv_back))
    share_last = lax.psum_scatter(
        tie(grads_last, share_first, kv_back), "shard", scatter_dimension=0, tiled=False
    )
    at = jnp.stack([ctx, shard % 2]).astype(jnp.int32)
    grad_own, grad_other, early_own, early_other, late_parts = tail(
        gq, cosine, sine, normed, columns, kv_back, early_parts, at, tile
    )
    grad_sum = (grad_own.astype(F32) + send_core(grad_other).astype(F32)).astype(BF16)
    token_back = to_chips(grad_sum)
    early_other, late_parts, _ = meet(early_other, late_parts, grad_sum)
    late = to_ctx(late_parts).astype(BF16)
    early_sum = (early_own.astype(F32) + send_core(early_other).astype(F32)).astype(BF16)
    late = all_to_all(late.reshape(shards, -1, width))
    early_back = to_chips(tie(early_sum, late))
    expert_share = jnp.concatenate([share_first, share_last], axis=0)
    grad_down = expert_share[:, 2 * depth :].reshape(experts, MODEL_WIDTH // FF, down_depth, FF)
    expert_grads = (
        jnp.transpose(expert_share[:, :depth], (1, 0, 2)).astype(F32),
        jnp.transpose(expert_share[:, depth : 2 * depth], (1, 0, 2)).astype(F32),
        jnp.transpose(grad_down, (2, 0, 1, 3)).reshape(down_depth, experts, -1).astype(F32),
    )
    early_back, late, token_back, mix_back = meet(early_back, late, token_back, mix_back)
    block_out = (middle + RESIDUAL_SCALE * add_up(mix_back)).astype(BF16)
    grad_normed = add_up(token_back)
    grad_tokens = grad_middle + norm_back(grad_normed, inputs, inverse_attn, gain_attn)
    first_row = (ctx * shards + shard) * share_rows
    own_gain = lax.dynamic_slice_in_dim(gain_attn, first_row, share_rows, 0)[:, None]
    grad_query, grad_key, grad_value, grad_out, fine = finish(
        late, own_weights, own_gain, early_back, q_width, copies, fine_rows
    )
    return (
        block_out,
        grad_tokens,
        grad_query,
        grad_key,
        grad_value,
        grad_out,
        fine[:, fine_rows],
        fine[:, expert_count],
        fine[:, :expert_count],
        *expert_grads,
    )


def solution(mesh):
    placed = (
        P(("ctx", "shard"), None),
        P("shard", None),
        P("shard", None),
        P("shard", None),
        P("shard", None),
        P("shard"),
        P("shard"),
        P("shard", None),
        P("shard", "ctx", None),
        P("shard", "ctx", None),
        P("shard", "ctx", None),
        P(("ctx", "shard"), None),
        P(("ctx", "shard"), None),
        P(("ctx", "shard"), None),
    )
    return jax.shard_map(
        local,
        mesh=mesh,
        in_specs=placed,
        out_specs=(
            P(("ctx", "shard"), None),
            P(("ctx", "shard"), None),
            P(("ctx", "shard"), None),
            P(("ctx", "shard"), None),
            P(("ctx", "shard"), None),
            P(("ctx", "shard"), None),
            P(("ctx", "shard")),
            P(("ctx", "shard")),
            P(("ctx", "shard"), None),
            P("shard", "ctx", None),
            P("shard", "ctx", None),
            P("shard", "ctx", None),
        ),
        check_vma=False,
    )
```

```python
import functools
import math

import jax
import jax.numpy as jnp
from jax import lax
from jax.experimental import pallas as pl
from jax.experimental.pallas import tpu as pltpu
from jax.sharding import PartitionSpec as P

MODEL_WIDTH = 1024
QUERY_HEADS = 16
KEY_VALUE_HEADS = 8
HEAD_SIZE = 64
FF = 512
TOPK = 8

NORM_EPS = 1e-06
RESIDUAL_SCALE = 0.22
SCORE_SCALE = 0.015625
ROPE_BASE = 10000.0
PRECISE = lax.Precision.HIGHEST
MASKED = -1e30
UNCHOSEN = 1 << 20
LANES = 128

F32 = jnp.float32
BF16 = jnp.bfloat16


def whole(shape):
    return pl.BlockSpec(tuple(shape), lambda i: (0,) * len(shape))


def dot(a, b, dims=((1,), (0,))):
    return lax.dot_general(a, b, (dims, ((), ())), preferred_element_type=F32)


def rotary_tables(positions):
    halfway = HEAD_SIZE // 2
    frequency = jnp.exp(
        jnp.arange(halfway, dtype=F32) * (-2.0 * math.log(ROPE_BASE) / HEAD_SIZE)
    )
    angles = frequency[:, None] * positions.astype(F32)[None, :]
    return (jnp.cos(angles), jnp.sin(angles))


def rotate(vectors, cosine, sine):
    rows, count = vectors.shape
    shaped = vectors.reshape(rows // HEAD_SIZE, 2, HEAD_SIZE // 2, count)
    front, behind = shaped[:, 0], shaped[:, 1]
    turned = jnp.stack(
        [front * cosine - behind * sine, behind * cosine + front * sine], axis=1
    )
    return turned.reshape(rows, count)


def rms_scale(value_rows):
    return lax.rsqrt(jnp.mean(value_rows * value_rows, axis=1, keepdims=True) + NORM_EPS)


def norm_back(upward, inputs, inverse_rms, gain_vector):
    weighted = upward * gain_vector.reshape(1, -1)
    cubed = inverse_rms * inverse_rms * inverse_rms
    return inverse_rms * weighted - inputs * cubed * jnp.mean(
        weighted * inputs, axis=1, keepdims=True
    )


def project_kernel(
    at_ref, columns_ref, cos_ref, sin_ref, *refs, count, tile, depth
):
    parts = refs[: 2 * count]
    normed_ref, q_ref, kv_ref, small_ref, block, gain = refs[2 * count :]
    shards = 2 * count
    width = normed_ref.shape[1]
    lane = lax.broadcasted_iota(jnp.int32, (1, width), 1) // depth
    gain[...] = jnp.zeros_like(gain)
    for k in range(count):
        for side in range(2):
            slot = at_ref[1] if side == 0 else 1 - at_ref[1]
            index = 2 * lax.rem(at_ref[0] - k + count, count) + slot
            part = parts[side * count + k]
            block[pl.ds(pl.multiple_of(index * tile, tile), tile), :] = part[:tile, :]
            small_ref[index] = part[tile:, :]
            row = part[tile : tile + 1, :].astype(F32)
            gain[...] += jnp.where(lane == index, row, 0.0)
    for s in range(shards):
        at = slice(s * tile, (s + 1) * tile)
        x = block[at, :].astype(F32)
        normed_ref[at, :] = (x * rms_scale(x) * gain[...]).astype(BF16)
    lin = dot(columns_ref[...].T, normed_ref[...], ((1,), (1,)))
    q_width = q_ref.shape[0]
    half = HEAD_SIZE // 2
    cosine, sine = cos_ref[...], sin_ref[...]

    def turn(first):
        front, behind = lin[first : first + half], lin[first + half : first + 2 * half]
        return front * cosine - behind * sine, behind * cosine + front * sine

    for h in range(q_width // HEAD_SIZE):
        front, behind = turn(h * HEAD_SIZE)
        at = h * HEAD_SIZE
        q_ref[at : at + half, :] = front.astype(BF16) * jnp.asarray(SCORE_SCALE, BF16)
        q_ref[at + half : at + 2 * half, :] = behind.astype(BF16) * jnp.asarray(SCORE_SCALE, BF16)
    front, behind = turn(q_width)
    kv_ref[:half, :] = front.astype(BF16)
    kv_ref[half:HEAD_SIZE, :] = behind.astype(BF16)
    kv_ref[HEAD_SIZE:, :] = lin[q_width + HEAD_SIZE :].astype(BF16)


def project(parts, others, columns, cosine, sine, at, tile, depth):
    count = len(parts)
    height, width = parts[0].shape
    rows = 2 * count * tile
    lin_width = columns.shape[1]
    shapes = [
        (rows, width),
        (lin_width - 2 * HEAD_SIZE, rows),
        (2 * HEAD_SIZE, rows),
        (2 * count, height - tile, width),
    ]
    args = [at, columns, cosine, sine, *parts, *others]
    return pl.pallas_call(
        functools.partial(project_kernel, count=count, tile=tile, depth=depth),
        grid=(1,),
        in_specs=[pl.BlockSpec(memory_space=pltpu.SMEM)] + [whole(v.shape) for v in args[1:]],
        out_specs=[whole(shape) for shape in shapes],
        out_shape=[jax.ShapeDtypeStruct(shape, BF16) for shape in shapes],
        scratch_shapes=[pltpu.VMEM((rows, width), BF16), pltpu.VMEM((1, width), F32)],
        compiler_params=pltpu.CompilerParams(vmem_limit_bytes=60 << 20),
        cost_estimate=pl.CostEstimate(
            flops=2 * rows * width * lin_width,
            transcendentals=0,
            bytes_accessed=4 * rows * width,
        ),
        name="project",
    )(*args)


def attention_blocks(rows):
    return min(512, rows)


def attend_kernel(c_ref, q_ref, *refs, ctx_count, heads, rows, block, tile):
    kv_refs = refs[:ctx_count]
    out_ref, wide_ref, log_ref = refs[ctx_count : ctx_count + 3]
    natural, peak, total, acc = refs[ctx_count + 3 :]
    step = pl.program_id(0)
    mine = c_ref[0]

    @pl.when(step == 0)
    def _():
        for k in range(ctx_count):

            @pl.when(mine >= k)
            def _(k=k):
                natural[k] = kv_refs[k][...].T

    zeros = jnp.zeros((HEAD_SIZE, block), BF16)
    wide_q = [
        jnp.concatenate([q_ref[h * HEAD_SIZE : (h + 1) * HEAD_SIZE, :], zeros], axis=0)
        for h in range(heads)
    ]
    for h in range(heads):
        peak[h] = jnp.full((1, block), MASKED, F32)
        total[h] = jnp.zeros((1, block), F32)
        acc[h] = jnp.zeros((HEAD_SIZE, block), F32)

    def visit(k, start, masked):
        keys = natural[k, pl.ds(start, block), :]
        values = kv_refs[k][HEAD_SIZE:, pl.ds(start, block)]
        for h in range(heads):
            scores = dot(keys, wide_q[h])
            if masked:
                place = lax.broadcasted_iota(jnp.int32, (block, block), 0)
                query = lax.broadcasted_iota(jnp.int32, (block, block), 1)
                scores = jnp.where(place <= query, scores, MASKED)
            old = peak[h]
            new = jnp.maximum(old, jnp.max(scores, axis=0, keepdims=True))
            shrink = jnp.exp(old - new)
            weights = jnp.exp(scores - new)
            peak[h] = new
            total[h] = total[h] * shrink + jnp.sum(weights, axis=0, keepdims=True)
            acc[h] = acc[h] * shrink + dot(values, weights.astype(BF16))

    def full(k):
        def body(j, carry):
            visit(k, pl.multiple_of(j * block, block), False)
            return carry

        return body

    for k in range(1, ctx_count):

        @pl.when(mine >= k)
        def _(k=k):
            lax.fori_loop(0, rows // block, full(k), 0)

    lax.fori_loop(0, step, full(0), 0)
    visit(0, pl.multiple_of(step * block, block), True)
    for h in range(heads):
        result = acc[h] / total[h]
        at = slice(h * HEAD_SIZE, (h + 1) * HEAD_SIZE)
        wide_ref[at, :] = result
        log_ref[h : h + 1, :] = peak[h] + jnp.log(total[h])
        for j in range(block // tile):
            out_ref[j, at, :] = result[:, j * tile : (j + 1) * tile].astype(BF16)


def attend(queries, key_values, ctx_index, tile):
    width, rows = queries.shape
    heads = width // HEAD_SIZE
    ctx_count = len(key_values)
    block = attention_blocks(rows)
    kv_width = key_values[0].shape[0]
    whole = pl.BlockSpec((kv_width, rows), lambda i, c: (0, 0))
    return pl.pallas_call(
        functools.partial(
            attend_kernel, ctx_count=ctx_count, heads=heads, rows=rows, block=block, tile=tile
        ),
        grid_spec=pltpu.PrefetchScalarGridSpec(
            num_scalar_prefetch=1,
            grid=(rows // block,),
            in_specs=[pl.BlockSpec((width, block), lambda i, c: (0, i))] + [whole] * ctx_count,
            out_specs=[
                pl.BlockSpec((block // tile, width, tile), lambda i, c: (i, 0, 0)),
                pl.BlockSpec((width, block), lambda i, c: (0, i)),
                pl.BlockSpec((heads, block), lambda i, c: (0, i)),
            ],
            scratch_shapes=[
                pltpu.VMEM((ctx_count, rows, kv_width), BF16),
                pltpu.VMEM((heads, 1, block), F32),
                pltpu.VMEM((heads, 1, block), F32),
                pltpu.VMEM((heads, HEAD_SIZE, block), F32),
            ],
        ),
        out_shape=[
            jax.ShapeDtypeStruct((rows // tile, width, tile), BF16),
            jax.ShapeDtypeStruct((width, rows), F32),
            jax.ShapeDtypeStruct((heads, rows), F32),
        ],
        compiler_params=pltpu.CompilerParams(
            dimension_semantics=("arbitrary",), vmem_limit_bytes=48 << 20
        ),
        cost_estimate=pl.CostEstimate(
            flops=64 * width * rows * rows * ctx_count // 2,
            transcendentals=heads * rows * rows * ctx_count // 2,
            bytes_accessed=2 * ctx_count * rows * kv_width,
        ),
        name="attend",
    )(ctx_index, queries, *key_values)


def attend_back_kernel(
    c_ref, q_ref, grad_ref, wide_ref, log_ref, *refs, ctx_count, heads, rows, block, tile
):
    kv_refs = refs[:ctx_count]
    gq_ref = refs[ctx_count]
    gkv_refs = refs[ctx_count + 1 : 2 * ctx_count + 1]
    natural, sums, gq_acc = refs[2 * ctx_count + 1 :]
    step = pl.program_id(0)
    last = pl.num_programs(0) - 1
    mine = c_ref[0]

    @pl.when(step == 0)
    def _():
        for k in range(ctx_count):

            @pl.when(mine >= k)
            def _(k=k):
                natural[k] = kv_refs[k][...].T
                sums[k] = jnp.zeros_like(sums[k])

    zeros = jnp.zeros((HEAD_SIZE, block), BF16)
    wide_q, wide_g, tall_q, tall_g, delta, level = [], [], [], [], [], []
    for h in range(heads):
        at = slice(h * HEAD_SIZE, (h + 1) * HEAD_SIZE)
        grad = jnp.concatenate([grad_ref[j, at, :] for j in range(block // tile)], axis=1)
        q_part = jnp.concatenate([q_ref[at, :], zeros], axis=0)
        g_part = jnp.concatenate([zeros, grad], axis=0)
        wide_q.append(q_part)
        wide_g.append(g_part)
        tall_q.append(q_part.T)
        tall_g.append(g_part.T)
        delta.append(jnp.sum(grad.astype(F32) * wide_ref[at, :], axis=0, keepdims=True))
        level.append(log_ref[h : h + 1, :])
        gq_acc[h] = jnp.zeros((HEAD_SIZE, block), F32)

    def visit(k, start, masked):
        both = natural[k, pl.ds(start, block), :]
        keys = kv_refs[k][:HEAD_SIZE, pl.ds(start, block)]
        add = None
        for h in range(heads):
            scores = dot(both, wide_q[h])
            if masked:
                place = lax.broadcasted_iota(jnp.int32, (block, block), 0)
                query = lax.broadcasted_iota(jnp.int32, (block, block), 1)
                scores = jnp.where(place <= query, scores, MASKED)
            weights = jnp.exp(scores - level[h])
            grad_probs = dot(both, wide_g[h])
            grad_scores = (weights * (grad_probs - delta[h])).astype(BF16)
            part = dot(grad_scores, tall_q[h]) + dot(weights.astype(BF16), tall_g[h])
            add = part if add is None else add + part
            gq_acc[h] += dot(keys, grad_scores)
        sums[k, pl.ds(start, block), :] += add

    def full(k):
        def body(j, carry):
            visit(k, pl.multiple_of(j * block, block), False)
            return carry

        return body

    for k in range(1, ctx_count):

        @pl.when(mine >= k)
        def _(k=k):
            lax.fori_loop(0, rows // block, full(k), 0)

    lax.fori_loop(0, step, full(0), 0)
    visit(0, pl.multiple_of(step * block, block), True)
    for h in range(heads):
        gq_ref[h * HEAD_SIZE : (h + 1) * HEAD_SIZE, :] = SCORE_SCALE * gq_acc[h]

    @pl.when(step == last)
    def _():
        gkv_refs[0][...] = sums[0]
        for k in range(1, ctx_count):

            @pl.when(mine >= k)
            def _(k=k):
                gkv_refs[k][...] = sums[k].astype(BF16)

            @pl.when(mine < k)
            def _(k=k):
                gkv_refs[k][...] = jnp.zeros((rows, sums.shape[2]), BF16)


def attend_back(queries, grads, wide, level, key_values, ctx_index):
    width, rows = queries.shape
    heads = width // HEAD_SIZE
    ctx_count = len(key_values)
    block = attention_blocks(rows)
    tile = grads.shape[2]
    kv_width = key_values[0].shape[0]
    whole = pl.BlockSpec((kv_width, rows), lambda i, c: (0, 0))
    tall = pl.BlockSpec((rows, kv_width), lambda i, c: (0, 0))
    return pl.pallas_call(
        functools.partial(
            attend_back_kernel, ctx_count=ctx_count, heads=heads, rows=rows, block=block, tile=tile
        ),
        grid_spec=pltpu.PrefetchScalarGridSpec(
            num_scalar_prefetch=1,
            grid=(rows // block,),
            in_specs=[
                pl.BlockSpec((width, block), lambda i, c: (0, i)),
                pl.BlockSpec((block // tile, width, tile), lambda i, c: (i, 0, 0)),
                pl.BlockSpec((width, block), lambda i, c: (0, i)),
                pl.BlockSpec((heads, block), lambda i, c: (0, i)),
            ]
            + [whole] * ctx_count,
            out_specs=[pl.BlockSpec((width, block), lambda i, c: (0, i))] + [tall] * ctx_count,
            scratch_shapes=[
                pltpu.VMEM((ctx_count, rows, kv_width), BF16),
                pltpu.VMEM((ctx_count, rows, kv_width), F32),
                pltpu.VMEM((heads, HEAD_SIZE, block), F32),
            ],
        ),
        out_shape=[jax.ShapeDtypeStruct((width, rows), F32)]
        + [
            jax.ShapeDtypeStruct((rows, kv_width), F32 if k == 0 else BF16)
            for k in range(ctx_count)
        ],
        compiler_params=pltpu.CompilerParams(
            dimension_semantics=("arbitrary",), vmem_limit_bytes=56 << 20
        ),
        cost_estimate=pl.CostEstimate(
            flops=96 * width * rows * rows * ctx_count // 2,
            transcendentals=heads * rows * rows * ctx_count // 2,
            bytes_accessed=4 * ctx_count * rows * kv_width,
        ),
        name="attend_back",
    )(ctx_index, queries, grads, wide, level, *key_values)


def tail_kernel(
    at_ref, gq_ref, cos_ref, sin_ref, normed_ref, columns_ref, fine_ref, *refs, ctx_count, tile
):
    kv_refs, early_refs = refs[:ctx_count], refs[ctx_count : 2 * ctx_count]
    own_ref, other_ref = refs[2 * ctx_count : 2 * ctx_count + 2]
    late_refs = refs[2 * ctx_count + 2 : 3 * ctx_count + 2]
    tall, late = refs[3 * ctx_count + 2 :]
    ctx, core = at_ref[0], at_ref[1]
    q_width = gq_ref.shape[0]
    lin_width = tall.shape[1]
    half = HEAD_SIZE // 2
    cosine, sine = cos_ref[...], sin_ref[...]

    def turn_back(vectors):
        front, behind = vectors[:half], vectors[half:]
        return [front * cosine + behind * sine, behind * cosine - front * sine]

    grad_kv = add_up([ref[...] for ref in kv_refs]).T
    pieces = []
    for h in range(q_width // HEAD_SIZE):
        pieces += turn_back(gq_ref[h * HEAD_SIZE : (h + 1) * HEAD_SIZE, :])
    pieces += turn_back(grad_kv[:HEAD_SIZE]) + [grad_kv[HEAD_SIZE:]]
    grad_lin = jnp.concatenate(pieces, axis=0).astype(BF16)
    tall[...] = grad_lin.T
    late[...] = dot(grad_lin, normed_ref[...]).astype(BF16).T
    block = late.shape[0] // ctx_count
    for k in range(ctx_count):
        first = pl.multiple_of(lax.rem(ctx - k + ctx_count, ctx_count) * block, block)
        late_refs[k][:, :lin_width] = late[pl.ds(first, block), :]
        late_refs[k][:, lin_width:] = fine_ref[pl.ds(first, block), :]
    early = add_up([ref[...] for ref in early_refs]).astype(BF16)
    chips = own_ref.shape[0]
    small = own_ref.shape[1] - tile
    swap = core == 1
    for chip in range(chips):
        at = [slice((2 * chip + j) * small, (2 * chip + j + 1) * small) for j in range(2)]
        own_ref[chip, tile:, :] = jnp.where(swap, early[at[1]], early[at[0]])
        other_ref[chip, tile:, :] = jnp.where(swap, early[at[0]], early[at[1]])
        for side, ref in ((core, own_ref), (1 - core, other_ref)):
            first = pl.multiple_of((2 * chip + side) * tile, tile)
            ref[chip, :tile, :] = dot(
                tall[pl.ds(first, tile), :], columns_ref[...], ((1,), (1,))
            ).astype(BF16)


def tail(gq, cosine, sine, normed, columns, fine, kv_back, early_back, at, tile):
    ctx_count = len(kv_back)
    rows, width = normed.shape
    lin_width = columns.shape[1]
    chips = rows // (2 * tile)
    small = early_back[0].shape[0] // (2 * chips)
    block = width // ctx_count
    args = [at, gq, cosine, sine, normed, columns, fine, *kv_back, *early_back]
    shapes = [((chips, tile + small, width), BF16)] * 2 + [
        ((block, lin_width + LANES), BF16)
    ] * ctx_count
    out = pl.pallas_call(
        functools.partial(tail_kernel, ctx_count=ctx_count, tile=tile),
        grid=(1,),
        in_specs=[pl.BlockSpec(memory_space=pltpu.SMEM)] + [whole(v.shape) for v in args[1:]],
        out_specs=[whole(shape) for shape, _ in shapes],
        out_shape=[jax.ShapeDtypeStruct(*shape) for shape in shapes],
        scratch_shapes=[pltpu.VMEM((rows, lin_width), BF16), pltpu.VMEM((width, lin_width), BF16)],
        compiler_params=pltpu.CompilerParams(vmem_limit_bytes=60 << 20),
        cost_estimate=pl.CostEstimate(
            flops=4 * rows * width * lin_width, transcendentals=0, bytes_accessed=12 * rows * width
        ),
        name="tail",
    )(*args)
    return out[0], out[1], out[2:]


def finish_kernel(
    late_ref, weight_ref, gain_ref, middle_ref, token_ref, inverse_ref, norm_ref, *refs,
    q_width, copies, experts, tile
):
    parts = refs[:-8]
    tokens_ref, q_ref, k_ref, v_ref, out_ref, attn_ref, ffn_ref, router_ref = refs[-8:]
    grad_normed = add_up([ref[:tile, :] for ref in parts])
    inputs = token_ref[...].astype(F32)
    tokens_ref[...] = middle_ref[...] + norm_back(
        grad_normed, inputs, inverse_ref[...], norm_ref[...]
    )
    out_ref[...] = add_up([ref[tile:, :] for ref in parts])
    shards, rows, _ = late_ref.shape
    width = q_width + 2 * HEAD_SIZE
    gain_grad = jnp.zeros((rows, 1), F32)
    values = [late_ref[s, :, :width].astype(F32) for s in range(shards)]
    for s in range(shards):
        weights = weight_ref[:, s * width : (s + 1) * width].astype(F32)
        gain_grad += jnp.sum(values[s] * weights, axis=1, keepdims=True)
    q_ref[...] = jnp.concatenate([v[:, :q_width] for v in values], axis=1)
    for ref, first in ((k_ref, q_width), (v_ref, q_width + HEAD_SIZE)):
        heads = [v[:, first : first + HEAD_SIZE] for v in values]
        ref[...] = jnp.concatenate(
            [add_up(heads[i : i + copies]) for i in range(0, shards, copies)], axis=1
        )
    fine = add_up([late_ref[s, :, width:] for s in range(shards)])
    count = experts + 1
    router_ref[...] = fine[:, :experts] + fine[:, count : count + experts]
    ffn_ref[...] = (fine[:, experts:count] + fine[:, count + experts : 2 * count]).T
    attn_ref[...] = (gain_grad / gain_ref[...]).T


def finish(
    late, own_weights, own_gain, grad_middle, tokens, inverse, gain, token_back,
    q_width, copies, experts
):
    shards, rows, _ = late.shape
    tile, model = grad_middle.shape
    args = [late, own_weights, own_gain, grad_middle, tokens, inverse, gain[None, :], *token_back]
    kv_width = shards // copies * HEAD_SIZE
    shapes = [(tile, model), (rows, shards * q_width), (rows, kv_width), (rows, kv_width)]
    shapes += [(rows, model), (1, rows), (1, rows), (rows, experts)]
    return pl.pallas_call(
        functools.partial(
            finish_kernel, q_width=q_width, copies=copies, experts=experts, tile=tile
        ),
        grid=(1,),
        in_specs=[whole(v.shape) for v in args],
        out_specs=[whole(shape) for shape in shapes],
        out_shape=[jax.ShapeDtypeStruct(shape, F32) for shape in shapes],
        compiler_params=pltpu.CompilerParams(vmem_limit_bytes=60 << 20),
        cost_estimate=pl.CostEstimate(
            flops=0, transcendentals=0, bytes_accessed=16 * tile * model
        ),
        name="finish",
    )(*args)


def unpack_kernel(first_ref, last_ref, gate_ref, up_ref, down_ref):
    rows, down_rows = gate_ref.shape[0], down_ref.shape[0]
    split = first_ref.shape[0]
    for e in range(split + last_ref.shape[0]):
        source, i = (first_ref, e) if e < split else (last_ref, e - split)
        gate_ref[:, e, :] = source[i, :rows, :].astype(F32)
        up_ref[:, e, :] = source[i, rows : 2 * rows, :].astype(F32)
        for half in range(down_ref.shape[2] // FF):
            at = 2 * rows + half * down_rows
            down_ref[:, e, half * FF : (half + 1) * FF] = source[
                i, at : at + down_rows, :
            ].astype(F32)


def unpack(first, last, rows, down_rows, model):
    experts = first.shape[0] + last.shape[0]
    shapes = [(rows, experts, FF), (rows, experts, FF), (down_rows, experts, model)]
    return pl.pallas_call(
        unpack_kernel,
        grid=(1,),
        in_specs=[whole(first.shape), whole(last.shape)],
        out_specs=[whole(shape) for shape in shapes],
        out_shape=[jax.ShapeDtypeStruct(shape, F32) for shape in shapes],
        compiler_params=pltpu.CompilerParams(vmem_limit_bytes=60 << 20),
        cost_estimate=pl.CostEstimate(
            flops=0, transcendentals=0, bytes_accessed=6 * (first.size + last.size)
        ),
        name="unpack",
    )(first, last)


def expert_kernel(
    c_ref, *refs, ctx_count, experts, first, carried, final, tile, rows, down_rows
):
    refs = list(refs)

    def take(count):
        taken = refs[:count]
        del refs[:count]
        return taken

    x_refs, u_refs, (w_ref,) = take(ctx_count), take(ctx_count), take(1)
    carry_refs = take(3 if carried else 0)
    if final:
        gin_refs, mix_refs = take(ctx_count), take(ctx_count)
    else:
        sums = take(3)
    (grad_ref,) = take(1)
    if final:
        sums = take(3)
    gin_acc, mix_acc, dots = sums
    x_all, x_turned, u_all, share, hid, g_out, g_gate, g_up = refs
    shards = w_ref.shape[0]
    e = pl.program_id(0)
    last = pl.num_programs(0) - 1
    width = u_all.shape[1]
    count = ctx_count * tile
    chunk = min(2 * tile, count)
    column = c_ref[0] * experts + first + e

    @pl.when(e == 0)
    def _():
        for k in range(ctx_count):
            at = slice(k * tile, (k + 1) * tile)
            part = x_refs[k][:, :width]
            x_all[at, :] = part
            x_turned[:, at] = part.T
            u_all[at, :] = u_refs[k][...]
            share[at, :] = x_refs[k][:, width:].astype(F32)
        for i, ref in enumerate(sums):
            ref[...] = carry_refs[i][...] if carried else jnp.zeros_like(ref)

    lane = lax.broadcasted_iota(jnp.int32, (chunk, LANES), 1)
    picked = (lane == column) | (lane == column + LANES // 2)
    down = 2 * rows

    def gate_matrix():
        return w_ref[:, 0, 0:rows, :].reshape(shards * rows, FF)

    def up_matrix():
        return w_ref[:, 0, rows : 2 * rows, :].reshape(shards * rows, FF)

    def down_matrix(half):
        at = down + half * down_rows
        return w_ref[:, 0, at : at + down_rows, :].reshape(FF, FF)

    def one_chunk(j, carry):
        at = pl.ds(pl.multiple_of(j * chunk, chunk), chunk)
        x = x_all[at, :]
        gate = dot(x, gate_matrix())
        up = dot(x, up_matrix())
        sig = jax.nn.sigmoid(gate)
        silu = gate * sig
        hidden = (silu * up).astype(BF16)
        hid[at, :] = hidden
        weight = jnp.sum(jnp.where(picked, share[at, :], 0.0), axis=1, keepdims=True)
        upstream = u_all[at, :].astype(F32) * RESIDUAL_SCALE
        down_grad = (upstream * weight).astype(BF16)
        g_out[at, :] = down_grad
        gathered = jnp.zeros((chunk, 1), F32)
        grad_hidden = jnp.zeros((chunk, FF), F32)
        for half in range(width // FF):
            cols = slice(half * FF, (half + 1) * FF)
            matrix = down_matrix(half)
            made = dot(hidden, matrix).astype(BF16).astype(F32)
            mix_acc[at, cols] += weight * made
            gathered += jnp.sum(upstream[:, cols] * made, axis=1, keepdims=True)
            grad_hidden += dot(down_grad[:, cols], matrix, ((1,), (1,)))
        dots[at, :] += jnp.where(picked, gathered, 0.0)
        grad_gate = (grad_hidden * up * sig * (1.0 + gate * (1.0 - sig))).astype(BF16)
        grad_up = (grad_hidden * silu).astype(BF16)
        g_gate[at, :] = grad_gate
        g_up[at, :] = grad_up
        gin_acc[at, :] += dot(grad_gate, gate_matrix(), ((1,), (1,))) + dot(
            grad_up, up_matrix(), ((1,), (1,))
        )
        return carry

    lax.fori_loop(0, count // chunk, one_chunk, 0)
    grad_ref[:, 0, 0:rows, :] = (
        dot(x_turned[...], g_gate[...]).astype(BF16).reshape(shards, rows, FF)
    )
    grad_ref[:, 0, rows : 2 * rows, :] = (
        dot(x_turned[...], g_up[...]).astype(BF16).reshape(shards, rows, FF)
    )
    hid_turned = hid[...].T
    for half in range(width // FF):
        at = down + half * down_rows
        grad_ref[:, 0, at : at + down_rows, :] = (
            dot(hid_turned, g_out[:, half * FF : (half + 1) * FF])
            .astype(BF16)
            .reshape(shards, down_rows, FF)
        )

    if not final:
        return

    @pl.when(e == last)
    def _():
        for k in range(ctx_count):
            at = slice(k * tile, (k + 1) * tile)
            gin_refs[k][:, :width] = gin_acc[at, :].astype(BF16)
            high = dots[at, :].astype(BF16)
            gin_refs[k][:, width : width + LANES // 2] = high[:, : LANES // 2]
            low = (dots[at, :] - high.astype(F32)).astype(BF16)
            gin_refs[k][:, width + LANES // 2 :] = low[:, LANES // 2 :]
            mix_refs[k][...] = mix_acc[at, :].astype(BF16)


def run_experts(x_parts, u_parts, weights, ctx_index, experts, first, carry, final):
    ctx_count = len(x_parts)
    tile, width = u_parts[0].shape
    shards, group, all_rows, _ = weights.shape
    rows = width // shards
    down_rows = FF // shards
    count = ctx_count * tile

    def flat(*shape, **options):
        return pl.BlockSpec(shape, lambda e, c: (0,) * len(shape), **options)

    expert_block = (shards, 1, all_rows, FF)
    by_expert = pl.BlockSpec(expert_block, lambda e, c: (0, e, 0, 0))
    made = pl.BlockSpec(expert_block, lambda e, c: (0, e, 0, 0))
    sum_shapes = [(count, width), (count, width), (count, LANES)]
    if final:
        out_specs = [flat(tile, width + LANES)] * ctx_count + [flat(tile, width)] * ctx_count
        out_shape = [jax.ShapeDtypeStruct((tile, width + LANES), BF16)] * ctx_count + [
            jax.ShapeDtypeStruct((tile, width), BF16)
        ] * ctx_count
        sum_scratch = [pltpu.VMEM(shape, F32) for shape in sum_shapes]
    else:
        out_specs = [flat(*shape) for shape in sum_shapes]
        out_shape = [jax.ShapeDtypeStruct(shape, F32) for shape in sum_shapes]
        sum_scratch = []
    once = pl.Buffered(1)
    out = pl.pallas_call(
        functools.partial(
            expert_kernel,
            ctx_count=ctx_count,
            experts=experts,
            first=first,
            carried=bool(carry),
            final=final,
            tile=tile,
            rows=rows,
            down_rows=down_rows,
        ),
        grid_spec=pltpu.PrefetchScalarGridSpec(
            num_scalar_prefetch=1,
            grid=(group,),
            in_specs=[flat(tile, width + LANES)] * ctx_count
            + [flat(tile, width)] * ctx_count
            + [by_expert]
            + [flat(*shape, pipeline_mode=once) for shape in sum_shapes[: len(carry)]],
            out_specs=out_specs + [made],
            scratch_shapes=sum_scratch
            + [
                pltpu.VMEM((count, width), BF16),
                pltpu.VMEM((width, count), BF16),
                pltpu.VMEM((count, width), BF16),
                pltpu.VMEM((count, LANES), F32),
                pltpu.VMEM((count, FF), BF16),
                pltpu.VMEM((count, width), BF16),
                pltpu.VMEM((count, FF), BF16),
                pltpu.VMEM((count, FF), BF16),
            ],
        ),
        out_shape=out_shape + [jax.ShapeDtypeStruct((shards, group, all_rows, FF), BF16)],
        compiler_params=pltpu.CompilerParams(
            dimension_semantics=("arbitrary",), vmem_limit_bytes=60 << 20
        ),
        cost_estimate=pl.CostEstimate(
            flops=24 * group * count * width * FF,
            transcendentals=group * count * FF,
            bytes_accessed=4 * shards * group * all_rows * FF,
        ),
        name="experts",
    )(ctx_index, *x_parts, *u_parts, weights, *carry)
    if final:
        return out[:ctx_count], out[ctx_count : 2 * ctx_count], out[2 * ctx_count]
    return out[:3], out[3]


def send_ctx(value, by):
    count = lax.axis_size("ctx")
    return lax.ppermute(value, "ctx", [(i, (i + by) % count) for i in range(count)])


def from_ctx(value):
    return [value] + [send_ctx(value, k) for k in range(1, lax.axis_size("ctx"))]


def from_later(parts):
    return [parts[0]] + [send_ctx(parts[k], -k) for k in range(1, len(parts))]


def add_up(parts):
    total = parts[0].astype(F32)
    for part in parts[1:]:
        total = total + part.astype(F32)
    return total


def to_ctx(parts):
    return add_up(from_later(parts))


def all_to_all(value):
    return lax.all_to_all(value, "shard", split_axis=0, concat_axis=0, tiled=True)


def send_chip(value, by):
    chips = lax.axis_size("shard") // 2
    return lax.ppermute(
        value,
        "shard",
        [(2 * i + j, 2 * ((i + by) % chips) + j) for i in range(chips) for j in range(2)],
    )


def send_core(value):
    return lax.ppermute(value, "shard", [(i, i ^ 1) for i in range(lax.axis_size("shard"))])


def tie(value, *others):
    return lax.optimization_barrier((value, others))[0]


def relay_chips(value):
    chips = lax.axis_size("shard") // 2
    chip = lax.axis_index("shard") // 2

    def step(block, by, done):
        pairs = [
            (2 * i + j, 2 * (i + by) + j)
            for i in range(chips)
            if 0 <= i + by < chips and 0 <= i - by * done < chips
            for j in range(2)
        ]
        return lax.ppermute(block, "shard", pairs)

    up, down = [value], [value]
    for k in range(1, chips):
        up.append(step(up[-1], 1, k - 1))
        down.append(step(down[-1], -1, k - 1))
    return [value] + [jnp.where(chip >= k, up[k], down[chips - k]) for k in range(1, chips)]


def meet(*values):
    return lax.optimization_barrier(values)


def arrive(own, send, count):
    return [own] + [send(own, k) for k in range(1, count)]


def assemble_kernel(at_ref, *refs, count, lead):
    parts, out_ref = refs[:-1], refs[-1]
    for k in range(count):
        index = lax.rem(at_ref[0] - k + count, count)
        for side in range(2):
            slot = at_ref[1] if side == 0 else 1 - at_ref[1]
            out_ref[(slice(None),) * lead + (index, slot)] = parts[side * count + k][...]


def assemble(parts, others, first, lead):
    count = len(parts)
    shape, dtype = parts[0].shape, parts[0].dtype
    at = jnp.stack([first, lax.axis_index("shard") % 2]).astype(jnp.int32)
    out_shape = shape[:lead] + (count, 2) + shape[lead:]
    return pl.pallas_call(
        functools.partial(assemble_kernel, count=count, lead=lead),
        grid=(1,),
        in_specs=[pl.BlockSpec(memory_space=pltpu.SMEM)] + [whole(shape)] * (2 * count),
        out_specs=whole(out_shape),
        out_shape=jax.ShapeDtypeStruct(out_shape, dtype),
        compiler_params=pltpu.CompilerParams(vmem_limit_bytes=60 << 20),
        cost_estimate=pl.CostEstimate(
            flops=0, transcendentals=0, bytes_accessed=8 * count * parts[0].size
        ),
        name="assemble",
    )(at, *parts, *others)


def spread_start(value):
    shards, ctx_count = lax.axis_size("shard"), lax.axis_size("ctx")
    shard, ctx = lax.axis_index("shard"), lax.axis_index("ctx")
    core, chips = shard % 2, shards // 2
    rows, columns = value.shape
    pieces = lax.dynamic_index_in_dim(
        value.reshape(ctx_count, 2, rows // (2 * ctx_count), columns), ctx, 0, keepdims=False
    )
    mine = lax.dynamic_index_in_dim(pieces, core, 0, keepdims=False)
    theirs = send_core(lax.dynamic_index_in_dim(pieces, 1 - core, 0, keepdims=False))
    pair = jnp.stack([jnp.where(core == 0, mine, theirs), jnp.where(core == 0, theirs, mine)])
    return arrive(pair, send_chip, chips)


def spread_join(parts):
    chips = len(parts)
    chip = lax.axis_index("shard") // 2
    joined = jnp.zeros((chips,) + parts[0].shape, parts[0].dtype)
    for k, part in enumerate(parts):
        joined = lax.dynamic_update_index_in_dim(joined, part, (chip - k) % chips, 0)
    return joined


def spread_ctx(joined):
    return arrive(joined, send_ctx, lax.axis_size("ctx"))


def spread_end(parts, others):
    return assemble(parts, others, lax.axis_index("ctx"), 2).reshape(MODEL_WIDTH, -1)


def to_chips(blocks):
    chips = blocks.shape[0]
    chip = lax.axis_index("shard") // 2
    parts = [lax.dynamic_index_in_dim(blocks, chip, 0, keepdims=False)]
    for k in range(1, chips):
        part = lax.dynamic_index_in_dim(blocks, (chip + k) % chips, 0, keepdims=False)
        parts.append(send_chip(part, k))
    return parts


def local(
    tokens,
    w_query,
    key_weight,
    value_weight,
    w_out,
    norm_attn,
    norm_ffn,
    w_router,
    w_gate,
    w_up,
    w_down,
    cotangent,
    choices,
    priority,
):
    shards = lax.axis_size("shard")
    ctx_count = lax.axis_size("ctx")
    ctx = lax.axis_index("ctx")
    shard = lax.axis_index("shard")
    ctx_index = ctx.astype(jnp.int32).reshape(1)
    tile = tokens.shape[0]
    rows = tile * shards
    expert_count = w_router.shape[1]
    experts = w_gate.shape[1]
    depth = w_query.shape[0]
    down_depth = w_down.shape[0]
    capacity = tile * TOPK * 5 // (4 * expert_count)
    heads = QUERY_HEADS // shards
    copies = max(1, shards // KEY_VALUE_HEADS)
    q_width = heads * HEAD_SIZE
    width = q_width + 2 * HEAD_SIZE
    share_rows = MODEL_WIDTH // (ctx_count * shards)

    halves = w_down.reshape(down_depth, experts, MODEL_WIDTH // FF, FF)
    expert_rows = jnp.concatenate(
        [
            jnp.transpose(w_gate, (1, 0, 2)),
            jnp.transpose(w_up, (1, 0, 2)),
            jnp.transpose(halves, (1, 2, 0, 3)).reshape(experts, -1, FF),
        ],
        axis=1,
    )
    grouped = jnp.concatenate(
        [
            w_query.reshape(depth, shards, q_width),
            jnp.repeat(key_weight.reshape(depth, KEY_VALUE_HEADS, HEAD_SIZE), copies, axis=1),
            jnp.repeat(value_weight.reshape(depth, KEY_VALUE_HEADS, HEAD_SIZE), copies, axis=1),
        ],
        axis=2,
    )
    small = jnp.concatenate(
        [
            jnp.tile(norm_attn, MODEL_WIDTH // depth)[None, :],
            jnp.tile(norm_ffn, MODEL_WIDTH // depth)[None, :],
            w_router.reshape(-1, MODEL_WIDTH),
        ],
        axis=0,
    )
    small = jnp.pad(small, ((0, 16 - small.shape[0]), (0, 0)))
    chips = shards // 2
    token_parts = relay_chips(jnp.concatenate([tokens, small], axis=0))
    columns = all_to_all(jnp.transpose(grouped, (1, 0, 2))).reshape(MODEL_WIDTH, width)
    cot_parts = from_ctx(cotangent)
    token_parts, columns, cot_parts = meet(token_parts, columns, cot_parts)
    positions = ctx * rows + jnp.arange(rows, dtype=jnp.int32)
    cosine, sine = rotary_tables(positions)
    split = 1
    weights_first = lax.all_gather(expert_rows[:split], "shard", axis=0, tiled=False)
    weights_last = lax.all_gather(
        tie(expert_rows[split:], weights_first, token_parts), "shard", axis=0, tiled=False
    )

    place = jnp.stack([shard // 2, shard % 2]).astype(jnp.int32)
    normed, queries, key_values, small = project(
        token_parts,
        [send_core(part) for part in token_parts],
        columns,
        cosine,
        sine,
        place,
        tile,
        depth,
    )
    gain_attn = small[:, 0, :depth].reshape(MODEL_WIDTH).astype(F32)
    gain_ffn = small[:, 1, :depth].reshape(MODEL_WIDTH).astype(F32)
    router_rows = w_router.size // MODEL_WIDTH
    router_wide = small[:, 2 : 2 + router_rows].reshape(MODEL_WIDTH, expert_count).astype(F32)
    kv_parts = from_ctx(key_values)
    out_parts = spread_start(tie(w_out, key_values))
    outcome, outcome_wide, level = attend(queries, kv_parts, ctx_index, tile)
    outcome, out_parts = meet(outcome, out_parts)
    out_ctx = spread_ctx(spread_join(out_parts))
    out_other = [send_core(part) for part in out_ctx]

    chosen = choices[:, :, None] == jnp.arange(expert_count, dtype=jnp.int32)[None, None, :]
    rank = jnp.min(jnp.where(chosen, priority[:, :, None], UNCHOSEN), axis=1)
    earlier = jnp.sum((rank.T[:, None, :] < rank.T[:, :, None]).astype(F32), axis=2).T
    named = rank < UNCHOSEN
    kept = named & (earlier < capacity)

    attended = all_to_all(outcome).reshape(MODEL_WIDTH, tile)
    attended, out_ctx, out_other = meet(attended, out_ctx, out_other)
    out_full = spread_end(out_ctx, out_other)
    inputs = tokens.astype(F32)
    inverse_attn = rms_scale(inputs)
    branch = dot(attended, out_full, ((0,), (0,)))
    middle = inputs + RESIDUAL_SCALE * branch
    inverse_ffn = rms_scale(middle)
    normed_ffn = middle * inverse_ffn * gain_ffn[None, :]
    logits = jnp.dot(normed_ffn, router_wide, precision=PRECISE)
    masked_logits = jnp.where(named, logits, MASKED)
    raised = jnp.where(
        named, jnp.exp(masked_logits - jnp.max(masked_logits, axis=1, keepdims=True)), 0.0
    )
    gate_weights = raised / jnp.sum(raised, axis=1, keepdims=True)
    kept_weights = jnp.where(kept, gate_weights, 0.0)
    high = kept_weights.astype(BF16)
    low = (kept_weights - high.astype(F32)).astype(BF16)
    spare = ((0, 0), (0, LANES // 2 - expert_count))
    packet = jnp.concatenate([normed_ffn.astype(BF16), jnp.pad(high, spare), jnp.pad(low, spare)], 1)
    x_parts = from_ctx(packet)
    grouped_rows = tie(grouped.reshape(depth, shards * width), packet)
    own_weights = lax.ppermute(
        lax.dynamic_slice_in_dim(
            grouped_rows, ctx * share_rows, share_rows, 0
        ),
        ("ctx", "shard"),
        [(j * shards + i, ctx_count * i + j) for j in range(ctx_count) for i in range(shards)],
    )
    x_parts, own_weights = meet(x_parts, own_weights)
    carry, grads_first = run_experts(
        x_parts, cot_parts, weights_first, ctx_index, experts, 0, [], False
    )
    gin_parts, mix_parts, grads_last = run_experts(
        x_parts, cot_parts, weights_last, ctx_index, experts, split, carry, True
    )
    back = to_ctx(gin_parts)
    share_first = lax.psum_scatter(grads_first, "shard", scatter_dimension=0, tiled=False)
    share_last = lax.psum_scatter(
        tie(grads_last, share_first, back), "shard", scatter_dimension=0, tiled=False
    )
    upstream = cotangent.astype(F32)
    grad_gates = jnp.where(
        kept,
        back[:, MODEL_WIDTH : MODEL_WIDTH + expert_count]
        + back[:, MODEL_WIDTH + LANES // 2 : MODEL_WIDTH + LANES // 2 + expert_count],
        0.0,
    )
    grad_logits = gate_weights * (
        grad_gates - jnp.sum(gate_weights * grad_gates, axis=1, keepdims=True)
    )
    grad_normed_ffn = back[:, :MODEL_WIDTH] + jnp.einsum(
        "te,de->td", grad_logits, router_wide, precision=PRECISE
    )
    grad_middle = upstream + norm_back(grad_normed_ffn, middle, inverse_ffn, gain_ffn)
    grad_branch = (RESIDUAL_SCALE * grad_middle).astype(BF16)
    grad_attended = dot(out_full, grad_branch, ((1,), (1,))).astype(BF16)
    grad_heads = all_to_all(grad_attended.reshape(shards, q_width, tile))

    grad_router = jnp.einsum("te,td->ed", grad_logits, normed_ffn, precision=PRECISE)
    grad_norm_ffn = jnp.sum(grad_normed_ffn * middle * inverse_ffn, axis=0)[None, :]
    fine = jnp.concatenate([grad_router, grad_norm_ffn], axis=0)
    fine_high = fine.astype(BF16)
    fine_low = (fine - fine_high.astype(F32)).astype(BF16)
    fine_rows = expert_count + 1
    fine = jnp.concatenate(
        [fine_high, fine_low, jnp.zeros((LANES - 2 * fine_rows, MODEL_WIDTH), BF16)], axis=0
    ).T
    block = MODEL_WIDTH // ctx_count
    early_parts = []
    for k in range(ctx_count):
        first = ((ctx - k) % ctx_count) * block
        part = lax.dynamic_slice_in_dim(attended, first, block, 0)
        early_parts.append(dot(part, grad_branch).astype(BF16))
    grad_heads, early_parts = meet(grad_heads, early_parts)
    early_parts = from_later(early_parts)

    out = attend_back(queries, grad_heads, outcome_wide, level, kv_parts, ctx_index)
    early_parts, gq, kv_out = meet(early_parts, out[0], out[1:])
    kv_back = from_later(kv_out)
    mix_back = from_later(tie(mix_parts, kv_back))
    at = jnp.stack([ctx, shard % 2]).astype(jnp.int32)
    own, other, late_parts = tail(
        gq, cosine, sine, normed, columns, fine, kv_back, early_parts, at, tile
    )
    chip_sum = (own.astype(F32) + send_core(other).astype(F32)).astype(BF16)
    token_back = to_chips(chip_sum)
    late = to_ctx(tie(late_parts, chip_sum)).astype(BF16)
    late = all_to_all(tie(late, token_back[1]).reshape(shards, share_rows, -1))
    expert_grads = unpack(share_first, share_last, depth, down_depth, MODEL_WIDTH)
    late, token_back, mix_back, expert_grads = meet(late, token_back, mix_back, expert_grads)
    block_out = (middle + RESIDUAL_SCALE * add_up(mix_back)).astype(BF16)
    first_row = (ctx * shards + shard) * share_rows
    own_gain = lax.dynamic_slice_in_dim(gain_attn, first_row, share_rows, 0)[:, None]
    grad_tokens, grad_query, grad_key, grad_value, grad_out, grad_gain, grad_gain_ffn, grad_router = (
        finish(
            late, own_weights, own_gain, grad_middle, tokens, inverse_attn, gain_attn, token_back,
            q_width, copies, expert_count
        )
    )
    return (
        block_out,
        grad_tokens,
        grad_query,
        grad_key,
        grad_value,
        grad_out,
        grad_gain[0],
        grad_gain_ffn[0],
        grad_router,
        *expert_grads,
    )


def solution(mesh):
    placed = (
        P(("ctx", "shard"), None),
        P("shard", None),
        P("shard", None),
        P("shard", None),
        P("shard", None),
        P("shard"),
        P("shard"),
        P("shard", None),
        P("shard", "ctx", None),
        P("shard", "ctx", None),
        P("shard", "ctx", None),
        P(("ctx", "shard"), None),
        P(("ctx", "shard"), None),
        P(("ctx", "shard"), None),
    )
    return jax.shard_map(
        local,
        mesh=mesh,
        in_specs=placed,
        out_specs=(
            P(("ctx", "shard"), None),
            P(("ctx", "shard"), None),
            P(("ctx", "shard"), None),
            P(("ctx", "shard"), None),
            P(("ctx", "shard"), None),
            P(("ctx", "shard"), None),
            P(("ctx", "shard")),
            P(("ctx", "shard")),
            P(("ctx", "shard"), None),
            P("shard", "ctx", None),
            P("shard", "ctx", None),
            P("shard", "ctx", None),
        ),
        check_vma=False,
    )
```

```python
import functools
import math

import jax
import jax.numpy as jnp
from jax import lax
from jax.experimental import pallas as pl
from jax.experimental.pallas import tpu as pltpu
from jax.sharding import PartitionSpec as P

MODEL_WIDTH = 1024
QUERY_HEADS = 16
KEY_VALUE_HEADS = 8
HEAD_SIZE = 64
FF = 512
TOPK = 8

NORM_EPS = 1e-06
RESIDUAL_SCALE = 0.22
SCORE_SCALE = 0.015625
ROPE_BASE = 10000.0
PRECISE = lax.Precision.HIGHEST
MASKED = -1e30
UNCHOSEN = 1 << 20
LANES = 128

F32 = jnp.float32
BF16 = jnp.bfloat16


def whole(shape):
    return pl.BlockSpec(tuple(shape), lambda i: (0,) * len(shape))


def dot(a, b, dims=((1,), (0,))):
    return lax.dot_general(a, b, (dims, ((), ())), preferred_element_type=F32)


def rotary_tables(positions):
    halfway = HEAD_SIZE // 2
    frequency = jnp.exp(
        jnp.arange(halfway, dtype=F32) * (-2.0 * math.log(ROPE_BASE) / HEAD_SIZE)
    )
    angles = frequency[:, None] * positions.astype(F32)[None, :]
    return (jnp.cos(angles), jnp.sin(angles))


def rotate(vectors, cosine, sine):
    rows, count = vectors.shape
    shaped = vectors.reshape(rows // HEAD_SIZE, 2, HEAD_SIZE // 2, count)
    front, behind = shaped[:, 0], shaped[:, 1]
    turned = jnp.stack(
        [front * cosine - behind * sine, behind * cosine + front * sine], axis=1
    )
    return turned.reshape(rows, count)


def rms_scale(value_rows):
    return lax.rsqrt(jnp.mean(value_rows * value_rows, axis=1, keepdims=True) + NORM_EPS)


def norm_back(upward, inputs, inverse_rms, gain_vector):
    weighted = upward * gain_vector.reshape(1, -1)
    cubed = inverse_rms * inverse_rms * inverse_rms
    return inverse_rms * weighted - inputs * cubed * jnp.mean(
        weighted * inputs, axis=1, keepdims=True
    )


def project_kernel(
    at_ref, columns_ref, cos_ref, sin_ref, *refs, count, tile, depth
):
    parts = refs[: 2 * count]
    normed_ref, q_ref, kv_ref, small_ref, block, gain = refs[2 * count :]
    shards = 2 * count
    width = normed_ref.shape[1]
    lane = lax.broadcasted_iota(jnp.int32, (1, width), 1) // depth
    gain[...] = jnp.zeros_like(gain)
    for k in range(count):
        for side in range(2):
            slot = at_ref[1] if side == 0 else 1 - at_ref[1]
            index = 2 * lax.rem(at_ref[0] - k + count, count) + slot
            part = parts[side * count + k]
            block[pl.ds(pl.multiple_of(index * tile, tile), tile), :] = part[:tile, :]
            small_ref[index] = part[tile:, :]
            row = part[tile : tile + 1, :].astype(F32)
            gain[...] += jnp.where(lane == index, row, 0.0)
    for s in range(shards):
        at = slice(s * tile, (s + 1) * tile)
        x = block[at, :].astype(F32)
        normed_ref[at, :] = (x * rms_scale(x) * gain[...]).astype(BF16)
    lin = dot(columns_ref[...].T, normed_ref[...], ((1,), (1,)))
    q_width = q_ref.shape[0]
    half = HEAD_SIZE // 2
    cosine, sine = cos_ref[...], sin_ref[...]

    def turn(first):
        front, behind = lin[first : first + half], lin[first + half : first + 2 * half]
        return front * cosine - behind * sine, behind * cosine + front * sine

    for h in range(q_width // HEAD_SIZE):
        front, behind = turn(h * HEAD_SIZE)
        at = h * HEAD_SIZE
        q_ref[at : at + half, :] = front.astype(BF16) * jnp.asarray(SCORE_SCALE, BF16)
        q_ref[at + half : at + 2 * half, :] = behind.astype(BF16) * jnp.asarray(SCORE_SCALE, BF16)
    front, behind = turn(q_width)
    kv_ref[:half, :] = front.astype(BF16)
    kv_ref[half:HEAD_SIZE, :] = behind.astype(BF16)
    kv_ref[HEAD_SIZE:, :] = lin[q_width + HEAD_SIZE :].astype(BF16)


def project(parts, others, columns, cosine, sine, at, tile, depth):
    count = len(parts)
    height, width = parts[0].shape
    rows = 2 * count * tile
    lin_width = columns.shape[1]
    shapes = [
        (rows, width),
        (lin_width - 2 * HEAD_SIZE, rows),
        (2 * HEAD_SIZE, rows),
        (2 * count, height - tile, width),
    ]
    args = [at, columns, cosine, sine, *parts, *others]
    return pl.pallas_call(
        functools.partial(project_kernel, count=count, tile=tile, depth=depth),
        grid=(1,),
        in_specs=[pl.BlockSpec(memory_space=pltpu.SMEM)] + [whole(v.shape) for v in args[1:]],
        out_specs=[whole(shape) for shape in shapes],
        out_shape=[jax.ShapeDtypeStruct(shape, BF16) for shape in shapes],
        scratch_shapes=[pltpu.VMEM((rows, width), BF16), pltpu.VMEM((1, width), F32)],
        compiler_params=pltpu.CompilerParams(vmem_limit_bytes=60 << 20),
        cost_estimate=pl.CostEstimate(
            flops=2 * rows * width * lin_width,
            transcendentals=0,
            bytes_accessed=4 * rows * width,
        ),
        name="project",
    )(*args)


def attention_blocks(rows):
    return min(512, rows)


def attend_kernel(c_ref, q_ref, *refs, ctx_count, heads, rows, block, tile):
    kv_refs = refs[:ctx_count]
    out_ref, wide_ref, log_ref = refs[ctx_count : ctx_count + 3]
    natural, peak, total, acc = refs[ctx_count + 3 :]
    step = pl.program_id(0)
    mine = c_ref[0]

    @pl.when(step == 0)
    def _():
        for k in range(ctx_count):

            @pl.when(mine >= k)
            def _(k=k):
                natural[k] = kv_refs[k][...].T

    zeros = jnp.zeros((HEAD_SIZE, block), BF16)
    wide_q = [
        jnp.concatenate([q_ref[h * HEAD_SIZE : (h + 1) * HEAD_SIZE, :], zeros], axis=0)
        for h in range(heads)
    ]
    for h in range(heads):
        peak[h] = jnp.full((1, block), MASKED, F32)
        total[h] = jnp.zeros((1, block), F32)
        acc[h] = jnp.zeros((HEAD_SIZE, block), F32)

    def visit(k, start, masked):
        keys = natural[k, pl.ds(start, block), :]
        values = kv_refs[k][HEAD_SIZE:, pl.ds(start, block)]
        for h in range(heads):
            scores = dot(keys, wide_q[h])
            if masked:
                place = lax.broadcasted_iota(jnp.int32, (block, block), 0)
                query = lax.broadcasted_iota(jnp.int32, (block, block), 1)
                scores = jnp.where(place <= query, scores, MASKED)
            old = peak[h]
            new = jnp.maximum(old, jnp.max(scores, axis=0, keepdims=True))
            shrink = jnp.exp(old - new)
            weights = jnp.exp(scores - new)
            peak[h] = new
            total[h] = total[h] * shrink + jnp.sum(weights, axis=0, keepdims=True)
            acc[h] = acc[h] * shrink + dot(values, weights.astype(BF16))

    def full(k):
        def body(j, carry):
            visit(k, pl.multiple_of(j * block, block), False)
            return carry

        return body

    for k in range(1, ctx_count):

        @pl.when(mine >= k)
        def _(k=k):
            lax.fori_loop(0, rows // block, full(k), 0, unroll=2)

    lax.fori_loop(0, step, full(0), 0)
    visit(0, pl.multiple_of(step * block, block), True)
    for h in range(heads):
        result = acc[h] / total[h]
        at = slice(h * HEAD_SIZE, (h + 1) * HEAD_SIZE)
        wide_ref[at, :] = result
        log_ref[h : h + 1, :] = peak[h] + jnp.log(total[h])
        for j in range(block // tile):
            out_ref[j, at, :] = result[:, j * tile : (j + 1) * tile].astype(BF16)


def attend(queries, key_values, ctx_index, tile):
    width, rows = queries.shape
    heads = width // HEAD_SIZE
    ctx_count = len(key_values)
    block = attention_blocks(rows)
    kv_width = key_values[0].shape[0]
    whole = pl.BlockSpec((kv_width, rows), lambda i, c: (0, 0))
    return pl.pallas_call(
        functools.partial(
            attend_kernel, ctx_count=ctx_count, heads=heads, rows=rows, block=block, tile=tile
        ),
        grid_spec=pltpu.PrefetchScalarGridSpec(
            num_scalar_prefetch=1,
            grid=(rows // block,),
            in_specs=[pl.BlockSpec((width, block), lambda i, c: (0, i))] + [whole] * ctx_count,
            out_specs=[
                pl.BlockSpec((block // tile, width, tile), lambda i, c: (i, 0, 0)),
                pl.BlockSpec((width, block), lambda i, c: (0, i)),
                pl.BlockSpec((heads, block), lambda i, c: (0, i)),
            ],
            scratch_shapes=[
                pltpu.VMEM((ctx_count, rows, kv_width), BF16),
                pltpu.VMEM((heads, 1, block), F32),
                pltpu.VMEM((heads, 1, block), F32),
                pltpu.VMEM((heads, HEAD_SIZE, block), F32),
            ],
        ),
        out_shape=[
            jax.ShapeDtypeStruct((rows // tile, width, tile), BF16),
            jax.ShapeDtypeStruct((width, rows), F32),
            jax.ShapeDtypeStruct((heads, rows), F32),
        ],
        compiler_params=pltpu.CompilerParams(
            dimension_semantics=("arbitrary",), vmem_limit_bytes=48 << 20
        ),
        cost_estimate=pl.CostEstimate(
            flops=64 * width * rows * rows * ctx_count // 2,
            transcendentals=heads * rows * rows * ctx_count // 2,
            bytes_accessed=2 * ctx_count * rows * kv_width,
        ),
        name="attend",
    )(ctx_index, queries, *key_values)


def attend_back_kernel(
    c_ref, q_ref, grad_ref, wide_ref, log_ref, *refs, ctx_count, heads, rows, block, tile
):
    kv_refs = refs[:ctx_count]
    gq_ref = refs[ctx_count]
    gkv_refs = refs[ctx_count + 1 : 2 * ctx_count + 1]
    natural, sums, gq_acc = refs[2 * ctx_count + 1 :]
    step = pl.program_id(0)
    last = pl.num_programs(0) - 1
    mine = c_ref[0]

    @pl.when(step == 0)
    def _():
        for k in range(ctx_count):

            @pl.when(mine >= k)
            def _(k=k):
                natural[k] = kv_refs[k][...].T
                sums[k] = jnp.zeros_like(sums[k])

    zeros = jnp.zeros((HEAD_SIZE, block), BF16)
    wide_q, wide_g, tall_q, tall_g, delta, level = [], [], [], [], [], []
    for h in range(heads):
        at = slice(h * HEAD_SIZE, (h + 1) * HEAD_SIZE)
        grad = jnp.concatenate([grad_ref[j, at, :] for j in range(block // tile)], axis=1)
        q_part = jnp.concatenate([q_ref[at, :], zeros], axis=0)
        g_part = jnp.concatenate([zeros, grad], axis=0)
        wide_q.append(q_part)
        wide_g.append(g_part)
        tall_q.append(q_part.T)
        tall_g.append(g_part.T)
        delta.append(jnp.sum(grad.astype(F32) * wide_ref[at, :], axis=0, keepdims=True))
        level.append(log_ref[h : h + 1, :])
        gq_acc[h] = jnp.zeros((HEAD_SIZE, block), F32)

    def visit(k, start, masked):
        both = natural[k, pl.ds(start, block), :]
        keys = kv_refs[k][:HEAD_SIZE, pl.ds(start, block)]
        add = None
        for h in range(heads):
            scores = dot(both, wide_q[h])
            if masked:
                place = lax.broadcasted_iota(jnp.int32, (block, block), 0)
                query = lax.broadcasted_iota(jnp.int32, (block, block), 1)
                scores = jnp.where(place <= query, scores, MASKED)
            weights = jnp.exp(scores - level[h])
            grad_probs = dot(both, wide_g[h])
            grad_scores = (weights * (grad_probs - delta[h])).astype(BF16)
            part = dot(grad_scores, tall_q[h]) + dot(weights.astype(BF16), tall_g[h])
            add = part if add is None else add + part
            gq_acc[h] += dot(keys, grad_scores)
        sums[k, pl.ds(start, block), :] += add

    def full(k):
        def body(j, carry):
            visit(k, pl.multiple_of(j * block, block), False)
            return carry

        return body

    for k in range(1, ctx_count):

        @pl.when(mine >= k)
        def _(k=k):
            lax.fori_loop(0, rows // block, full(k), 0, unroll=2)

    lax.fori_loop(0, step, full(0), 0)
    visit(0, pl.multiple_of(step * block, block), True)
    for h in range(heads):
        gq_ref[h * HEAD_SIZE : (h + 1) * HEAD_SIZE, :] = SCORE_SCALE * gq_acc[h]

    @pl.when(step == last)
    def _():
        gkv_refs[0][...] = sums[0]
        for k in range(1, ctx_count):

            @pl.when(mine >= k)
            def _(k=k):
                gkv_refs[k][...] = sums[k].astype(BF16)

            @pl.when(mine < k)
            def _(k=k):
                gkv_refs[k][...] = jnp.zeros((rows, sums.shape[2]), BF16)


def attend_back(queries, grads, wide, level, key_values, ctx_index):
    width, rows = queries.shape
    heads = width // HEAD_SIZE
    ctx_count = len(key_values)
    block = attention_blocks(rows)
    tile = grads.shape[2]
    kv_width = key_values[0].shape[0]
    whole = pl.BlockSpec((kv_width, rows), lambda i, c: (0, 0))
    tall = pl.BlockSpec((rows, kv_width), lambda i, c: (0, 0))
    return pl.pallas_call(
        functools.partial(
            attend_back_kernel, ctx_count=ctx_count, heads=heads, rows=rows, block=block, tile=tile
        ),
        grid_spec=pltpu.PrefetchScalarGridSpec(
            num_scalar_prefetch=1,
            grid=(rows // block,),
            in_specs=[
                pl.BlockSpec((width, block), lambda i, c: (0, i)),
                pl.BlockSpec((block // tile, width, tile), lambda i, c: (i, 0, 0)),
                pl.BlockSpec((width, block), lambda i, c: (0, i)),
                pl.BlockSpec((heads, block), lambda i, c: (0, i)),
            ]
            + [whole] * ctx_count,
            out_specs=[pl.BlockSpec((width, block), lambda i, c: (0, i))] + [tall] * ctx_count,
            scratch_shapes=[
                pltpu.VMEM((ctx_count, rows, kv_width), BF16),
                pltpu.VMEM((ctx_count, rows, kv_width), F32),
                pltpu.VMEM((heads, HEAD_SIZE, block), F32),
            ],
        ),
        out_shape=[jax.ShapeDtypeStruct((width, rows), F32)]
        + [
            jax.ShapeDtypeStruct((rows, kv_width), F32 if k == 0 else BF16)
            for k in range(ctx_count)
        ],
        compiler_params=pltpu.CompilerParams(
            dimension_semantics=("arbitrary",), vmem_limit_bytes=56 << 20
        ),
        cost_estimate=pl.CostEstimate(
            flops=96 * width * rows * rows * ctx_count // 2,
            transcendentals=heads * rows * rows * ctx_count // 2,
            bytes_accessed=4 * ctx_count * rows * kv_width,
        ),
        name="attend_back",
    )(ctx_index, queries, grads, wide, level, *key_values)


def tail_kernel(
    at_ref, gq_ref, cos_ref, sin_ref, normed_ref, columns_ref, fine_ref, *refs, ctx_count, tile
):
    kv_refs, early_refs = refs[:ctx_count], refs[ctx_count : 2 * ctx_count]
    own_ref, other_ref = refs[2 * ctx_count : 2 * ctx_count + 2]
    late_refs = refs[2 * ctx_count + 2 : 3 * ctx_count + 2]
    tall, late = refs[3 * ctx_count + 2 :]
    ctx, core = at_ref[0], at_ref[1]
    q_width = gq_ref.shape[0]
    lin_width = tall.shape[1]
    half = HEAD_SIZE // 2
    cosine, sine = cos_ref[...], sin_ref[...]

    def turn_back(vectors):
        front, behind = vectors[:half], vectors[half:]
        return [front * cosine + behind * sine, behind * cosine - front * sine]

    grad_kv = add_up([ref[...] for ref in kv_refs]).T
    pieces = []
    for h in range(q_width // HEAD_SIZE):
        pieces += turn_back(gq_ref[h * HEAD_SIZE : (h + 1) * HEAD_SIZE, :])
    pieces += turn_back(grad_kv[:HEAD_SIZE]) + [grad_kv[HEAD_SIZE:]]
    grad_lin = jnp.concatenate(pieces, axis=0).astype(BF16)
    tall[...] = grad_lin.T
    late[...] = dot(grad_lin, normed_ref[...]).astype(BF16).T
    block = late.shape[0] // ctx_count
    for k in range(ctx_count):
        first = pl.multiple_of(lax.rem(ctx - k + ctx_count, ctx_count) * block, block)
        late_refs[k][:, :lin_width] = late[pl.ds(first, block), :]
        late_refs[k][:, lin_width:] = fine_ref[pl.ds(first, block), :]
    early = add_up([ref[...] for ref in early_refs]).astype(BF16)
    chips = own_ref.shape[0]
    small = own_ref.shape[1] - tile
    swap = core == 1
    for chip in range(chips):
        at = [slice((2 * chip + j) * small, (2 * chip + j + 1) * small) for j in range(2)]
        own_ref[chip, tile:, :] = jnp.where(swap, early[at[1]], early[at[0]])
        other_ref[chip, tile:, :] = jnp.where(swap, early[at[0]], early[at[1]])
        for side, ref in ((core, own_ref), (1 - core, other_ref)):
            first = pl.multiple_of((2 * chip + side) * tile, tile)
            ref[chip, :tile, :] = dot(
                tall[pl.ds(first, tile), :], columns_ref[...], ((1,), (1,))
            ).astype(BF16)


def tail(gq, cosine, sine, normed, columns, fine, kv_back, early_back, at, tile):
    ctx_count = len(kv_back)
    rows, width = normed.shape
    lin_width = columns.shape[1]
    chips = rows // (2 * tile)
    small = early_back[0].shape[0] // (2 * chips)
    block = width // ctx_count
    args = [at, gq, cosine, sine, normed, columns, fine, *kv_back, *early_back]
    shapes = [((chips, tile + small, width), BF16)] * 2 + [
        ((block, lin_width + LANES), BF16)
    ] * ctx_count
    out = pl.pallas_call(
        functools.partial(tail_kernel, ctx_count=ctx_count, tile=tile),
        grid=(1,),
        in_specs=[pl.BlockSpec(memory_space=pltpu.SMEM)] + [whole(v.shape) for v in args[1:]],
        out_specs=[whole(shape) for shape, _ in shapes],
        out_shape=[jax.ShapeDtypeStruct(*shape) for shape in shapes],
        scratch_shapes=[pltpu.VMEM((rows, lin_width), BF16), pltpu.VMEM((width, lin_width), BF16)],
        compiler_params=pltpu.CompilerParams(vmem_limit_bytes=60 << 20),
        cost_estimate=pl.CostEstimate(
            flops=4 * rows * width * lin_width, transcendentals=0, bytes_accessed=12 * rows * width
        ),
        name="tail",
    )(*args)
    return out[0], out[1], out[2:]


def finish_kernel(
    late_ref, weight_ref, gain_ref, middle_ref, token_ref, inverse_ref, norm_ref, *refs,
    q_width, copies, experts, tile
):
    parts = refs[:-8]
    tokens_ref, q_ref, k_ref, v_ref, out_ref, attn_ref, ffn_ref, router_ref = refs[-8:]
    grad_normed = add_up([ref[:tile, :] for ref in parts])
    inputs = token_ref[...].astype(F32)
    tokens_ref[...] = middle_ref[...] + norm_back(
        grad_normed, inputs, inverse_ref[...], norm_ref[...]
    )
    out_ref[...] = add_up([ref[tile:, :] for ref in parts])
    shards, rows, _ = late_ref.shape
    width = q_width + 2 * HEAD_SIZE
    gain_grad = jnp.zeros((rows, 1), F32)
    values = [late_ref[s, :, :width].astype(F32) for s in range(shards)]
    for s in range(shards):
        weights = weight_ref[:, s * width : (s + 1) * width].astype(F32)
        gain_grad += jnp.sum(values[s] * weights, axis=1, keepdims=True)
    q_ref[...] = jnp.concatenate([v[:, :q_width] for v in values], axis=1)
    for ref, first in ((k_ref, q_width), (v_ref, q_width + HEAD_SIZE)):
        heads = [v[:, first : first + HEAD_SIZE] for v in values]
        ref[...] = jnp.concatenate(
            [add_up(heads[i : i + copies]) for i in range(0, shards, copies)], axis=1
        )
    fine = add_up([late_ref[s, :, width:] for s in range(shards)])
    count = experts + 1
    router_ref[...] = (fine[:, :experts] + fine[:, count : count + experts]).T
    ffn_ref[...] = (fine[:, experts:count] + fine[:, count + experts : 2 * count]).T
    attn_ref[...] = (gain_grad / gain_ref[...]).T


def finish(
    late, own_weights, own_gain, grad_middle, tokens, inverse, gain, token_back,
    q_width, copies, experts
):
    shards, rows, _ = late.shape
    tile, model = grad_middle.shape
    args = [late, own_weights, own_gain, grad_middle, tokens, inverse, gain[None, :], *token_back]
    kv_width = shards // copies * HEAD_SIZE
    shapes = [(tile, model), (rows, shards * q_width), (rows, kv_width), (rows, kv_width)]
    shapes += [(rows, model), (1, rows), (1, rows), (experts, rows)]
    return pl.pallas_call(
        functools.partial(
            finish_kernel, q_width=q_width, copies=copies, experts=experts, tile=tile
        ),
        grid=(1,),
        in_specs=[whole(v.shape) for v in args],
        out_specs=[whole(shape) for shape in shapes],
        out_shape=[jax.ShapeDtypeStruct(shape, F32) for shape in shapes],
        compiler_params=pltpu.CompilerParams(vmem_limit_bytes=60 << 20),
        cost_estimate=pl.CostEstimate(
            flops=0, transcendentals=0, bytes_accessed=16 * tile * model
        ),
        name="finish",
    )(*args)


def unpack_kernel(first_ref, last_ref, gate_ref, up_ref, down_ref):
    rows, down_rows = gate_ref.shape[0], down_ref.shape[0]
    split = first_ref.shape[0]
    for e in range(split + last_ref.shape[0]):
        source, i = (first_ref, e) if e < split else (last_ref, e - split)
        gate_ref[:, e, :] = source[i, :rows, :].astype(F32)
        up_ref[:, e, :] = source[i, rows : 2 * rows, :].astype(F32)
        for half in range(down_ref.shape[2] // FF):
            at = 2 * rows + half * down_rows
            down_ref[:, e, half * FF : (half + 1) * FF] = source[
                i, at : at + down_rows, :
            ].astype(F32)


def unpack(first, last, rows, down_rows, model):
    experts = first.shape[0] + last.shape[0]
    shapes = [(rows, experts, FF), (rows, experts, FF), (down_rows, experts, model)]
    return pl.pallas_call(
        unpack_kernel,
        grid=(1,),
        in_specs=[whole(first.shape), whole(last.shape)],
        out_specs=[whole(shape) for shape in shapes],
        out_shape=[jax.ShapeDtypeStruct(shape, F32) for shape in shapes],
        compiler_params=pltpu.CompilerParams(vmem_limit_bytes=60 << 20),
        cost_estimate=pl.CostEstimate(
            flops=0, transcendentals=0, bytes_accessed=6 * (first.size + last.size)
        ),
        name="unpack",
    )(first, last)


def expert_kernel(
    c_ref, *refs, ctx_count, experts, first, carried, final, tile, rows, down_rows
):
    refs = list(refs)

    def take(count):
        taken = refs[:count]
        del refs[:count]
        return taken

    x_refs, u_refs, (w_ref,) = take(ctx_count), take(ctx_count), take(1)
    carry_refs = take(3 if carried else 0)
    if final:
        gin_refs, mix_refs = take(ctx_count), take(ctx_count)
    else:
        sums = take(3)
    (grad_ref,) = take(1)
    if final:
        sums = take(3)
    gin_acc, mix_acc, dots = sums
    x_all, x_turned, u_all, share, hid, g_out, g_gate, g_up = refs
    shards = w_ref.shape[0]
    e = pl.program_id(0)
    last = pl.num_programs(0) - 1
    width = u_all.shape[1]
    count = ctx_count * tile
    chunk = min(2 * tile, count)
    column = c_ref[0] * experts + first + e

    @pl.when(e == 0)
    def _():
        for k in range(ctx_count):
            at = slice(k * tile, (k + 1) * tile)
            part = x_refs[k][:, :width]
            x_all[at, :] = part
            x_turned[:, at] = part.T
            u_all[at, :] = u_refs[k][...]
            share[at, :] = x_refs[k][:, width:].astype(F32)
        for i, ref in enumerate(sums):
            ref[...] = carry_refs[i][...] if carried else jnp.zeros_like(ref)

    lane = lax.broadcasted_iota(jnp.int32, (chunk, LANES), 1)
    picked = (lane == column) | (lane == column + LANES // 2)
    down = 2 * rows

    def gate_matrix():
        return w_ref[:, 0, 0:rows, :].reshape(shards * rows, FF)

    def up_matrix():
        return w_ref[:, 0, rows : 2 * rows, :].reshape(shards * rows, FF)

    def down_matrix(half):
        at = down + half * down_rows
        return w_ref[:, 0, at : at + down_rows, :].reshape(FF, FF)

    def one_chunk(j, carry):
        at = pl.ds(pl.multiple_of(j * chunk, chunk), chunk)
        x = x_all[at, :]
        gate = dot(x, gate_matrix())
        up = dot(x, up_matrix())
        sig = jax.nn.sigmoid(gate)
        silu = gate * sig
        hidden = (silu * up).astype(BF16)
        hid[at, :] = hidden
        weight = jnp.sum(jnp.where(picked, share[at, :], 0.0), axis=1, keepdims=True)
        upstream = u_all[at, :].astype(F32) * RESIDUAL_SCALE
        down_grad = (upstream * weight).astype(BF16)
        g_out[at, :] = down_grad
        gathered = jnp.zeros((chunk, 1), F32)
        grad_hidden = jnp.zeros((chunk, FF), F32)
        for half in range(width // FF):
            cols = slice(half * FF, (half + 1) * FF)
            matrix = down_matrix(half)
            made = dot(hidden, matrix).astype(BF16).astype(F32)
            mix_acc[at, cols] += weight * made
            gathered += jnp.sum(upstream[:, cols] * made, axis=1, keepdims=True)
            grad_hidden += dot(down_grad[:, cols], matrix, ((1,), (1,)))
        dots[at, :] += jnp.where(picked, gathered, 0.0)
        grad_gate = (grad_hidden * up * sig * (1.0 + gate * (1.0 - sig))).astype(BF16)
        grad_up = (grad_hidden * silu).astype(BF16)
        g_gate[at, :] = grad_gate
        g_up[at, :] = grad_up
        gin_acc[at, :] += dot(grad_gate, gate_matrix(), ((1,), (1,))) + dot(
            grad_up, up_matrix(), ((1,), (1,))
        )
        return carry

    lax.fori_loop(0, count // chunk, one_chunk, 0, unroll=True)
    grad_ref[:, 0, 0:rows, :] = (
        dot(x_turned[...], g_gate[...]).astype(BF16).reshape(shards, rows, FF)
    )
    grad_ref[:, 0, rows : 2 * rows, :] = (
        dot(x_turned[...], g_up[...]).astype(BF16).reshape(shards, rows, FF)
    )
    hid_turned = hid[...].T
    for half in range(width // FF):
        at = down + half * down_rows
        grad_ref[:, 0, at : at + down_rows, :] = (
            dot(hid_turned, g_out[:, half * FF : (half + 1) * FF])
            .astype(BF16)
            .reshape(shards, down_rows, FF)
        )

    if not final:
        return

    @pl.when(e == last)
    def _():
        for k in range(ctx_count):
            at = slice(k * tile, (k + 1) * tile)
            gin_refs[k][:, :width] = gin_acc[at, :].astype(BF16)
            high = dots[at, :].astype(BF16)
            gin_refs[k][:, width : width + LANES // 2] = high[:, : LANES // 2]
            low = (dots[at, :] - high.astype(F32)).astype(BF16)
            gin_refs[k][:, width + LANES // 2 :] = low[:, LANES // 2 :]
            mix_refs[k][...] = mix_acc[at, :].astype(BF16)


def run_experts(x_parts, u_parts, weights, ctx_index, experts, first, carry, final):
    ctx_count = len(x_parts)
    tile, width = u_parts[0].shape
    shards, group, all_rows, _ = weights.shape
    rows = width // shards
    down_rows = FF // shards
    count = ctx_count * tile

    def flat(*shape, **options):
        return pl.BlockSpec(shape, lambda e, c: (0,) * len(shape), **options)

    expert_block = (shards, 1, all_rows, FF)
    by_expert = pl.BlockSpec(expert_block, lambda e, c: (0, e, 0, 0))
    made = pl.BlockSpec(expert_block, lambda e, c: (0, e, 0, 0))
    sum_shapes = [(count, width), (count, width), (count, LANES)]
    if final:
        out_specs = [flat(tile, width + LANES)] * ctx_count + [flat(tile, width)] * ctx_count
        out_shape = [jax.ShapeDtypeStruct((tile, width + LANES), BF16)] * ctx_count + [
            jax.ShapeDtypeStruct((tile, width), BF16)
        ] * ctx_count
        sum_scratch = [pltpu.VMEM(shape, F32) for shape in sum_shapes]
    else:
        out_specs = [flat(*shape) for shape in sum_shapes]
        out_shape = [jax.ShapeDtypeStruct(shape, F32) for shape in sum_shapes]
        sum_scratch = []
    once = pl.Buffered(1)
    out = pl.pallas_call(
        functools.partial(
            expert_kernel,
            ctx_count=ctx_count,
            experts=experts,
            first=first,
            carried=bool(carry),
            final=final,
            tile=tile,
            rows=rows,
            down_rows=down_rows,
        ),
        grid_spec=pltpu.PrefetchScalarGridSpec(
            num_scalar_prefetch=1,
            grid=(group,),
            in_specs=[flat(tile, width + LANES)] * ctx_count
            + [flat(tile, width)] * ctx_count
            + [by_expert]
            + [flat(*shape, pipeline_mode=once) for shape in sum_shapes[: len(carry)]],
            out_specs=out_specs + [made],
            scratch_shapes=sum_scratch
            + [
                pltpu.VMEM((count, width), BF16),
                pltpu.VMEM((width, count), BF16),
                pltpu.VMEM((count, width), BF16),
                pltpu.VMEM((count, LANES), F32),
                pltpu.VMEM((count, FF), BF16),
                pltpu.VMEM((count, width), BF16),
                pltpu.VMEM((count, FF), BF16),
                pltpu.VMEM((count, FF), BF16),
            ],
        ),
        out_shape=out_shape + [jax.ShapeDtypeStruct((shards, group, all_rows, FF), BF16)],
        compiler_params=pltpu.CompilerParams(
            dimension_semantics=("arbitrary",), vmem_limit_bytes=60 << 20
        ),
        cost_estimate=pl.CostEstimate(
            flops=24 * group * count * width * FF,
            transcendentals=group * count * FF,
            bytes_accessed=4 * shards * group * all_rows * FF,
        ),
        name="experts",
    )(ctx_index, *x_parts, *u_parts, weights, *carry)
    if final:
        return out[:ctx_count], out[ctx_count : 2 * ctx_count], out[2 * ctx_count]
    return out[:3], out[3]


def send_ctx(value, by):
    count = lax.axis_size("ctx")
    return lax.ppermute(value, "ctx", [(i, (i + by) % count) for i in range(count)])


def from_ctx(value):
    return [value] + [send_ctx(value, k) for k in range(1, lax.axis_size("ctx"))]


def from_later(parts):
    return [parts[0]] + [send_ctx(parts[k], -k) for k in range(1, len(parts))]


def add_up(parts):
    total = parts[0].astype(F32)
    for part in parts[1:]:
        total = total + part.astype(F32)
    return total


def to_ctx(parts):
    return add_up(from_later(parts))


def all_to_all(value):
    return lax.all_to_all(value, "shard", split_axis=0, concat_axis=0, tiled=True)


def send_chip(value, by):
    chips = lax.axis_size("shard") // 2
    return lax.ppermute(
        value,
        "shard",
        [(2 * i + j, 2 * ((i + by) % chips) + j) for i in range(chips) for j in range(2)],
    )


def send_core(value):
    return lax.ppermute(value, "shard", [(i, i ^ 1) for i in range(lax.axis_size("shard"))])


def tie(value, *others):
    return lax.optimization_barrier((value, others))[0]


def relay_chips(value):
    chips = lax.axis_size("shard") // 2
    chip = lax.axis_index("shard") // 2

    def step(block, by, done):
        pairs = [
            (2 * i + j, 2 * (i + by) + j)
            for i in range(chips)
            if 0 <= i + by < chips and 0 <= i - by * done < chips
            for j in range(2)
        ]
        return lax.ppermute(block, "shard", pairs)

    up, down = [value], [value]
    for k in range(1, chips):
        up.append(step(up[-1], 1, k - 1))
        down.append(step(down[-1], -1, k - 1))
    return [value] + [jnp.where(chip >= k, up[k], down[chips - k]) for k in range(1, chips)]


def meet(*values):
    return lax.optimization_barrier(values)


def arrive(own, send, count):
    return [own] + [send(own, k) for k in range(1, count)]


def assemble_kernel(at_ref, *refs, count, lead):
    parts, out_ref = refs[:-1], refs[-1]
    for k in range(count):
        index = lax.rem(at_ref[0] - k + count, count)
        for side in range(2):
            slot = at_ref[1] if side == 0 else 1 - at_ref[1]
            out_ref[(slice(None),) * lead + (index, slot)] = parts[side * count + k][...]


def assemble(parts, others, first, lead):
    count = len(parts)
    shape, dtype = parts[0].shape, parts[0].dtype
    at = jnp.stack([first, lax.axis_index("shard") % 2]).astype(jnp.int32)
    out_shape = shape[:lead] + (count, 2) + shape[lead:]
    return pl.pallas_call(
        functools.partial(assemble_kernel, count=count, lead=lead),
        grid=(1,),
        in_specs=[pl.BlockSpec(memory_space=pltpu.SMEM)] + [whole(shape)] * (2 * count),
        out_specs=whole(out_shape),
        out_shape=jax.ShapeDtypeStruct(out_shape, dtype),
        compiler_params=pltpu.CompilerParams(vmem_limit_bytes=60 << 20),
        cost_estimate=pl.CostEstimate(
            flops=0, transcendentals=0, bytes_accessed=8 * count * parts[0].size
        ),
        name="assemble",
    )(at, *parts, *others)


def spread_start(value):
    shards, ctx_count = lax.axis_size("shard"), lax.axis_size("ctx")
    shard, ctx = lax.axis_index("shard"), lax.axis_index("ctx")
    core, chips = shard % 2, shards // 2
    rows, columns = value.shape
    pieces = lax.dynamic_index_in_dim(
        value.reshape(ctx_count, 2, rows // (2 * ctx_count), columns), ctx, 0, keepdims=False
    )
    mine = lax.dynamic_index_in_dim(pieces, core, 0, keepdims=False)
    theirs = send_core(lax.dynamic_index_in_dim(pieces, 1 - core, 0, keepdims=False))
    pair = jnp.stack([jnp.where(core == 0, mine, theirs), jnp.where(core == 0, theirs, mine)])
    return arrive(pair, send_chip, chips)


def spread_join(parts):
    chips = len(parts)
    chip = lax.axis_index("shard") // 2
    joined = jnp.zeros((chips,) + parts[0].shape, parts[0].dtype)
    for k, part in enumerate(parts):
        joined = lax.dynamic_update_index_in_dim(joined, part, (chip - k) % chips, 0)
    return joined


def spread_ctx(joined):
    return arrive(joined, send_ctx, lax.axis_size("ctx"))


def spread_end(parts, others):
    return assemble(parts, others, lax.axis_index("ctx"), 2).reshape(MODEL_WIDTH, -1)


def halve_chips(blocks):
    shards = lax.axis_size("shard")
    chip = lax.axis_index("shard") // 2
    distance, first = 1, None
    while True:
        pairs = blocks.reshape((blocks.shape[0] // 2, 2) + blocks.shape[1:])
        side = (chip // distance) % 2
        keep = lax.dynamic_index_in_dim(pairs, side, 1, keepdims=False)
        sent = lax.dynamic_index_in_dim(pairs, 1 - side, 1, keepdims=False)
        came = lax.ppermute(sent, "shard", [(i, i ^ (2 * distance)) for i in range(shards)])
        first = came if first is None else first
        if keep.shape[0] == 1:
            return [keep[0], came[0]], first
        blocks = (keep.astype(F32) + came.astype(F32)).astype(BF16)
        distance *= 2


def local(
    tokens,
    w_query,
    key_weight,
    value_weight,
    w_out,
    norm_attn,
    norm_ffn,
    w_router,
    w_gate,
    w_up,
    w_down,
    cotangent,
    choices,
    priority,
):
    shards = lax.axis_size("shard")
    ctx_count = lax.axis_size("ctx")
    ctx = lax.axis_index("ctx")
    shard = lax.axis_index("shard")
    ctx_index = ctx.astype(jnp.int32).reshape(1)
    tile = tokens.shape[0]
    rows = tile * shards
    expert_count = w_router.shape[1]
    experts = w_gate.shape[1]
    depth = w_query.shape[0]
    down_depth = w_down.shape[0]
    capacity = tile * TOPK * 5 // (4 * expert_count)
    heads = QUERY_HEADS // shards
    copies = max(1, shards // KEY_VALUE_HEADS)
    q_width = heads * HEAD_SIZE
    width = q_width + 2 * HEAD_SIZE
    share_rows = MODEL_WIDTH // (ctx_count * shards)

    halves = w_down.reshape(down_depth, experts, MODEL_WIDTH // FF, FF)
    expert_rows = jnp.concatenate(
        [
            jnp.transpose(w_gate, (1, 0, 2)),
            jnp.transpose(w_up, (1, 0, 2)),
            jnp.transpose(halves, (1, 2, 0, 3)).reshape(experts, -1, FF),
        ],
        axis=1,
    )
    grouped = jnp.concatenate(
        [
            w_query.reshape(depth, shards, q_width),
            jnp.repeat(key_weight.reshape(depth, KEY_VALUE_HEADS, HEAD_SIZE), copies, axis=1),
            jnp.repeat(value_weight.reshape(depth, KEY_VALUE_HEADS, HEAD_SIZE), copies, axis=1),
        ],
        axis=2,
    )
    small = jnp.concatenate(
        [
            jnp.tile(norm_attn, MODEL_WIDTH // depth)[None, :],
            jnp.tile(norm_ffn, MODEL_WIDTH // depth)[None, :],
            w_router.reshape(-1, MODEL_WIDTH),
        ],
        axis=0,
    )
    small = jnp.pad(small, ((0, 16 - small.shape[0]), (0, 0)))
    chips = shards // 2
    token_parts = relay_chips(jnp.concatenate([tokens, small], axis=0))
    columns = all_to_all(jnp.transpose(grouped, (1, 0, 2))).reshape(MODEL_WIDTH, width)
    cot_parts = from_ctx(cotangent)
    token_parts, columns, cot_parts = meet(token_parts, columns, cot_parts)
    positions = ctx * rows + jnp.arange(rows, dtype=jnp.int32)
    cosine, sine = rotary_tables(positions)
    split = 1
    weights_first = lax.all_gather(expert_rows[:split], "shard", axis=0, tiled=False)
    weights_last = lax.all_gather(
        tie(expert_rows[split:], weights_first, token_parts), "shard", axis=0, tiled=False
    )

    place = jnp.stack([shard // 2, shard % 2]).astype(jnp.int32)
    normed, queries, key_values, small = project(
        token_parts,
        [send_core(part) for part in token_parts],
        columns,
        cosine,
        sine,
        place,
        tile,
        depth,
    )
    gain_attn = small[:, 0, :depth].reshape(MODEL_WIDTH).astype(F32)
    gain_ffn = small[:, 1, :depth].reshape(MODEL_WIDTH).astype(F32)
    router_rows = w_router.size // MODEL_WIDTH
    router_wide = small[:, 2 : 2 + router_rows].reshape(MODEL_WIDTH, expert_count).astype(F32)
    kv_parts = from_ctx(key_values)
    out_parts = spread_start(tie(w_out, key_values))
    outcome, outcome_wide, level = attend(queries, kv_parts, ctx_index, tile)
    outcome, out_parts = meet(outcome, out_parts)
    out_ctx = spread_ctx(spread_join(out_parts))
    out_other = [send_core(part) for part in out_ctx]

    chosen = choices[:, :, None] == jnp.arange(expert_count, dtype=jnp.int32)[None, None, :]
    rank = jnp.min(jnp.where(chosen, priority[:, :, None], UNCHOSEN), axis=1)
    earlier = jnp.sum((rank.T[:, None, :] < rank.T[:, :, None]).astype(F32), axis=2).T
    named = rank < UNCHOSEN
    kept = named & (earlier < capacity)

    attended = all_to_all(outcome).reshape(MODEL_WIDTH, tile)
    attended, out_ctx, out_other = meet(attended, out_ctx, out_other)
    out_full = spread_end(out_ctx, out_other)
    inputs = tokens.astype(F32)
    inverse_attn = rms_scale(inputs)
    branch = dot(attended, out_full, ((0,), (0,)))
    middle = inputs + RESIDUAL_SCALE * branch
    inverse_ffn = rms_scale(middle)
    normed_ffn = middle * inverse_ffn * gain_ffn[None, :]
    logits = jnp.dot(normed_ffn, router_wide, precision=PRECISE)
    masked_logits = jnp.where(named, logits, MASKED)
    raised = jnp.where(
        named, jnp.exp(masked_logits - jnp.max(masked_logits, axis=1, keepdims=True)), 0.0
    )
    gate_weights = raised / jnp.sum(raised, axis=1, keepdims=True)
    kept_weights = jnp.where(kept, gate_weights, 0.0)
    high = kept_weights.astype(BF16)
    low = (kept_weights - high.astype(F32)).astype(BF16)
    spare = ((0, 0), (0, LANES // 2 - expert_count))
    packet = jnp.concatenate([normed_ffn.astype(BF16), jnp.pad(high, spare), jnp.pad(low, spare)], 1)
    x_parts = from_ctx(packet)
    grouped_rows = tie(grouped.reshape(depth, shards * width), packet)
    own_weights = lax.ppermute(
        lax.dynamic_slice_in_dim(
            grouped_rows, ctx * share_rows, share_rows, 0
        ),
        ("ctx", "shard"),
        [(j * shards + i, ctx_count * i + j) for j in range(ctx_count) for i in range(shards)],
    )
    x_parts, own_weights = meet(x_parts, own_weights)
    carry, grads_first = run_experts(
        x_parts, cot_parts, weights_first, ctx_index, experts, 0, [], False
    )
    gin_parts, mix_parts, grads_last = run_experts(
        x_parts, cot_parts, weights_last, ctx_index, experts, split, carry, True
    )
    back = to_ctx(gin_parts)
    share_first = lax.psum_scatter(grads_first, "shard", scatter_dimension=0, tiled=False)
    share_last = lax.psum_scatter(
        tie(grads_last, share_first, back), "shard", scatter_dimension=0, tiled=False
    )
    upstream = cotangent.astype(F32)
    grad_gates = jnp.where(
        kept,
        back[:, MODEL_WIDTH : MODEL_WIDTH + expert_count]
        + back[:, MODEL_WIDTH + LANES // 2 : MODEL_WIDTH + LANES // 2 + expert_count],
        0.0,
    )
    grad_logits = gate_weights * (
        grad_gates - jnp.sum(gate_weights * grad_gates, axis=1, keepdims=True)
    )
    grad_normed_ffn = back[:, :MODEL_WIDTH] + jnp.einsum(
        "te,de->td", grad_logits, router_wide, precision=PRECISE
    )
    grad_middle = upstream + norm_back(grad_normed_ffn, middle, inverse_ffn, gain_ffn)
    grad_branch = (RESIDUAL_SCALE * grad_middle).astype(BF16)
    grad_attended = dot(out_full, grad_branch, ((1,), (1,))).astype(BF16)
    grad_heads = all_to_all(grad_attended.reshape(shards, q_width, tile))

    grad_router = jnp.einsum("te,td->ed", grad_logits, normed_ffn, precision=PRECISE)
    grad_norm_ffn = jnp.sum(grad_normed_ffn * middle * inverse_ffn, axis=0)[None, :]
    fine = jnp.concatenate([grad_router, grad_norm_ffn], axis=0)
    fine_high = fine.astype(BF16)
    fine_low = (fine - fine_high.astype(F32)).astype(BF16)
    fine_rows = expert_count + 1
    fine = jnp.concatenate(
        [fine_high, fine_low, jnp.zeros((LANES - 2 * fine_rows, MODEL_WIDTH), BF16)], axis=0
    ).T
    block = MODEL_WIDTH // ctx_count
    early_parts = []
    for k in range(ctx_count):
        first = ((ctx - k) % ctx_count) * block
        part = lax.dynamic_slice_in_dim(attended, first, block, 0)
        early_parts.append(dot(part, grad_branch).astype(BF16))
    grad_heads, early_parts = meet(grad_heads, early_parts)
    early_parts = from_later(early_parts)

    out = attend_back(queries, grad_heads, outcome_wide, level, kv_parts, ctx_index)
    early_parts, gq, kv_out = meet(early_parts, out[0], out[1:])
    kv_back = from_later(kv_out)
    mix_back = from_later(tie(mix_parts, kv_back))
    at = jnp.stack([ctx, shard % 2]).astype(jnp.int32)
    own, other, late_parts = tail(
        gq, cosine, sine, normed, columns, fine, kv_back, early_parts, at, tile
    )
    chip_sum = (own.astype(F32) + send_core(other).astype(F32)).astype(BF16)
    token_back, halfway = halve_chips(chip_sum)
    late = to_ctx(tie(late_parts, chip_sum)).astype(BF16)
    late = all_to_all(tie(late, halfway).reshape(shards, share_rows, -1))
    expert_grads = unpack(share_first, share_last, depth, down_depth, MODEL_WIDTH)
    block_out = (middle + RESIDUAL_SCALE * add_up(mix_back)).astype(BF16)
    late, token_back, block_out, expert_grads = meet(late, token_back, block_out, expert_grads)
    first_row = (ctx * shards + shard) * share_rows
    own_gain = lax.dynamic_slice_in_dim(gain_attn, first_row, share_rows, 0)[:, None]
    grad_tokens, grad_query, grad_key, grad_value, grad_out, grad_gain, grad_gain_ffn, grad_router = (
        finish(
            late, own_weights, own_gain, grad_middle, tokens, inverse_attn, gain_attn, token_back,
            q_width, copies, expert_count
        )
    )
    return (
        block_out,
        grad_tokens,
        grad_query,
        grad_key,
        grad_value,
        grad_out,
        grad_gain[0],
        grad_gain_ffn[0],
        grad_router.T,
        *expert_grads,
    )


def solution(mesh):
    placed = (
        P(("ctx", "shard"), None),
        P("shard", None),
        P("shard", None),
        P("shard", None),
        P("shard", None),
        P("shard"),
        P("shard"),
        P("shard", None),
        P("shard", "ctx", None),
        P("shard", "ctx", None),
        P("shard", "ctx", None),
        P(("ctx", "shard"), None),
        P(("ctx", "shard"), None),
        P(("ctx", "shard"), None),
    )
    return jax.shard_map(
        local,
        mesh=mesh,
        in_specs=placed,
        out_specs=(
            P(("ctx", "shard"), None),
            P(("ctx", "shard"), None),
            P(("ctx", "shard"), None),
            P(("ctx", "shard"), None),
            P(("ctx", "shard"), None),
            P(("ctx", "shard"), None),
            P(("ctx", "shard")),
            P(("ctx", "shard")),
            P(("ctx", "shard"), None),
            P("shard", "ctx", None),
            P("shard", "ctx", None),
            P("shard", "ctx", None),
        ),
        check_vma=False,
    )
```

```python
import functools
import math

import jax
import jax.numpy as jnp
from jax import lax
from jax.experimental import pallas as pl
from jax.experimental.pallas import tpu as pltpu
from jax.sharding import PartitionSpec as P

MODEL_WIDTH = 1024
QUERY_HEADS = 16
KEY_VALUE_HEADS = 8
HEAD_SIZE = 64
FF = 512
TOPK = 8

NORM_EPS = 1e-06
RESIDUAL_SCALE = 0.22
SCORE_SCALE = 0.015625
ROPE_BASE = 10000.0
PRECISE = lax.Precision.HIGHEST
MASKED = -1e30
UNCHOSEN = 1 << 20
LANES = 128

F32 = jnp.float32
BF16 = jnp.bfloat16


def whole(shape):
    return pl.BlockSpec(tuple(shape), lambda i: (0,) * len(shape))


def dot(a, b, dims=((1,), (0,))):
    return lax.dot_general(a, b, (dims, ((), ())), preferred_element_type=F32)


def rotary_tables(positions):
    halfway = HEAD_SIZE // 2
    frequency = jnp.exp(
        jnp.arange(halfway, dtype=F32) * (-2.0 * math.log(ROPE_BASE) / HEAD_SIZE)
    )
    angles = frequency[:, None] * positions.astype(F32)[None, :]
    return (jnp.cos(angles), jnp.sin(angles))


def rotate(vectors, cosine, sine):
    rows, count = vectors.shape
    shaped = vectors.reshape(rows // HEAD_SIZE, 2, HEAD_SIZE // 2, count)
    front, behind = shaped[:, 0], shaped[:, 1]
    turned = jnp.stack(
        [front * cosine - behind * sine, behind * cosine + front * sine], axis=1
    )
    return turned.reshape(rows, count)


def rms_scale(value_rows):
    return lax.rsqrt(jnp.mean(value_rows * value_rows, axis=1, keepdims=True) + NORM_EPS)


def norm_back(upward, inputs, inverse_rms, gain_vector):
    weighted = upward * gain_vector.reshape(1, -1)
    cubed = inverse_rms * inverse_rms * inverse_rms
    return inverse_rms * weighted - inputs * cubed * jnp.mean(
        weighted * inputs, axis=1, keepdims=True
    )


def project_kernel(
    at_ref, columns_ref, cos_ref, sin_ref, *refs, count, tile, depth
):
    parts = refs[: 2 * count]
    normed_ref, q_ref, kv_ref, small_ref, block, gain = refs[2 * count :]
    shards = 2 * count
    width = normed_ref.shape[1]
    lane = lax.broadcasted_iota(jnp.int32, (1, width), 1) // depth
    gain[...] = jnp.zeros_like(gain)
    for k in range(count):
        for side in range(2):
            slot = at_ref[1] if side == 0 else 1 - at_ref[1]
            index = 2 * lax.rem(at_ref[0] - k + count, count) + slot
            part = parts[side * count + k]
            block[pl.ds(pl.multiple_of(index * tile, tile), tile), :] = part[:tile, :]
            small_ref[index] = part[tile:, :]
            row = part[tile : tile + 1, :].astype(F32)
            gain[...] += jnp.where(lane == index, row, 0.0)
    for s in range(shards):
        at = slice(s * tile, (s + 1) * tile)
        x = block[at, :].astype(F32)
        normed_ref[at, :] = (x * rms_scale(x) * gain[...]).astype(BF16)
    lin = dot(columns_ref[...].T, normed_ref[...], ((1,), (1,)))
    q_width = q_ref.shape[0]
    half = HEAD_SIZE // 2
    cosine, sine = cos_ref[...], sin_ref[...]

    def turn(first):
        front, behind = lin[first : first + half], lin[first + half : first + 2 * half]
        return front * cosine - behind * sine, behind * cosine + front * sine

    for h in range(q_width // HEAD_SIZE):
        front, behind = turn(h * HEAD_SIZE)
        at = h * HEAD_SIZE
        q_ref[at : at + half, :] = front.astype(BF16) * jnp.asarray(SCORE_SCALE, BF16)
        q_ref[at + half : at + 2 * half, :] = behind.astype(BF16) * jnp.asarray(SCORE_SCALE, BF16)
    front, behind = turn(q_width)
    kv_ref[:half, :] = front.astype(BF16)
    kv_ref[half:HEAD_SIZE, :] = behind.astype(BF16)
    kv_ref[HEAD_SIZE:, :] = lin[q_width + HEAD_SIZE :].astype(BF16)


def project(parts, others, columns, cosine, sine, at, tile, depth):
    count = len(parts)
    height, width = parts[0].shape
    rows = 2 * count * tile
    lin_width = columns.shape[1]
    shapes = [
        (rows, width),
        (lin_width - 2 * HEAD_SIZE, rows),
        (2 * HEAD_SIZE, rows),
        (2 * count, height - tile, width),
    ]
    args = [at, columns, cosine, sine, *parts, *others]
    return pl.pallas_call(
        functools.partial(project_kernel, count=count, tile=tile, depth=depth),
        grid=(1,),
        in_specs=[pl.BlockSpec(memory_space=pltpu.SMEM)] + [whole(v.shape) for v in args[1:]],
        out_specs=[whole(shape) for shape in shapes],
        out_shape=[jax.ShapeDtypeStruct(shape, BF16) for shape in shapes],
        scratch_shapes=[pltpu.VMEM((rows, width), BF16), pltpu.VMEM((1, width), F32)],
        compiler_params=pltpu.CompilerParams(vmem_limit_bytes=60 << 20),
        cost_estimate=pl.CostEstimate(
            flops=2 * rows * width * lin_width,
            transcendentals=0,
            bytes_accessed=4 * rows * width,
        ),
        name="project",
    )(*args)


def attention_blocks(rows):
    return min(512, rows)


def attend_kernel(c_ref, q_ref, *refs, ctx_count, heads, rows, block, tile):
    kv_refs = refs[:ctx_count]
    out_ref, wide_ref, log_ref = refs[ctx_count : ctx_count + 3]
    natural, peak, total, acc = refs[ctx_count + 3 :]
    step = pl.program_id(0)
    mine = c_ref[0]

    @pl.when(step == 0)
    def _():
        for k in range(ctx_count):

            @pl.when(mine >= k)
            def _(k=k):
                natural[k] = kv_refs[k][...].T

    zeros = jnp.zeros((HEAD_SIZE, block), BF16)
    wide_q = [
        jnp.concatenate([q_ref[h * HEAD_SIZE : (h + 1) * HEAD_SIZE, :], zeros], axis=0)
        for h in range(heads)
    ]
    for h in range(heads):
        peak[h] = jnp.full((1, block), MASKED, F32)
        total[h] = jnp.zeros((1, block), F32)
        acc[h] = jnp.zeros((HEAD_SIZE, block), F32)

    def visit(k, start, masked):
        keys = natural[k, pl.ds(start, block), :]
        values = kv_refs[k][HEAD_SIZE:, pl.ds(start, block)]
        for h in range(heads):
            scores = dot(keys, wide_q[h])
            if masked:
                place = lax.broadcasted_iota(jnp.int32, (block, block), 0)
                query = lax.broadcasted_iota(jnp.int32, (block, block), 1)
                scores = jnp.where(place <= query, scores, MASKED)
            old = peak[h]
            new = jnp.maximum(old, jnp.max(scores, axis=0, keepdims=True))
            shrink = jnp.exp(old - new)
            weights = jnp.exp(scores - new)
            peak[h] = new
            total[h] = total[h] * shrink + jnp.sum(weights, axis=0, keepdims=True)
            acc[h] = acc[h] * shrink + dot(values, weights.astype(BF16))

    def full(k):
        def body(j, carry):
            visit(k, pl.multiple_of(j * block, block), False)
            return carry

        return body

    for k in range(1, ctx_count):

        @pl.when(mine >= k)
        def _(k=k):
            lax.fori_loop(0, rows // block, full(k), 0, unroll=2)

    lax.fori_loop(0, step, full(0), 0)
    visit(0, pl.multiple_of(step * block, block), True)
    for h in range(heads):
        result = acc[h] / total[h]
        at = slice(h * HEAD_SIZE, (h + 1) * HEAD_SIZE)
        wide_ref[at, :] = result
        log_ref[h : h + 1, :] = peak[h] + jnp.log(total[h])
        for j in range(block // tile):
            out_ref[j, at, :] = result[:, j * tile : (j + 1) * tile].astype(BF16)


def attend(queries, key_values, ctx_index, tile):
    width, rows = queries.shape
    heads = width // HEAD_SIZE
    ctx_count = len(key_values)
    block = attention_blocks(rows)
    kv_width = key_values[0].shape[0]
    whole = pl.BlockSpec((kv_width, rows), lambda i, c: (0, 0))
    return pl.pallas_call(
        functools.partial(
            attend_kernel, ctx_count=ctx_count, heads=heads, rows=rows, block=block, tile=tile
        ),
        grid_spec=pltpu.PrefetchScalarGridSpec(
            num_scalar_prefetch=1,
            grid=(rows // block,),
            in_specs=[pl.BlockSpec((width, block), lambda i, c: (0, i))] + [whole] * ctx_count,
            out_specs=[
                pl.BlockSpec((block // tile, width, tile), lambda i, c: (i, 0, 0)),
                pl.BlockSpec((width, block), lambda i, c: (0, i)),
                pl.BlockSpec((heads, block), lambda i, c: (0, i)),
            ],
            scratch_shapes=[
                pltpu.VMEM((ctx_count, rows, kv_width), BF16),
                pltpu.VMEM((heads, 1, block), F32),
                pltpu.VMEM((heads, 1, block), F32),
                pltpu.VMEM((heads, HEAD_SIZE, block), F32),
            ],
        ),
        out_shape=[
            jax.ShapeDtypeStruct((rows // tile, width, tile), BF16),
            jax.ShapeDtypeStruct((width, rows), F32),
            jax.ShapeDtypeStruct((heads, rows), F32),
        ],
        compiler_params=pltpu.CompilerParams(
            dimension_semantics=("arbitrary",), vmem_limit_bytes=60 << 20
        ),
        cost_estimate=pl.CostEstimate(
            flops=64 * width * rows * rows * ctx_count // 2,
            transcendentals=heads * rows * rows * ctx_count // 2,
            bytes_accessed=2 * ctx_count * rows * kv_width,
        ),
        name="attend",
    )(ctx_index, queries, *key_values)


def attend_back_kernel(
    c_ref, q_ref, grad_ref, wide_ref, log_ref, *refs, ctx_count, heads, rows, block, tile
):
    kv_refs = refs[:ctx_count]
    gq_ref = refs[ctx_count]
    gkv_refs = refs[ctx_count + 1 : 2 * ctx_count + 1]
    natural, sums, gq_acc = refs[2 * ctx_count + 1 :]
    step = pl.program_id(0)
    last = pl.num_programs(0) - 1
    mine = c_ref[0]

    @pl.when(step == 0)
    def _():
        for k in range(ctx_count):

            @pl.when(mine >= k)
            def _(k=k):
                natural[k] = kv_refs[k][...].T
                sums[k] = jnp.zeros_like(sums[k])

    zeros = jnp.zeros((HEAD_SIZE, block), BF16)
    wide_q, wide_g, tall_q, tall_g, delta, level = [], [], [], [], [], []
    for h in range(heads):
        at = slice(h * HEAD_SIZE, (h + 1) * HEAD_SIZE)
        grad = jnp.concatenate([grad_ref[j, at, :] for j in range(block // tile)], axis=1)
        q_part = jnp.concatenate([q_ref[at, :], zeros], axis=0)
        g_part = jnp.concatenate([zeros, grad], axis=0)
        wide_q.append(q_part)
        wide_g.append(g_part)
        tall_q.append(q_part.T)
        tall_g.append(g_part.T)
        delta.append(jnp.sum(grad.astype(F32) * wide_ref[at, :], axis=0, keepdims=True))
        level.append(log_ref[h : h + 1, :])
        gq_acc[h] = jnp.zeros((HEAD_SIZE, block), F32)

    def visit(k, start, masked):
        both = natural[k, pl.ds(start, block), :]
        keys = kv_refs[k][:HEAD_SIZE, pl.ds(start, block)]
        add = None
        for h in range(heads):
            scores = dot(both, wide_q[h])
            if masked:
                place = lax.broadcasted_iota(jnp.int32, (block, block), 0)
                query = lax.broadcasted_iota(jnp.int32, (block, block), 1)
                scores = jnp.where(place <= query, scores, MASKED)
            weights = jnp.exp(scores - level[h])
            grad_probs = dot(both, wide_g[h])
            grad_scores = (weights * (grad_probs - delta[h])).astype(BF16)
            part = dot(grad_scores, tall_q[h]) + dot(weights.astype(BF16), tall_g[h])
            add = part if add is None else add + part
            gq_acc[h] += dot(keys, grad_scores)
        sums[k, pl.ds(start, block), :] += add

    def full(k):
        def body(j, carry):
            visit(k, pl.multiple_of(j * block, block), False)
            return carry

        return body

    for k in range(1, ctx_count):

        @pl.when(mine >= k)
        def _(k=k):
            lax.fori_loop(0, rows // block, full(k), 0, unroll=2)

    lax.fori_loop(0, step, full(0), 0)
    visit(0, pl.multiple_of(step * block, block), True)
    for h in range(heads):
        gq_ref[h * HEAD_SIZE : (h + 1) * HEAD_SIZE, :] = SCORE_SCALE * gq_acc[h]

    @pl.when(step == last)
    def _():
        gkv_refs[0][...] = sums[0]
        for k in range(1, ctx_count):

            @pl.when(mine >= k)
            def _(k=k):
                gkv_refs[k][...] = sums[k].astype(BF16)

            @pl.when(mine < k)
            def _(k=k):
                gkv_refs[k][...] = jnp.zeros((rows, sums.shape[2]), BF16)


def attend_back(queries, grads, wide, level, key_values, ctx_index):
    width, rows = queries.shape
    heads = width // HEAD_SIZE
    ctx_count = len(key_values)
    block = attention_blocks(rows)
    tile = grads.shape[2]
    kv_width = key_values[0].shape[0]
    whole = pl.BlockSpec((kv_width, rows), lambda i, c: (0, 0))
    tall = pl.BlockSpec((rows, kv_width), lambda i, c: (0, 0))
    return pl.pallas_call(
        functools.partial(
            attend_back_kernel, ctx_count=ctx_count, heads=heads, rows=rows, block=block, tile=tile
        ),
        grid_spec=pltpu.PrefetchScalarGridSpec(
            num_scalar_prefetch=1,
            grid=(rows // block,),
            in_specs=[
                pl.BlockSpec((width, block), lambda i, c: (0, i)),
                pl.BlockSpec((block // tile, width, tile), lambda i, c: (i, 0, 0)),
                pl.BlockSpec((width, block), lambda i, c: (0, i)),
                pl.BlockSpec((heads, block), lambda i, c: (0, i)),
            ]
            + [whole] * ctx_count,
            out_specs=[pl.BlockSpec((width, block), lambda i, c: (0, i))] + [tall] * ctx_count,
            scratch_shapes=[
                pltpu.VMEM((ctx_count, rows, kv_width), BF16),
                pltpu.VMEM((ctx_count, rows, kv_width), F32),
                pltpu.VMEM((heads, HEAD_SIZE, block), F32),
            ],
        ),
        out_shape=[jax.ShapeDtypeStruct((width, rows), F32)]
        + [
            jax.ShapeDtypeStruct((rows, kv_width), F32 if k == 0 else BF16)
            for k in range(ctx_count)
        ],
        compiler_params=pltpu.CompilerParams(
            dimension_semantics=("arbitrary",), vmem_limit_bytes=60 << 20
        ),
        cost_estimate=pl.CostEstimate(
            flops=96 * width * rows * rows * ctx_count // 2,
            transcendentals=heads * rows * rows * ctx_count // 2,
            bytes_accessed=4 * ctx_count * rows * kv_width,
        ),
        name="attend_back",
    )(ctx_index, queries, grads, wide, level, *key_values)


def tail_kernel(
    at_ref, gq_ref, cos_ref, sin_ref, normed_ref, columns_ref, fine_ref, *refs, ctx_count, tile
):
    kv_refs = refs[:ctx_count]
    own_ref, other_ref = refs[ctx_count : ctx_count + 2]
    late_refs = refs[ctx_count + 2 : 2 * ctx_count + 2]
    tall, late = refs[2 * ctx_count + 2 :]
    ctx, core = at_ref[0], at_ref[1]
    q_width = gq_ref.shape[0]
    lin_width = tall.shape[1]
    half = HEAD_SIZE // 2
    cosine, sine = cos_ref[...], sin_ref[...]

    def turn_back(vectors):
        front, behind = vectors[:half], vectors[half:]
        return [front * cosine + behind * sine, behind * cosine - front * sine]

    grad_kv = add_up([ref[...] for ref in kv_refs]).T
    pieces = []
    for h in range(q_width // HEAD_SIZE):
        pieces += turn_back(gq_ref[h * HEAD_SIZE : (h + 1) * HEAD_SIZE, :])
    pieces += turn_back(grad_kv[:HEAD_SIZE]) + [grad_kv[HEAD_SIZE:]]
    grad_lin = jnp.concatenate(pieces, axis=0).astype(BF16)
    tall[...] = grad_lin.T
    late[...] = dot(grad_lin, normed_ref[...]).astype(BF16).T
    block = late.shape[0] // ctx_count
    for k in range(ctx_count):
        first = pl.multiple_of(lax.rem(ctx - k + ctx_count, ctx_count) * block, block)
        late_refs[k][:, :lin_width] = late[pl.ds(first, block), :]
        late_refs[k][:, lin_width:] = fine_ref[pl.ds(first, block), :]
    chips = own_ref.shape[0]
    for chip in range(chips):
        for side, ref in ((core, own_ref), (1 - core, other_ref)):
            first = pl.multiple_of((2 * chip + side) * tile, tile)
            ref[chip] = dot(
                tall[pl.ds(first, tile), :], columns_ref[...], ((1,), (1,))
            ).astype(BF16)


def tail(gq, cosine, sine, normed, columns, fine, kv_back, at, tile):
    ctx_count = len(kv_back)
    rows, width = normed.shape
    lin_width = columns.shape[1]
    chips = rows // (2 * tile)
    block = width // ctx_count
    args = [at, gq, cosine, sine, normed, columns, fine, *kv_back]
    shapes = [((chips, tile, width), BF16)] * 2 + [
        ((block, lin_width + LANES), BF16)
    ] * ctx_count
    out = pl.pallas_call(
        functools.partial(tail_kernel, ctx_count=ctx_count, tile=tile),
        grid=(1,),
        in_specs=[pl.BlockSpec(memory_space=pltpu.SMEM)] + [whole(v.shape) for v in args[1:]],
        out_specs=[whole(shape) for shape, _ in shapes],
        out_shape=[jax.ShapeDtypeStruct(*shape) for shape in shapes],
        scratch_shapes=[pltpu.VMEM((rows, lin_width), BF16), pltpu.VMEM((width, lin_width), BF16)],
        compiler_params=pltpu.CompilerParams(vmem_limit_bytes=60 << 20),
        cost_estimate=pl.CostEstimate(
            flops=4 * rows * width * lin_width, transcendentals=0, bytes_accessed=12 * rows * width
        ),
        name="tail",
    )(*args)
    return out[0], out[1], out[2:]


def finish_kernel(
    late_ref, weight_ref, gain_ref, middle_ref, token_ref, inverse_ref, norm_ref, *refs,
    q_width, copies, experts, tile
):
    parts = refs[:-8]
    tokens_ref, q_ref, k_ref, v_ref, out_ref, attn_ref, ffn_ref, router_ref = refs[-8:]
    parts, out_parts = parts[: len(parts) // 2], parts[len(parts) // 2 :]
    grad_normed = add_up([ref[...] for ref in parts])
    inputs = token_ref[...].astype(F32)
    tokens_ref[...] = middle_ref[...] + norm_back(
        grad_normed, inputs, inverse_ref[...], norm_ref[...]
    )
    out_ref[...] = add_up([ref[...] for ref in out_parts])
    shards, rows, _ = late_ref.shape
    width = q_width + 2 * HEAD_SIZE
    gain_grad = jnp.zeros((rows, 1), F32)
    values = [late_ref[s, :, :width].astype(F32) for s in range(shards)]
    for s in range(shards):
        weights = weight_ref[:, s * width : (s + 1) * width].astype(F32)
        gain_grad += jnp.sum(values[s] * weights, axis=1, keepdims=True)
    q_ref[...] = jnp.concatenate([v[:, :q_width] for v in values], axis=1)
    for ref, first in ((k_ref, q_width), (v_ref, q_width + HEAD_SIZE)):
        heads = [v[:, first : first + HEAD_SIZE] for v in values]
        ref[...] = jnp.concatenate(
            [add_up(heads[i : i + copies]) for i in range(0, shards, copies)], axis=1
        )
    fine = add_up([late_ref[s, :, width:] for s in range(shards)])
    count = experts + 1
    router_ref[...] = (fine[:, :experts] + fine[:, count : count + experts]).T
    ffn_ref[...] = (fine[:, experts:count] + fine[:, count + experts : 2 * count]).T
    attn_ref[...] = (gain_grad / gain_ref[...]).T


def finish(
    late, own_weights, own_gain, grad_middle, tokens, inverse, gain, token_back,
    q_width, copies, experts
):
    shards, rows, _ = late.shape
    tile, model = grad_middle.shape
    args = [late, own_weights, own_gain, grad_middle, tokens, inverse, gain[None, :], *token_back]
    kv_width = shards // copies * HEAD_SIZE
    shapes = [(tile, model), (rows, shards * q_width), (rows, kv_width), (rows, kv_width)]
    shapes += [(rows, model), (1, rows), (1, rows), (experts, rows)]
    return pl.pallas_call(
        functools.partial(
            finish_kernel, q_width=q_width, copies=copies, experts=experts, tile=tile
        ),
        grid=(1,),
        in_specs=[whole(v.shape) for v in args],
        out_specs=[whole(shape) for shape in shapes],
        out_shape=[jax.ShapeDtypeStruct(shape, F32) for shape in shapes],
        compiler_params=pltpu.CompilerParams(vmem_limit_bytes=60 << 20),
        cost_estimate=pl.CostEstimate(
            flops=0, transcendentals=0, bytes_accessed=16 * tile * model
        ),
        name="finish",
    )(*args)


def unpack_kernel(first_ref, last_ref, gate_ref, up_ref, down_ref):
    rows, down_rows = gate_ref.shape[0], down_ref.shape[0]
    split = first_ref.shape[0]
    for e in range(split + last_ref.shape[0]):
        source, i = (first_ref, e) if e < split else (last_ref, e - split)
        gate_ref[:, e, :] = source[i, :rows, :].astype(F32)
        up_ref[:, e, :] = source[i, rows : 2 * rows, :].astype(F32)
        for half in range(down_ref.shape[2] // FF):
            at = 2 * rows + half * down_rows
            down_ref[:, e, half * FF : (half + 1) * FF] = source[
                i, at : at + down_rows, :
            ].astype(F32)


def unpack(first, last, rows, down_rows, model):
    experts = first.shape[0] + last.shape[0]
    shapes = [(rows, experts, FF), (rows, experts, FF), (down_rows, experts, model)]
    return pl.pallas_call(
        unpack_kernel,
        grid=(1,),
        in_specs=[whole(first.shape), whole(last.shape)],
        out_specs=[whole(shape) for shape in shapes],
        out_shape=[jax.ShapeDtypeStruct(shape, F32) for shape in shapes],
        compiler_params=pltpu.CompilerParams(vmem_limit_bytes=60 << 20),
        cost_estimate=pl.CostEstimate(
            flops=0, transcendentals=0, bytes_accessed=6 * (first.size + last.size)
        ),
        name="unpack",
    )(first, last)


def expert_kernel(
    c_ref, *refs, ctx_count, experts, first, carried, final, tile, rows, down_rows
):
    refs = list(refs)

    def take(count):
        taken = refs[:count]
        del refs[:count]
        return taken

    x_refs, u_refs, (w_ref,) = take(ctx_count), take(ctx_count), take(1)
    carry_refs = take(3 if carried else 0)
    if final:
        gin_refs, mix_refs = take(ctx_count), take(ctx_count)
    else:
        sums = take(3)
    (grad_ref,) = take(1)
    if final:
        sums = take(3)
    gin_acc, mix_acc, dots = sums
    x_all, x_turned, u_all, share, hid, g_out, g_gate, g_up = refs
    shards = w_ref.shape[0]
    e = pl.program_id(0)
    last = pl.num_programs(0) - 1
    width = u_all.shape[1]
    count = ctx_count * tile
    chunk = min(2 * tile, count)
    column = c_ref[0] * experts + first + e

    @pl.when(e == 0)
    def _():
        for k in range(ctx_count):
            at = slice(k * tile, (k + 1) * tile)
            part = x_refs[k][:, :width]
            x_all[at, :] = part
            x_turned[:, at] = part.T
            u_all[at, :] = u_refs[k][...]
            share[at, :] = x_refs[k][:, width:].astype(F32)
        for i, ref in enumerate(sums):
            ref[...] = carry_refs[i][...] if carried else jnp.zeros_like(ref)

    lane = lax.broadcasted_iota(jnp.int32, (chunk, LANES), 1)
    picked = (lane == column) | (lane == column + LANES // 2)
    down = 2 * rows

    def gate_matrix():
        return w_ref[:, 0, 0:rows, :].reshape(shards * rows, FF)

    def up_matrix():
        return w_ref[:, 0, rows : 2 * rows, :].reshape(shards * rows, FF)

    def down_matrix(half):
        at = down + half * down_rows
        return w_ref[:, 0, at : at + down_rows, :].reshape(FF, FF)

    def one_chunk(j, carry):
        at = pl.ds(pl.multiple_of(j * chunk, chunk), chunk)
        x = x_all[at, :]
        gate = dot(x, gate_matrix())
        up = dot(x, up_matrix())
        sig = jax.nn.sigmoid(gate)
        silu = gate * sig
        hidden = (silu * up).astype(BF16)
        hid[at, :] = hidden
        weight = jnp.sum(jnp.where(picked, share[at, :], 0.0), axis=1, keepdims=True)
        upstream = u_all[at, :].astype(F32) * RESIDUAL_SCALE
        down_grad = (upstream * weight).astype(BF16)
        g_out[at, :] = down_grad
        gathered = jnp.zeros((chunk, 1), F32)
        grad_hidden = jnp.zeros((chunk, FF), F32)
        for half in range(width // FF):
            cols = slice(half * FF, (half + 1) * FF)
            matrix = down_matrix(half)
            made = dot(hidden, matrix).astype(BF16).astype(F32)
            mix_acc[at, cols] += weight * made
            gathered += jnp.sum(upstream[:, cols] * made, axis=1, keepdims=True)
            grad_hidden += dot(down_grad[:, cols], matrix, ((1,), (1,)))
        dots[at, :] += jnp.where(picked, gathered, 0.0)
        grad_gate = (grad_hidden * up * sig * (1.0 + gate * (1.0 - sig))).astype(BF16)
        grad_up = (grad_hidden * silu).astype(BF16)
        g_gate[at, :] = grad_gate
        g_up[at, :] = grad_up
        gin_acc[at, :] += dot(grad_gate, gate_matrix(), ((1,), (1,))) + dot(
            grad_up, up_matrix(), ((1,), (1,))
        )
        return carry

    lax.fori_loop(0, count // chunk, one_chunk, 0, unroll=True)
    grad_ref[:, 0, 0:rows, :] = (
        dot(x_turned[...], g_gate[...]).astype(BF16).reshape(shards, rows, FF)
    )
    grad_ref[:, 0, rows : 2 * rows, :] = (
        dot(x_turned[...], g_up[...]).astype(BF16).reshape(shards, rows, FF)
    )
    hid_turned = hid[...].T
    for half in range(width // FF):
        at = down + half * down_rows
        grad_ref[:, 0, at : at + down_rows, :] = (
            dot(hid_turned, g_out[:, half * FF : (half + 1) * FF])
            .astype(BF16)
            .reshape(shards, down_rows, FF)
        )

    if not final:
        return

    @pl.when(e == last)
    def _():
        for k in range(ctx_count):
            at = slice(k * tile, (k + 1) * tile)
            gin_refs[k][:, :width] = gin_acc[at, :].astype(BF16)
            high = dots[at, :].astype(BF16)
            gin_refs[k][:, width : width + LANES // 2] = high[:, : LANES // 2]
            low = (dots[at, :] - high.astype(F32)).astype(BF16)
            gin_refs[k][:, width + LANES // 2 :] = low[:, LANES // 2 :]
            mix_refs[k][...] = mix_acc[at, :].astype(BF16)


def run_experts(x_parts, u_parts, weights, ctx_index, experts, first, carry, final):
    ctx_count = len(x_parts)
    tile, width = u_parts[0].shape
    shards, group, all_rows, _ = weights.shape
    rows = width // shards
    down_rows = FF // shards
    count = ctx_count * tile

    def flat(*shape, **options):
        return pl.BlockSpec(shape, lambda e, c: (0,) * len(shape), **options)

    expert_block = (shards, 1, all_rows, FF)
    by_expert = pl.BlockSpec(expert_block, lambda e, c: (0, e, 0, 0))
    made = pl.BlockSpec(expert_block, lambda e, c: (0, e, 0, 0))
    sum_shapes = [(count, width), (count, width), (count, LANES)]
    if final:
        out_specs = [flat(tile, width + LANES)] * ctx_count + [flat(tile, width)] * ctx_count
        out_shape = [jax.ShapeDtypeStruct((tile, width + LANES), BF16)] * ctx_count + [
            jax.ShapeDtypeStruct((tile, width), BF16)
        ] * ctx_count
        sum_scratch = [pltpu.VMEM(shape, F32) for shape in sum_shapes]
    else:
        out_specs = [flat(*shape) for shape in sum_shapes]
        out_shape = [jax.ShapeDtypeStruct(shape, F32) for shape in sum_shapes]
        sum_scratch = []
    once = pl.Buffered(1)
    out = pl.pallas_call(
        functools.partial(
            expert_kernel,
            ctx_count=ctx_count,
            experts=experts,
            first=first,
            carried=bool(carry),
            final=final,
            tile=tile,
            rows=rows,
            down_rows=down_rows,
        ),
        grid_spec=pltpu.PrefetchScalarGridSpec(
            num_scalar_prefetch=1,
            grid=(group,),
            in_specs=[flat(tile, width + LANES)] * ctx_count
            + [flat(tile, width)] * ctx_count
            + [by_expert]
            + [flat(*shape, pipeline_mode=once) for shape in sum_shapes[: len(carry)]],
            out_specs=out_specs + [made],
            scratch_shapes=sum_scratch
            + [
                pltpu.VMEM((count, width), BF16),
                pltpu.VMEM((width, count), BF16),
                pltpu.VMEM((count, width), BF16),
                pltpu.VMEM((count, LANES), F32),
                pltpu.VMEM((count, FF), BF16),
                pltpu.VMEM((count, width), BF16),
                pltpu.VMEM((count, FF), BF16),
                pltpu.VMEM((count, FF), BF16),
            ],
        ),
        out_shape=out_shape + [jax.ShapeDtypeStruct((shards, group, all_rows, FF), BF16)],
        compiler_params=pltpu.CompilerParams(
            dimension_semantics=("arbitrary",), vmem_limit_bytes=60 << 20
        ),
        cost_estimate=pl.CostEstimate(
            flops=24 * group * count * width * FF,
            transcendentals=group * count * FF,
            bytes_accessed=4 * shards * group * all_rows * FF,
        ),
        name="experts",
    )(ctx_index, *x_parts, *u_parts, weights, *carry)
    if final:
        return out[:ctx_count], out[ctx_count : 2 * ctx_count], out[2 * ctx_count]
    return out[:3], out[3]


def send_ctx(value, by):
    count = lax.axis_size("ctx")
    return lax.ppermute(value, "ctx", [(i, (i + by) % count) for i in range(count)])


def from_ctx(value):
    return [value] + [send_ctx(value, k) for k in range(1, lax.axis_size("ctx"))]


def from_later(parts):
    return [parts[0]] + [send_ctx(parts[k], -k) for k in range(1, len(parts))]


def add_up(parts):
    total = parts[0].astype(F32)
    for part in parts[1:]:
        total = total + part.astype(F32)
    return total


def to_ctx(parts):
    return add_up(from_later(parts))


def all_to_all(value):
    return lax.all_to_all(value, "shard", split_axis=0, concat_axis=0, tiled=True)


def send_chip(value, by):
    chips = lax.axis_size("shard") // 2
    return lax.ppermute(
        value,
        "shard",
        [(2 * i + j, 2 * ((i + by) % chips) + j) for i in range(chips) for j in range(2)],
    )


def send_core(value):
    return lax.ppermute(value, "shard", [(i, i ^ 1) for i in range(lax.axis_size("shard"))])


def tie(value, *others):
    return lax.optimization_barrier((value, others))[0]


def relay_chips(value):
    chips = lax.axis_size("shard") // 2
    chip = lax.axis_index("shard") // 2

    def step(block, by, done):
        pairs = [
            (2 * i + j, 2 * (i + by) + j)
            for i in range(chips)
            if 0 <= i + by < chips and 0 <= i - by * done < chips
            for j in range(2)
        ]
        return lax.ppermute(block, "shard", pairs)

    up, down = [value], [value]
    for k in range(1, chips):
        up.append(step(up[-1], 1, k - 1))
        down.append(step(down[-1], -1, k - 1))
    return [value] + [jnp.where(chip >= k, up[k], down[chips - k]) for k in range(1, chips)]


def meet(*values):
    return lax.optimization_barrier(values)


def arrive(own, send, count):
    return [own] + [send(own, k) for k in range(1, count)]


def assemble_kernel(at_ref, *refs, count, lead):
    parts, out_ref = refs[:-1], refs[-1]
    for k in range(count):
        index = lax.rem(at_ref[0] - k + count, count)
        for side in range(2):
            slot = at_ref[1] if side == 0 else 1 - at_ref[1]
            out_ref[(slice(None),) * lead + (index, slot)] = parts[side * count + k][...]


def assemble(parts, others, first, lead):
    count = len(parts)
    shape, dtype = parts[0].shape, parts[0].dtype
    at = jnp.stack([first, lax.axis_index("shard") % 2]).astype(jnp.int32)
    out_shape = shape[:lead] + (count, 2) + shape[lead:]
    return pl.pallas_call(
        functools.partial(assemble_kernel, count=count, lead=lead),
        grid=(1,),
        in_specs=[pl.BlockSpec(memory_space=pltpu.SMEM)] + [whole(shape)] * (2 * count),
        out_specs=whole(out_shape),
        out_shape=jax.ShapeDtypeStruct(out_shape, dtype),
        compiler_params=pltpu.CompilerParams(vmem_limit_bytes=60 << 20),
        cost_estimate=pl.CostEstimate(
            flops=0, transcendentals=0, bytes_accessed=8 * count * parts[0].size
        ),
        name="assemble",
    )(at, *parts, *others)


def spread_start(value):
    shards, ctx_count = lax.axis_size("shard"), lax.axis_size("ctx")
    shard, ctx = lax.axis_index("shard"), lax.axis_index("ctx")
    core, chips = shard % 2, shards // 2
    rows, columns = value.shape
    pieces = lax.dynamic_index_in_dim(
        value.reshape(ctx_count, 2, rows // (2 * ctx_count), columns), ctx, 0, keepdims=False
    )
    mine = lax.dynamic_index_in_dim(pieces, core, 0, keepdims=False)
    theirs = send_core(lax.dynamic_index_in_dim(pieces, 1 - core, 0, keepdims=False))
    pair = jnp.stack([jnp.where(core == 0, mine, theirs), jnp.where(core == 0, theirs, mine)])
    return arrive(pair, send_chip, chips)


def spread_join(parts):
    chips = len(parts)
    chip = lax.axis_index("shard") // 2
    joined = jnp.zeros((chips,) + parts[0].shape, parts[0].dtype)
    for k, part in enumerate(parts):
        joined = lax.dynamic_update_index_in_dim(joined, part, (chip - k) % chips, 0)
    return joined


def spread_ctx(joined):
    return arrive(joined, send_ctx, lax.axis_size("ctx"))


def spread_end(parts, others):
    return assemble(parts, others, lax.axis_index("ctx"), 2).reshape(MODEL_WIDTH, -1)


def halve_chips(blocks):
    shards = lax.axis_size("shard")
    chip = lax.axis_index("shard") // 2
    distance, first = 1, None
    while True:
        pairs = blocks.reshape((blocks.shape[0] // 2, 2) + blocks.shape[1:])
        side = (chip // distance) % 2
        keep = lax.dynamic_index_in_dim(pairs, side, 1, keepdims=False)
        sent = lax.dynamic_index_in_dim(pairs, 1 - side, 1, keepdims=False)
        came = lax.ppermute(sent, "shard", [(i, i ^ (2 * distance)) for i in range(shards)])
        first = came if first is None else first
        if keep.shape[0] == 1:
            return [keep[0], came[0]], first
        blocks = (keep.astype(F32) + came.astype(F32)).astype(BF16)
        distance *= 2


def local(
    tokens,
    w_query,
    key_weight,
    value_weight,
    w_out,
    norm_attn,
    norm_ffn,
    w_router,
    w_gate,
    w_up,
    w_down,
    cotangent,
    choices,
    priority,
):
    shards = lax.axis_size("shard")
    ctx_count = lax.axis_size("ctx")
    ctx = lax.axis_index("ctx")
    shard = lax.axis_index("shard")
    ctx_index = ctx.astype(jnp.int32).reshape(1)
    tile = tokens.shape[0]
    rows = tile * shards
    expert_count = w_router.shape[1]
    experts = w_gate.shape[1]
    depth = w_query.shape[0]
    down_depth = w_down.shape[0]
    capacity = tile * TOPK * 5 // (4 * expert_count)
    heads = QUERY_HEADS // shards
    copies = max(1, shards // KEY_VALUE_HEADS)
    q_width = heads * HEAD_SIZE
    width = q_width + 2 * HEAD_SIZE
    share_rows = MODEL_WIDTH // (ctx_count * shards)

    halves = w_down.reshape(down_depth, experts, MODEL_WIDTH // FF, FF)
    expert_rows = jnp.concatenate(
        [
            jnp.transpose(w_gate, (1, 0, 2)),
            jnp.transpose(w_up, (1, 0, 2)),
            jnp.transpose(halves, (1, 2, 0, 3)).reshape(experts, -1, FF),
        ],
        axis=1,
    )
    grouped = jnp.concatenate(
        [
            w_query.reshape(depth, shards, q_width),
            jnp.repeat(key_weight.reshape(depth, KEY_VALUE_HEADS, HEAD_SIZE), copies, axis=1),
            jnp.repeat(value_weight.reshape(depth, KEY_VALUE_HEADS, HEAD_SIZE), copies, axis=1),
        ],
        axis=2,
    )
    small = jnp.concatenate(
        [
            jnp.tile(norm_attn, MODEL_WIDTH // depth)[None, :],
            jnp.tile(norm_ffn, MODEL_WIDTH // depth)[None, :],
            w_router.reshape(-1, MODEL_WIDTH),
        ],
        axis=0,
    )
    small = jnp.pad(small, ((0, 16 - small.shape[0]), (0, 0)))
    chips = shards // 2
    token_parts = relay_chips(jnp.concatenate([tokens, small], axis=0))
    columns = all_to_all(jnp.transpose(grouped, (1, 0, 2))).reshape(MODEL_WIDTH, width)
    cot_parts = from_ctx(cotangent)
    token_parts, columns, cot_parts = meet(token_parts, columns, cot_parts)
    positions = ctx * rows + jnp.arange(rows, dtype=jnp.int32)
    cosine, sine = rotary_tables(positions)
    split = 1
    weights_first = lax.all_gather(expert_rows[:split], "shard", axis=0, tiled=False)
    weights_last = lax.all_gather(
        tie(expert_rows[split:], weights_first, token_parts), "shard", axis=0, tiled=False
    )

    place = jnp.stack([shard // 2, shard % 2]).astype(jnp.int32)
    normed, queries, key_values, small = project(
        token_parts,
        [send_core(part) for part in token_parts],
        columns,
        cosine,
        sine,
        place,
        tile,
        depth,
    )
    gain_attn = small[:, 0, :depth].reshape(MODEL_WIDTH).astype(F32)
    gain_ffn = small[:, 1, :depth].reshape(MODEL_WIDTH).astype(F32)
    router_rows = w_router.size // MODEL_WIDTH
    router_wide = small[:, 2 : 2 + router_rows].reshape(MODEL_WIDTH, expert_count).astype(F32)
    kv_parts = from_ctx(key_values)
    out_parts = spread_start(tie(w_out, key_values))
    outcome, outcome_wide, level = attend(queries, kv_parts, ctx_index, tile)
    outcome, out_parts = meet(outcome, out_parts)
    out_ctx = spread_ctx(spread_join(out_parts))
    out_other = [send_core(part) for part in out_ctx]

    chosen = choices[:, :, None] == jnp.arange(expert_count, dtype=jnp.int32)[None, None, :]
    rank = jnp.min(jnp.where(chosen, priority[:, :, None], UNCHOSEN), axis=1)
    earlier = jnp.sum((rank.T[:, None, :] < rank.T[:, :, None]).astype(F32), axis=2).T
    named = rank < UNCHOSEN
    kept = named & (earlier < capacity)

    attended = all_to_all(outcome).reshape(MODEL_WIDTH, tile)
    attended, out_ctx, out_other = meet(attended, out_ctx, out_other)
    out_full = spread_end(out_ctx, out_other)
    inputs = tokens.astype(F32)
    inverse_attn = rms_scale(inputs)
    branch = dot(attended, out_full, ((0,), (0,)))
    middle = inputs + RESIDUAL_SCALE * branch
    inverse_ffn = rms_scale(middle)
    normed_ffn = middle * inverse_ffn * gain_ffn[None, :]
    logits = jnp.dot(normed_ffn, router_wide, precision=PRECISE)
    masked_logits = jnp.where(named, logits, MASKED)
    raised = jnp.where(
        named, jnp.exp(masked_logits - jnp.max(masked_logits, axis=1, keepdims=True)), 0.0
    )
    gate_weights = raised / jnp.sum(raised, axis=1, keepdims=True)
    kept_weights = jnp.where(kept, gate_weights, 0.0)
    high = kept_weights.astype(BF16)
    low = (kept_weights - high.astype(F32)).astype(BF16)
    spare = ((0, 0), (0, LANES // 2 - expert_count))
    packet = jnp.concatenate([normed_ffn.astype(BF16), jnp.pad(high, spare), jnp.pad(low, spare)], 1)
    x_parts = from_ctx(packet)
    grouped_rows = tie(grouped.reshape(depth, shards * width), packet)
    own_weights = lax.ppermute(
        lax.dynamic_slice_in_dim(
            grouped_rows, ctx * share_rows, share_rows, 0
        ),
        ("ctx", "shard"),
        [(j * shards + i, ctx_count * i + j) for j in range(ctx_count) for i in range(shards)],
    )
    x_parts, own_weights = meet(x_parts, own_weights)
    carry, grads_first = run_experts(
        x_parts, cot_parts, weights_first, ctx_index, experts, 0, [], False
    )
    gin_parts, mix_parts, grads_last = run_experts(
        x_parts, cot_parts, weights_last, ctx_index, experts, split, carry, True
    )
    back = to_ctx(gin_parts)
    share_first = lax.psum_scatter(grads_first, "shard", scatter_dimension=0, tiled=False)
    share_last = lax.psum_scatter(
        tie(grads_last, share_first, back), "shard", scatter_dimension=0, tiled=False
    )
    upstream = cotangent.astype(F32)
    grad_gates = jnp.where(
        kept,
        back[:, MODEL_WIDTH : MODEL_WIDTH + expert_count]
        + back[:, MODEL_WIDTH + LANES // 2 : MODEL_WIDTH + LANES // 2 + expert_count],
        0.0,
    )
    grad_logits = gate_weights * (
        grad_gates - jnp.sum(gate_weights * grad_gates, axis=1, keepdims=True)
    )
    grad_normed_ffn = back[:, :MODEL_WIDTH] + jnp.einsum(
        "te,de->td", grad_logits, router_wide, precision=PRECISE
    )
    grad_middle = upstream + norm_back(grad_normed_ffn, middle, inverse_ffn, gain_ffn)
    grad_branch = (RESIDUAL_SCALE * grad_middle).astype(BF16)
    grad_attended = dot(out_full, grad_branch, ((1,), (1,))).astype(BF16)
    grad_heads = all_to_all(grad_attended.reshape(shards, q_width, tile))

    grad_router = jnp.einsum("te,td->ed", grad_logits, normed_ffn, precision=PRECISE)
    grad_norm_ffn = jnp.sum(grad_normed_ffn * middle * inverse_ffn, axis=0)[None, :]
    fine = jnp.concatenate([grad_router, grad_norm_ffn], axis=0)
    fine_high = fine.astype(BF16)
    fine_low = (fine - fine_high.astype(F32)).astype(BF16)
    fine_rows = expert_count + 1
    fine = jnp.concatenate(
        [fine_high, fine_low, jnp.zeros((LANES - 2 * fine_rows, MODEL_WIDTH), BF16)], axis=0
    ).T
    block = MODEL_WIDTH // ctx_count
    early_parts = []
    for k in range(ctx_count):
        first = ((ctx - k) % ctx_count) * block
        part = lax.dynamic_slice_in_dim(attended, first, block, 0)
        early_parts.append(dot(part, grad_branch).astype(BF16))
    grad_heads, early_parts = meet(grad_heads, early_parts)
    early_parts = from_later(early_parts)

    out = attend_back(queries, grad_heads, outcome_wide, level, kv_parts, ctx_index)
    early_parts, gq, kv_out = meet(early_parts, out[0], out[1:])
    kv_back = from_later(kv_out)
    early = add_up(early_parts).astype(BF16).reshape(chips, 2, -1, MODEL_WIDTH)
    mine = lax.dynamic_index_in_dim(early, shard % 2, 1, keepdims=False)
    theirs = send_core(lax.dynamic_index_in_dim(early, 1 - shard % 2, 1, keepdims=False))
    out_back, _ = halve_chips((mine.astype(F32) + theirs.astype(F32)).astype(BF16))
    mix_back = from_later(tie(mix_parts, kv_back))
    at = jnp.stack([ctx, shard % 2]).astype(jnp.int32)
    own, other, late_parts = tail(
        gq, cosine, sine, normed, columns, fine, kv_back, at, tile
    )
    chip_sum = (own.astype(F32) + send_core(other).astype(F32)).astype(BF16)
    token_back, _ = halve_chips(chip_sum)
    late = to_ctx(tie(late_parts, chip_sum)).astype(BF16)
    late = all_to_all(late.reshape(shards, share_rows, -1))
    expert_grads = unpack(share_first, share_last, depth, down_depth, MODEL_WIDTH)
    block_out = (middle + RESIDUAL_SCALE * add_up(mix_back)).astype(BF16)
    late, token_back, out_back, block_out, expert_grads = meet(
        late, token_back, out_back, block_out, expert_grads
    )
    first_row = (ctx * shards + shard) * share_rows
    own_gain = lax.dynamic_slice_in_dim(gain_attn, first_row, share_rows, 0)[:, None]
    grad_tokens, grad_query, grad_key, grad_value, grad_out, grad_gain, grad_gain_ffn, grad_router = (
        finish(
            late, own_weights, own_gain, grad_middle, tokens, inverse_attn, gain_attn,
            token_back + out_back,
            q_width, copies, expert_count
        )
    )
    return (
        block_out,
        grad_tokens,
        grad_query,
        grad_key,
        grad_value,
        grad_out,
        grad_gain[0],
        grad_gain_ffn[0],
        grad_router.T,
        *expert_grads,
    )


def solution(mesh):
    placed = (
        P(("ctx", "shard"), None),
        P("shard", None),
        P("shard", None),
        P("shard", None),
        P("shard", None),
        P("shard"),
        P("shard"),
        P("shard", None),
        P("shard", "ctx", None),
        P("shard", "ctx", None),
        P("shard", "ctx", None),
        P(("ctx", "shard"), None),
        P(("ctx", "shard"), None),
        P(("ctx", "shard"), None),
    )
    return jax.shard_map(
        local,
        mesh=mesh,
        in_specs=placed,
        out_specs=(
            P(("ctx", "shard"), None),
            P(("ctx", "shard"), None),
            P(("ctx", "shard"), None),
            P(("ctx", "shard"), None),
            P(("ctx", "shard"), None),
            P(("ctx", "shard"), None),
            P(("ctx", "shard")),
            P(("ctx", "shard")),
            P(("ctx", "shard"), None),
            P("shard", "ctx", None),
            P("shard", "ctx", None),
            P("shard", "ctx", None),
        ),
        check_vma=False,
    )
```

```python
import functools
import math

import jax
import jax.numpy as jnp
from jax import lax
from jax.experimental import pallas as pl
from jax.experimental.pallas import tpu as pltpu
from jax.sharding import PartitionSpec as P

MODEL_WIDTH = 1024
QUERY_HEADS = 16
KEY_VALUE_HEADS = 8
HEAD_SIZE = 64
FF = 512
TOPK = 8

NORM_EPS = 1e-06
RESIDUAL_SCALE = 0.22
SCORE_SCALE = 0.015625
ROPE_BASE = 10000.0
PRECISE = lax.Precision.HIGHEST
MASKED = -1e30
UNCHOSEN = 1 << 20
LANES = 128

F32 = jnp.float32
BF16 = jnp.bfloat16


def whole(shape):
    return pl.BlockSpec(tuple(shape), lambda i: (0,) * len(shape))


def dot(a, b, dims=((1,), (0,))):
    return lax.dot_general(a, b, (dims, ((), ())), preferred_element_type=F32)


def rotary_tables(positions):
    halfway = HEAD_SIZE // 2
    frequency = jnp.exp(
        jnp.arange(halfway, dtype=F32) * (-2.0 * math.log(ROPE_BASE) / HEAD_SIZE)
    )
    angles = frequency[:, None] * positions.astype(F32)[None, :]
    return (jnp.cos(angles), jnp.sin(angles))


def rotate(vectors, cosine, sine):
    rows, count = vectors.shape
    shaped = vectors.reshape(rows // HEAD_SIZE, 2, HEAD_SIZE // 2, count)
    front, behind = shaped[:, 0], shaped[:, 1]
    turned = jnp.stack(
        [front * cosine - behind * sine, behind * cosine + front * sine], axis=1
    )
    return turned.reshape(rows, count)


def rms_scale(value_rows):
    return lax.rsqrt(jnp.mean(value_rows * value_rows, axis=1, keepdims=True) + NORM_EPS)


def norm_back(upward, inputs, inverse_rms, gain_vector):
    weighted = upward * gain_vector.reshape(1, -1)
    cubed = inverse_rms * inverse_rms * inverse_rms
    return inverse_rms * weighted - inputs * cubed * jnp.mean(
        weighted * inputs, axis=1, keepdims=True
    )


def project_kernel(
    at_ref, columns_ref, cos_ref, sin_ref, *refs, count, tile, depth
):
    parts = refs[: 2 * count]
    normed_ref, q_ref, kv_ref, small_ref, block, gain = refs[2 * count :]
    shards = 2 * count
    width = normed_ref.shape[1]
    lane = lax.broadcasted_iota(jnp.int32, (1, width), 1) // depth
    gain[...] = jnp.zeros_like(gain)
    for k in range(count):
        for side in range(2):
            slot = at_ref[1] if side == 0 else 1 - at_ref[1]
            index = 2 * lax.rem(at_ref[0] - k + count, count) + slot
            part = parts[side * count + k]
            block[pl.ds(pl.multiple_of(index * tile, tile), tile), :] = part[:tile, :]
            small_ref[index] = part[tile:, :]
            row = part[tile : tile + 1, :].astype(F32)
            gain[...] += jnp.where(lane == index, row, 0.0)
    for s in range(shards):
        at = slice(s * tile, (s + 1) * tile)
        x = block[at, :].astype(F32)
        normed_ref[at, :] = (x * rms_scale(x) * gain[...]).astype(BF16)
    lin = dot(columns_ref[...].T, normed_ref[...], ((1,), (1,)))
    q_width = q_ref.shape[0]
    half = HEAD_SIZE // 2
    cosine, sine = cos_ref[...], sin_ref[...]

    def turn(first):
        front, behind = lin[first : first + half], lin[first + half : first + 2 * half]
        return front * cosine - behind * sine, behind * cosine + front * sine

    for h in range(q_width // HEAD_SIZE):
        front, behind = turn(h * HEAD_SIZE)
        at = h * HEAD_SIZE
        q_ref[at : at + half, :] = front.astype(BF16) * jnp.asarray(SCORE_SCALE, BF16)
        q_ref[at + half : at + 2 * half, :] = behind.astype(BF16) * jnp.asarray(SCORE_SCALE, BF16)
    front, behind = turn(q_width)
    kv_ref[:half, :] = front.astype(BF16)
    kv_ref[half:HEAD_SIZE, :] = behind.astype(BF16)
    kv_ref[HEAD_SIZE:, :] = lin[q_width + HEAD_SIZE :].astype(BF16)


def project(parts, others, columns, cosine, sine, at, tile, depth):
    count = len(parts)
    height, width = parts[0].shape
    rows = 2 * count * tile
    lin_width = columns.shape[1]
    shapes = [
        (rows, width),
        (lin_width - 2 * HEAD_SIZE, rows),
        (2 * HEAD_SIZE, rows),
        (2 * count, height - tile, width),
    ]
    args = [at, columns, cosine, sine, *parts, *others]
    return pl.pallas_call(
        functools.partial(project_kernel, count=count, tile=tile, depth=depth),
        grid=(1,),
        in_specs=[pl.BlockSpec(memory_space=pltpu.SMEM)] + [whole(v.shape) for v in args[1:]],
        out_specs=[whole(shape) for shape in shapes],
        out_shape=[jax.ShapeDtypeStruct(shape, BF16) for shape in shapes],
        scratch_shapes=[pltpu.VMEM((rows, width), BF16), pltpu.VMEM((1, width), F32)],
        compiler_params=pltpu.CompilerParams(vmem_limit_bytes=60 << 20),
        cost_estimate=pl.CostEstimate(
            flops=2 * rows * width * lin_width,
            transcendentals=0,
            bytes_accessed=4 * rows * width,
        ),
        name="project",
    )(*args)


def attention_blocks(rows):
    return min(512, rows)


def attend_kernel(c_ref, q_ref, *refs, ctx_count, heads, rows, block, tile):
    kv_refs = refs[:ctx_count]
    out_ref, wide_ref, log_ref = refs[ctx_count : ctx_count + 3]
    natural, peak, total, acc = refs[ctx_count + 3 :]
    step = pl.program_id(0)
    mine = c_ref[0]

    @pl.when(step == 0)
    def _():
        for k in range(ctx_count):

            @pl.when(mine >= k)
            def _(k=k):
                natural[k] = kv_refs[k][...].T

    zeros = jnp.zeros((HEAD_SIZE, block), BF16)
    wide_q = [
        jnp.concatenate([q_ref[h * HEAD_SIZE : (h + 1) * HEAD_SIZE, :], zeros], axis=0)
        for h in range(heads)
    ]
    for h in range(heads):
        peak[h] = jnp.full((1, block), MASKED, F32)
        total[h] = jnp.zeros((1, block), F32)
        acc[h] = jnp.zeros((HEAD_SIZE, block), F32)

    def visit(k, start, masked):
        keys = natural[k, pl.ds(start, block), :]
        values = kv_refs[k][HEAD_SIZE:, pl.ds(start, block)]
        for h in range(heads):
            scores = dot(keys, wide_q[h])
            if masked:
                place = lax.broadcasted_iota(jnp.int32, (block, block), 0)
                query = lax.broadcasted_iota(jnp.int32, (block, block), 1)
                scores = jnp.where(place <= query, scores, MASKED)
            old = peak[h]
            new = jnp.maximum(old, jnp.max(scores, axis=0, keepdims=True))
            shrink = jnp.exp(old - new)
            weights = jnp.exp(scores - new)
            peak[h] = new
            total[h] = total[h] * shrink + jnp.sum(weights, axis=0, keepdims=True)
            acc[h] = acc[h] * shrink + dot(values, weights.astype(BF16))

    def full(k):
        def body(j, carry):
            visit(k, pl.multiple_of(j * block, block), False)
            return carry

        return body

    for k in range(1, ctx_count):

        @pl.when(mine >= k)
        def _(k=k):
            lax.fori_loop(0, rows // block, full(k), 0, unroll=2)

    lax.fori_loop(0, step, full(0), 0)
    visit(0, pl.multiple_of(step * block, block), True)
    for h in range(heads):
        result = acc[h] / total[h]
        at = slice(h * HEAD_SIZE, (h + 1) * HEAD_SIZE)
        wide_ref[at, :] = result
        log_ref[h : h + 1, :] = peak[h] + jnp.log(total[h])
        for j in range(block // tile):
            out_ref[j, at, :] = result[:, j * tile : (j + 1) * tile].astype(BF16)


def attend(queries, key_values, ctx_index, tile):
    width, rows = queries.shape
    heads = width // HEAD_SIZE
    ctx_count = len(key_values)
    block = attention_blocks(rows)
    kv_width = key_values[0].shape[0]
    whole = pl.BlockSpec((kv_width, rows), lambda i, c: (0, 0))
    return pl.pallas_call(
        functools.partial(
            attend_kernel, ctx_count=ctx_count, heads=heads, rows=rows, block=block, tile=tile
        ),
        grid_spec=pltpu.PrefetchScalarGridSpec(
            num_scalar_prefetch=1,
            grid=(rows // block,),
            in_specs=[pl.BlockSpec((width, block), lambda i, c: (0, i))] + [whole] * ctx_count,
            out_specs=[
                pl.BlockSpec((block // tile, width, tile), lambda i, c: (i, 0, 0)),
                pl.BlockSpec((width, block), lambda i, c: (0, i)),
                pl.BlockSpec((heads, block), lambda i, c: (0, i)),
            ],
            scratch_shapes=[
                pltpu.VMEM((ctx_count, rows, kv_width), BF16),
                pltpu.VMEM((heads, 1, block), F32),
                pltpu.VMEM((heads, 1, block), F32),
                pltpu.VMEM((heads, HEAD_SIZE, block), F32),
            ],
        ),
        out_shape=[
            jax.ShapeDtypeStruct((rows // tile, width, tile), BF16),
            jax.ShapeDtypeStruct((width, rows), F32),
            jax.ShapeDtypeStruct((heads, rows), F32),
        ],
        compiler_params=pltpu.CompilerParams(
            dimension_semantics=("arbitrary",), vmem_limit_bytes=60 << 20
        ),
        cost_estimate=pl.CostEstimate(
            flops=64 * width * rows * rows * ctx_count // 2,
            transcendentals=heads * rows * rows * ctx_count // 2,
            bytes_accessed=2 * ctx_count * rows * kv_width,
        ),
        name="attend",
    )(ctx_index, queries, *key_values)


def attend_back_kernel(
    c_ref, q_ref, grad_ref, wide_ref, log_ref, *refs, ctx_count, heads, rows, block, tile
):
    kv_refs = refs[:ctx_count]
    gq_ref = refs[ctx_count]
    gkv_refs = refs[ctx_count + 1 : 2 * ctx_count + 1]
    natural, sums, gq_acc = refs[2 * ctx_count + 1 :]
    step = pl.program_id(0)
    last = pl.num_programs(0) - 1
    mine = c_ref[0]

    @pl.when(step == 0)
    def _():
        for k in range(ctx_count):

            @pl.when(mine >= k)
            def _(k=k):
                natural[k] = kv_refs[k][...].T
                sums[k] = jnp.zeros_like(sums[k])

    zeros = jnp.zeros((HEAD_SIZE, block), BF16)
    wide_q, wide_g, tall_q, tall_g, delta, level = [], [], [], [], [], []
    for h in range(heads):
        at = slice(h * HEAD_SIZE, (h + 1) * HEAD_SIZE)
        grad = jnp.concatenate([grad_ref[j, at, :] for j in range(block // tile)], axis=1)
        q_part = jnp.concatenate([q_ref[at, :], zeros], axis=0)
        g_part = jnp.concatenate([zeros, grad], axis=0)
        wide_q.append(q_part)
        wide_g.append(g_part)
        tall_q.append(q_part.T)
        tall_g.append(g_part.T)
        delta.append(jnp.sum(grad.astype(F32) * wide_ref[at, :], axis=0, keepdims=True))
        level.append(log_ref[h : h + 1, :])
        gq_acc[h] = jnp.zeros((HEAD_SIZE, block), F32)

    def visit(k, start, masked):
        both = natural[k, pl.ds(start, block), :]
        keys = kv_refs[k][:HEAD_SIZE, pl.ds(start, block)]
        add = None
        for h in range(heads):
            scores = dot(both, wide_q[h])
            if masked:
                place = lax.broadcasted_iota(jnp.int32, (block, block), 0)
                query = lax.broadcasted_iota(jnp.int32, (block, block), 1)
                scores = jnp.where(place <= query, scores, MASKED)
            weights = jnp.exp(scores - level[h])
            grad_probs = dot(both, wide_g[h])
            grad_scores = (weights * (grad_probs - delta[h])).astype(BF16)
            part = dot(grad_scores, tall_q[h]) + dot(weights.astype(BF16), tall_g[h])
            add = part if add is None else add + part
            gq_acc[h] += dot(keys, grad_scores)
        sums[k, pl.ds(start, block), :] += add

    def full(k):
        def body(j, carry):
            visit(k, pl.multiple_of(j * block, block), False)
            return carry

        return body

    for k in range(1, ctx_count):

        @pl.when(mine >= k)
        def _(k=k):
            lax.fori_loop(0, rows // block, full(k), 0, unroll=2)

    lax.fori_loop(0, step, full(0), 0)
    visit(0, pl.multiple_of(step * block, block), True)
    for h in range(heads):
        gq_ref[h * HEAD_SIZE : (h + 1) * HEAD_SIZE, :] = SCORE_SCALE * gq_acc[h]

    @pl.when(step == last)
    def _():
        gkv_refs[0][...] = sums[0]
        for k in range(1, ctx_count):

            @pl.when(mine >= k)
            def _(k=k):
                gkv_refs[k][...] = sums[k].astype(BF16)

            @pl.when(mine < k)
            def _(k=k):
                gkv_refs[k][...] = jnp.zeros((rows, sums.shape[2]), BF16)


def attend_back(queries, grads, wide, level, key_values, ctx_index):
    width, rows = queries.shape
    heads = width // HEAD_SIZE
    ctx_count = len(key_values)
    block = attention_blocks(rows)
    tile = grads.shape[2]
    kv_width = key_values[0].shape[0]
    whole = pl.BlockSpec((kv_width, rows), lambda i, c: (0, 0))
    tall = pl.BlockSpec((rows, kv_width), lambda i, c: (0, 0))
    return pl.pallas_call(
        functools.partial(
            attend_back_kernel, ctx_count=ctx_count, heads=heads, rows=rows, block=block, tile=tile
        ),
        grid_spec=pltpu.PrefetchScalarGridSpec(
            num_scalar_prefetch=1,
            grid=(rows // block,),
            in_specs=[
                pl.BlockSpec((width, block), lambda i, c: (0, i)),
                pl.BlockSpec((block // tile, width, tile), lambda i, c: (i, 0, 0)),
                pl.BlockSpec((width, block), lambda i, c: (0, i)),
                pl.BlockSpec((heads, block), lambda i, c: (0, i)),
            ]
            + [whole] * ctx_count,
            out_specs=[pl.BlockSpec((width, block), lambda i, c: (0, i))] + [tall] * ctx_count,
            scratch_shapes=[
                pltpu.VMEM((ctx_count, rows, kv_width), BF16),
                pltpu.VMEM((ctx_count, rows, kv_width), F32),
                pltpu.VMEM((heads, HEAD_SIZE, block), F32),
            ],
        ),
        out_shape=[jax.ShapeDtypeStruct((width, rows), F32)]
        + [
            jax.ShapeDtypeStruct((rows, kv_width), F32 if k == 0 else BF16)
            for k in range(ctx_count)
        ],
        compiler_params=pltpu.CompilerParams(
            dimension_semantics=("arbitrary",), vmem_limit_bytes=60 << 20
        ),
        cost_estimate=pl.CostEstimate(
            flops=96 * width * rows * rows * ctx_count // 2,
            transcendentals=heads * rows * rows * ctx_count // 2,
            bytes_accessed=4 * ctx_count * rows * kv_width,
        ),
        name="attend_back",
    )(ctx_index, queries, grads, wide, level, *key_values)


def tail_kernel(
    at_ref, gq_ref, cos_ref, sin_ref, normed_ref, columns_ref, fine_ref, *refs, ctx_count, tile
):
    kv_refs = refs[:ctx_count]
    own_ref, other_ref = refs[ctx_count : ctx_count + 2]
    late_refs = refs[ctx_count + 2 : 2 * ctx_count + 2]
    tall, late = refs[2 * ctx_count + 2 :]
    ctx, core = at_ref[0], at_ref[1]
    q_width = gq_ref.shape[0]
    lin_width = tall.shape[1]
    half = HEAD_SIZE // 2
    cosine, sine = cos_ref[...], sin_ref[...]

    def turn_back(vectors):
        front, behind = vectors[:half], vectors[half:]
        return [front * cosine + behind * sine, behind * cosine - front * sine]

    grad_kv = add_up([ref[...] for ref in kv_refs]).T
    pieces = []
    for h in range(q_width // HEAD_SIZE):
        pieces += turn_back(gq_ref[h * HEAD_SIZE : (h + 1) * HEAD_SIZE, :])
    pieces += turn_back(grad_kv[:HEAD_SIZE]) + [grad_kv[HEAD_SIZE:]]
    grad_lin = jnp.concatenate(pieces, axis=0).astype(BF16)
    tall[...] = grad_lin.T
    late[...] = dot(grad_lin, normed_ref[...]).astype(BF16).T
    block = late.shape[0] // ctx_count
    for k in range(ctx_count):
        first = pl.multiple_of(lax.rem(ctx - k + ctx_count, ctx_count) * block, block)
        late_refs[k][:, :lin_width] = late[pl.ds(first, block), :]
        late_refs[k][:, lin_width:] = fine_ref[pl.ds(first, block), :]
    chips = own_ref.shape[0]
    for chip in range(chips):
        for side, ref in ((core, own_ref), (1 - core, other_ref)):
            first = pl.multiple_of((2 * chip + side) * tile, tile)
            ref[chip] = dot(
                tall[pl.ds(first, tile), :], columns_ref[...], ((1,), (1,))
            ).astype(BF16)


def tail(gq, cosine, sine, normed, columns, fine, kv_back, at, tile):
    ctx_count = len(kv_back)
    rows, width = normed.shape
    lin_width = columns.shape[1]
    chips = rows // (2 * tile)
    block = width // ctx_count
    args = [at, gq, cosine, sine, normed, columns, fine, *kv_back]
    shapes = [((chips, tile, width), BF16)] * 2 + [
        ((block, lin_width + LANES), BF16)
    ] * ctx_count
    out = pl.pallas_call(
        functools.partial(tail_kernel, ctx_count=ctx_count, tile=tile),
        grid=(1,),
        in_specs=[pl.BlockSpec(memory_space=pltpu.SMEM)] + [whole(v.shape) for v in args[1:]],
        out_specs=[whole(shape) for shape, _ in shapes],
        out_shape=[jax.ShapeDtypeStruct(*shape) for shape in shapes],
        scratch_shapes=[pltpu.VMEM((rows, lin_width), BF16), pltpu.VMEM((width, lin_width), BF16)],
        compiler_params=pltpu.CompilerParams(vmem_limit_bytes=60 << 20),
        cost_estimate=pl.CostEstimate(
            flops=4 * rows * width * lin_width, transcendentals=0, bytes_accessed=12 * rows * width
        ),
        name="tail",
    )(*args)
    return out[0], out[1], out[2:]


def finish_kernel(
    late_ref, weight_ref, gain_ref, middle_ref, token_ref, inverse_ref, norm_ref, *refs,
    q_width, copies, experts, tile
):
    parts = refs[:-8]
    tokens_ref, q_ref, k_ref, v_ref, out_ref, attn_ref, ffn_ref, router_ref = refs[-8:]
    parts, out_parts = parts[: len(parts) // 2], parts[len(parts) // 2 :]
    grad_normed = add_up([ref[...] for ref in parts])
    inputs = token_ref[...].astype(F32)
    tokens_ref[...] = middle_ref[...] + norm_back(
        grad_normed, inputs, inverse_ref[...], norm_ref[...]
    )
    out_ref[...] = add_up([ref[...] for ref in out_parts])
    shards, rows, _ = late_ref.shape
    width = q_width + 2 * HEAD_SIZE
    gain_grad = jnp.zeros((rows, 1), F32)
    values = [late_ref[s, :, :width].astype(F32) for s in range(shards)]
    for s in range(shards):
        weights = weight_ref[:, s * width : (s + 1) * width].astype(F32)
        gain_grad += jnp.sum(values[s] * weights, axis=1, keepdims=True)
    q_ref[...] = jnp.concatenate([v[:, :q_width] for v in values], axis=1)
    for ref, first in ((k_ref, q_width), (v_ref, q_width + HEAD_SIZE)):
        heads = [v[:, first : first + HEAD_SIZE] for v in values]
        ref[...] = jnp.concatenate(
            [add_up(heads[i : i + copies]) for i in range(0, shards, copies)], axis=1
        )
    fine = add_up([late_ref[s, :, width:] for s in range(shards)])
    count = experts + 1
    router_ref[...] = (fine[:, :experts] + fine[:, count : count + experts]).T
    ffn_ref[...] = (fine[:, experts:count] + fine[:, count + experts : 2 * count]).T
    attn_ref[...] = (gain_grad / gain_ref[...]).T


def finish(
    late, own_weights, own_gain, grad_middle, tokens, inverse, gain, token_back,
    q_width, copies, experts
):
    shards, rows, _ = late.shape
    tile, model = grad_middle.shape
    args = [late, own_weights, own_gain, grad_middle, tokens, inverse, gain[None, :], *token_back]
    kv_width = shards // copies * HEAD_SIZE
    shapes = [(tile, model), (rows, shards * q_width), (rows, kv_width), (rows, kv_width)]
    shapes += [(rows, model), (1, rows), (1, rows), (experts, rows)]
    return pl.pallas_call(
        functools.partial(
            finish_kernel, q_width=q_width, copies=copies, experts=experts, tile=tile
        ),
        grid=(1,),
        in_specs=[whole(v.shape) for v in args],
        out_specs=[whole(shape) for shape in shapes],
        out_shape=[jax.ShapeDtypeStruct(shape, F32) for shape in shapes],
        compiler_params=pltpu.CompilerParams(vmem_limit_bytes=60 << 20),
        cost_estimate=pl.CostEstimate(
            flops=0, transcendentals=0, bytes_accessed=16 * tile * model
        ),
        name="finish",
    )(*args)


def unpack_kernel(first_ref, last_ref, gate_ref, up_ref, down_ref):
    rows, down_rows = gate_ref.shape[0], down_ref.shape[0]
    split = first_ref.shape[0]
    for e in range(split + last_ref.shape[0]):
        source, i = (first_ref, e) if e < split else (last_ref, e - split)
        gate_ref[:, e, :] = source[i, :rows, :].astype(F32)
        up_ref[:, e, :] = source[i, rows : 2 * rows, :].astype(F32)
        for half in range(down_ref.shape[2] // FF):
            at = 2 * rows + half * down_rows
            down_ref[:, e, half * FF : (half + 1) * FF] = source[
                i, at : at + down_rows, :
            ].astype(F32)


def unpack(first, last, rows, down_rows, model):
    experts = first.shape[0] + last.shape[0]
    shapes = [(rows, experts, FF), (rows, experts, FF), (down_rows, experts, model)]
    return pl.pallas_call(
        unpack_kernel,
        grid=(1,),
        in_specs=[whole(first.shape), whole(last.shape)],
        out_specs=[whole(shape) for shape in shapes],
        out_shape=[jax.ShapeDtypeStruct(shape, F32) for shape in shapes],
        compiler_params=pltpu.CompilerParams(vmem_limit_bytes=60 << 20),
        cost_estimate=pl.CostEstimate(
            flops=0, transcendentals=0, bytes_accessed=6 * (first.size + last.size)
        ),
        name="unpack",
    )(first, last)


def expert_kernel(
    c_ref, *refs, ctx_count, experts, first, carried, final, tile, rows, down_rows
):
    refs = list(refs)

    def take(count):
        taken = refs[:count]
        del refs[:count]
        return taken

    x_refs, u_refs, (w_ref,) = take(ctx_count), take(ctx_count), take(1)
    carry_refs = take(3 if carried else 0)
    if final:
        gin_refs, mix_refs = take(ctx_count), take(ctx_count)
    else:
        sums = take(3)
    (grad_ref,) = take(1)
    if final:
        sums = take(3)
    gin_acc, mix_acc, dots = sums
    x_all, x_turned, u_all, share, hid, g_out, g_gate, g_up = refs
    shards = w_ref.shape[0]
    e = pl.program_id(0)
    last = pl.num_programs(0) - 1
    width = u_all.shape[1]
    count = ctx_count * tile
    chunk = min(4 * tile, count)
    column = c_ref[0] * experts + first + e

    @pl.when(e == 0)
    def _():
        for k in range(ctx_count):
            at = slice(k * tile, (k + 1) * tile)
            part = x_refs[k][:, :width]
            x_all[at, :] = part
            x_turned[:, at] = part.T
            u_all[at, :] = u_refs[k][...]
            share[at, :] = x_refs[k][:, width:].astype(F32)
        for i, ref in enumerate(sums):
            ref[...] = carry_refs[i][...] if carried else jnp.zeros_like(ref)

    lane = lax.broadcasted_iota(jnp.int32, (chunk, LANES), 1)
    picked = (lane == column) | (lane == column + LANES // 2)
    down = 2 * rows

    def gate_matrix():
        return w_ref[:, 0, 0:rows, :].reshape(shards * rows, FF)

    def up_matrix():
        return w_ref[:, 0, rows : 2 * rows, :].reshape(shards * rows, FF)

    def down_matrix(half):
        at = down + half * down_rows
        return w_ref[:, 0, at : at + down_rows, :].reshape(FF, FF)

    def one_chunk(j, carry):
        at = pl.ds(pl.multiple_of(j * chunk, chunk), chunk)
        x = x_all[at, :]
        gate = dot(x, gate_matrix())
        up = dot(x, up_matrix())
        sig = jax.nn.sigmoid(gate)
        silu = gate * sig
        hidden = (silu * up).astype(BF16)
        hid[at, :] = hidden
        weight = jnp.sum(jnp.where(picked, share[at, :], 0.0), axis=1, keepdims=True)
        upstream = u_all[at, :].astype(F32) * RESIDUAL_SCALE
        down_grad = (upstream * weight).astype(BF16)
        g_out[at, :] = down_grad
        gathered = jnp.zeros((chunk, 1), F32)
        grad_hidden = jnp.zeros((chunk, FF), F32)
        for half in range(width // FF):
            cols = slice(half * FF, (half + 1) * FF)
            matrix = down_matrix(half)
            made = dot(hidden, matrix).astype(BF16).astype(F32)
            mix_acc[at, cols] += weight * made
            gathered += jnp.sum(upstream[:, cols] * made, axis=1, keepdims=True)
            grad_hidden += dot(down_grad[:, cols], matrix, ((1,), (1,)))
        dots[at, :] += jnp.where(picked, gathered, 0.0)
        grad_gate = (grad_hidden * up * sig * (1.0 + gate * (1.0 - sig))).astype(BF16)
        grad_up = (grad_hidden * silu).astype(BF16)
        g_gate[at, :] = grad_gate
        g_up[at, :] = grad_up
        gin_acc[at, :] += dot(grad_gate, gate_matrix(), ((1,), (1,))) + dot(
            grad_up, up_matrix(), ((1,), (1,))
        )
        return carry

    lax.fori_loop(0, count // chunk, one_chunk, 0, unroll=True)
    grad_ref[:, 0, 0:rows, :] = (
        dot(x_turned[...], g_gate[...]).astype(BF16).reshape(shards, rows, FF)
    )
    grad_ref[:, 0, rows : 2 * rows, :] = (
        dot(x_turned[...], g_up[...]).astype(BF16).reshape(shards, rows, FF)
    )
    hid_turned = hid[...].T
    for half in range(width // FF):
        at = down + half * down_rows
        grad_ref[:, 0, at : at + down_rows, :] = (
            dot(hid_turned, g_out[:, half * FF : (half + 1) * FF])
            .astype(BF16)
            .reshape(shards, down_rows, FF)
        )

    if not final:
        return

    @pl.when(e == last)
    def _():
        for k in range(ctx_count):
            at = slice(k * tile, (k + 1) * tile)
            gin_refs[k][:, :width] = gin_acc[at, :].astype(BF16)
            high = dots[at, :].astype(BF16)
            gin_refs[k][:, width : width + LANES // 2] = high[:, : LANES // 2]
            low = (dots[at, :] - high.astype(F32)).astype(BF16)
            gin_refs[k][:, width + LANES // 2 :] = low[:, LANES // 2 :]
            mix_refs[k][...] = mix_acc[at, :].astype(BF16)


def run_experts(x_parts, u_parts, weights, ctx_index, experts, first, carry, final):
    ctx_count = len(x_parts)
    tile, width = u_parts[0].shape
    shards, group, all_rows, _ = weights.shape
    rows = width // shards
    down_rows = FF // shards
    count = ctx_count * tile

    def flat(*shape, **options):
        return pl.BlockSpec(shape, lambda e, c: (0,) * len(shape), **options)

    expert_block = (shards, 1, all_rows, FF)
    by_expert = pl.BlockSpec(expert_block, lambda e, c: (0, e, 0, 0))
    made = pl.BlockSpec(expert_block, lambda e, c: (0, e, 0, 0))
    sum_shapes = [(count, width), (count, width), (count, LANES)]
    if final:
        out_specs = [flat(tile, width + LANES)] * ctx_count + [flat(tile, width)] * ctx_count
        out_shape = [jax.ShapeDtypeStruct((tile, width + LANES), BF16)] * ctx_count + [
            jax.ShapeDtypeStruct((tile, width), BF16)
        ] * ctx_count
        sum_scratch = [pltpu.VMEM(shape, F32) for shape in sum_shapes]
    else:
        out_specs = [flat(*shape) for shape in sum_shapes]
        out_shape = [jax.ShapeDtypeStruct(shape, F32) for shape in sum_shapes]
        sum_scratch = []
    once = pl.Buffered(1)
    out = pl.pallas_call(
        functools.partial(
            expert_kernel,
            ctx_count=ctx_count,
            experts=experts,
            first=first,
            carried=bool(carry),
            final=final,
            tile=tile,
            rows=rows,
            down_rows=down_rows,
        ),
        grid_spec=pltpu.PrefetchScalarGridSpec(
            num_scalar_prefetch=1,
            grid=(group,),
            in_specs=[flat(tile, width + LANES)] * ctx_count
            + [flat(tile, width)] * ctx_count
            + [by_expert]
            + [flat(*shape, pipeline_mode=once) for shape in sum_shapes[: len(carry)]],
            out_specs=out_specs + [made],
            scratch_shapes=sum_scratch
            + [
                pltpu.VMEM((count, width), BF16),
                pltpu.VMEM((width, count), BF16),
                pltpu.VMEM((count, width), BF16),
                pltpu.VMEM((count, LANES), F32),
                pltpu.VMEM((count, FF), BF16),
                pltpu.VMEM((count, width), BF16),
                pltpu.VMEM((count, FF), BF16),
                pltpu.VMEM((count, FF), BF16),
            ],
        ),
        out_shape=out_shape + [jax.ShapeDtypeStruct((shards, group, all_rows, FF), BF16)],
        compiler_params=pltpu.CompilerParams(
            dimension_semantics=("arbitrary",), vmem_limit_bytes=60 << 20
        ),
        cost_estimate=pl.CostEstimate(
            flops=24 * group * count * width * FF,
            transcendentals=group * count * FF,
            bytes_accessed=4 * shards * group * all_rows * FF,
        ),
        name="experts",
    )(ctx_index, *x_parts, *u_parts, weights, *carry)
    if final:
        return out[:ctx_count], out[ctx_count : 2 * ctx_count], out[2 * ctx_count]
    return out[:3], out[3]


def send_ctx(value, by):
    count = lax.axis_size("ctx")
    return lax.ppermute(value, "ctx", [(i, (i + by) % count) for i in range(count)])


def from_ctx(value):
    return [value] + [send_ctx(value, k) for k in range(1, lax.axis_size("ctx"))]


def from_later(parts):
    return [parts[0]] + [send_ctx(parts[k], -k) for k in range(1, len(parts))]


def add_up(parts):
    total = parts[0].astype(F32)
    for part in parts[1:]:
        total = total + part.astype(F32)
    return total


def to_ctx(parts):
    return add_up(from_later(parts))


def all_to_all(value):
    return lax.all_to_all(value, "shard", split_axis=0, concat_axis=0, tiled=True)


def send_chip(value, by):
    chips = lax.axis_size("shard") // 2
    return lax.ppermute(
        value,
        "shard",
        [(2 * i + j, 2 * ((i + by) % chips) + j) for i in range(chips) for j in range(2)],
    )


def send_core(value):
    return lax.ppermute(value, "shard", [(i, i ^ 1) for i in range(lax.axis_size("shard"))])


def tie(value, *others):
    return lax.optimization_barrier((value, others))[0]


def relay_chips(value):
    chips = lax.axis_size("shard") // 2
    chip = lax.axis_index("shard") // 2

    def step(block, by, done):
        pairs = [
            (2 * i + j, 2 * (i + by) + j)
            for i in range(chips)
            if 0 <= i + by < chips and 0 <= i - by * done < chips
            for j in range(2)
        ]
        return lax.ppermute(block, "shard", pairs)

    up, down = [value], [value]
    for k in range(1, chips):
        up.append(step(up[-1], 1, k - 1))
        down.append(step(down[-1], -1, k - 1))
    return [value] + [jnp.where(chip >= k, up[k], down[chips - k]) for k in range(1, chips)]


def meet(*values):
    return lax.optimization_barrier(values)


def arrive(own, send, count):
    return [own] + [send(own, k) for k in range(1, count)]


def assemble_kernel(at_ref, *refs, count, lead):
    parts, out_ref = refs[:-1], refs[-1]
    for k in range(count):
        index = lax.rem(at_ref[0] - k + count, count)
        for side in range(2):
            slot = at_ref[1] if side == 0 else 1 - at_ref[1]
            out_ref[(slice(None),) * lead + (index, slot)] = parts[side * count + k][...]


def assemble(parts, others, first, lead):
    count = len(parts)
    shape, dtype = parts[0].shape, parts[0].dtype
    at = jnp.stack([first, lax.axis_index("shard") % 2]).astype(jnp.int32)
    out_shape = shape[:lead] + (count, 2) + shape[lead:]
    return pl.pallas_call(
        functools.partial(assemble_kernel, count=count, lead=lead),
        grid=(1,),
        in_specs=[pl.BlockSpec(memory_space=pltpu.SMEM)] + [whole(shape)] * (2 * count),
        out_specs=whole(out_shape),
        out_shape=jax.ShapeDtypeStruct(out_shape, dtype),
        compiler_params=pltpu.CompilerParams(vmem_limit_bytes=60 << 20),
        cost_estimate=pl.CostEstimate(
            flops=0, transcendentals=0, bytes_accessed=8 * count * parts[0].size
        ),
        name="assemble",
    )(at, *parts, *others)


def spread_start(value):
    shards, ctx_count = lax.axis_size("shard"), lax.axis_size("ctx")
    shard, ctx = lax.axis_index("shard"), lax.axis_index("ctx")
    core, chips = shard % 2, shards // 2
    rows, columns = value.shape
    pieces = lax.dynamic_index_in_dim(
        value.reshape(ctx_count, 2, rows // (2 * ctx_count), columns), ctx, 0, keepdims=False
    )
    mine = lax.dynamic_index_in_dim(pieces, core, 0, keepdims=False)
    theirs = send_core(lax.dynamic_index_in_dim(pieces, 1 - core, 0, keepdims=False))
    pair = jnp.stack([jnp.where(core == 0, mine, theirs), jnp.where(core == 0, theirs, mine)])
    return arrive(pair, send_chip, chips)


def spread_join(parts):
    chips = len(parts)
    chip = lax.axis_index("shard") // 2
    joined = jnp.zeros((chips,) + parts[0].shape, parts[0].dtype)
    for k, part in enumerate(parts):
        joined = lax.dynamic_update_index_in_dim(joined, part, (chip - k) % chips, 0)
    return joined


def spread_ctx(joined):
    return arrive(joined, send_ctx, lax.axis_size("ctx"))


def spread_end(parts, others):
    return assemble(parts, others, lax.axis_index("ctx"), 2).reshape(MODEL_WIDTH, -1)


def halve_chips(blocks):
    shards = lax.axis_size("shard")
    chip = lax.axis_index("shard") // 2
    distance, first = 1, None
    while True:
        pairs = blocks.reshape((blocks.shape[0] // 2, 2) + blocks.shape[1:])
        side = (chip // distance) % 2
        keep = lax.dynamic_index_in_dim(pairs, side, 1, keepdims=False)
        sent = lax.dynamic_index_in_dim(pairs, 1 - side, 1, keepdims=False)
        came = lax.ppermute(sent, "shard", [(i, i ^ (2 * distance)) for i in range(shards)])
        first = came if first is None else first
        if keep.shape[0] == 1:
            return [keep[0], came[0]], first
        blocks = (keep.astype(F32) + came.astype(F32)).astype(BF16)
        distance *= 2


def local(
    tokens,
    w_query,
    key_weight,
    value_weight,
    w_out,
    norm_attn,
    norm_ffn,
    w_router,
    w_gate,
    w_up,
    w_down,
    cotangent,
    choices,
    priority,
):
    shards = lax.axis_size("shard")
    ctx_count = lax.axis_size("ctx")
    ctx = lax.axis_index("ctx")
    shard = lax.axis_index("shard")
    ctx_index = ctx.astype(jnp.int32).reshape(1)
    tile = tokens.shape[0]
    rows = tile * shards
    expert_count = w_router.shape[1]
    experts = w_gate.shape[1]
    depth = w_query.shape[0]
    down_depth = w_down.shape[0]
    capacity = tile * TOPK * 5 // (4 * expert_count)
    heads = QUERY_HEADS // shards
    copies = max(1, shards // KEY_VALUE_HEADS)
    q_width = heads * HEAD_SIZE
    width = q_width + 2 * HEAD_SIZE
    share_rows = MODEL_WIDTH // (ctx_count * shards)

    halves = w_down.reshape(down_depth, experts, MODEL_WIDTH // FF, FF)
    expert_rows = jnp.concatenate(
        [
            jnp.transpose(w_gate, (1, 0, 2)),
            jnp.transpose(w_up, (1, 0, 2)),
            jnp.transpose(halves, (1, 2, 0, 3)).reshape(experts, -1, FF),
        ],
        axis=1,
    )
    grouped = jnp.concatenate(
        [
            w_query.reshape(depth, shards, q_width),
            jnp.repeat(key_weight.reshape(depth, KEY_VALUE_HEADS, HEAD_SIZE), copies, axis=1),
            jnp.repeat(value_weight.reshape(depth, KEY_VALUE_HEADS, HEAD_SIZE), copies, axis=1),
        ],
        axis=2,
    )
    small = jnp.concatenate(
        [
            jnp.tile(norm_attn, MODEL_WIDTH // depth)[None, :],
            jnp.tile(norm_ffn, MODEL_WIDTH // depth)[None, :],
            w_router.reshape(-1, MODEL_WIDTH),
        ],
        axis=0,
    )
    small = jnp.pad(small, ((0, 16 - small.shape[0]), (0, 0)))
    chips = shards // 2
    token_parts = relay_chips(jnp.concatenate([tokens, small], axis=0))
    columns = all_to_all(jnp.transpose(grouped, (1, 0, 2))).reshape(MODEL_WIDTH, width)
    cot_parts = from_ctx(cotangent)
    token_parts, columns, cot_parts = meet(token_parts, columns, cot_parts)
    positions = ctx * rows + jnp.arange(rows, dtype=jnp.int32)
    cosine, sine = rotary_tables(positions)
    split = 1
    weights_first = lax.all_gather(expert_rows[:split], "shard", axis=0, tiled=False)
    weights_last = lax.all_gather(
        tie(expert_rows[split:], weights_first, token_parts), "shard", axis=0, tiled=False
    )

    place = jnp.stack([shard // 2, shard % 2]).astype(jnp.int32)
    normed, queries, key_values, small = project(
        token_parts,
        [send_core(part) for part in token_parts],
        columns,
        cosine,
        sine,
        place,
        tile,
        depth,
    )
    gain_attn = small[:, 0, :depth].reshape(MODEL_WIDTH).astype(F32)
    gain_ffn = small[:, 1, :depth].reshape(MODEL_WIDTH).astype(F32)
    router_rows = w_router.size // MODEL_WIDTH
    router_wide = small[:, 2 : 2 + router_rows].reshape(MODEL_WIDTH, expert_count).astype(F32)
    kv_parts = from_ctx(key_values)
    out_parts = spread_start(tie(w_out, key_values))
    outcome, outcome_wide, level = attend(queries, kv_parts, ctx_index, tile)
    outcome, out_parts = meet(outcome, out_parts)
    out_ctx = spread_ctx(spread_join(out_parts))
    out_other = [send_core(part) for part in out_ctx]

    chosen = choices[:, :, None] == jnp.arange(expert_count, dtype=jnp.int32)[None, None, :]
    rank = jnp.min(jnp.where(chosen, priority[:, :, None], UNCHOSEN), axis=1)
    earlier = jnp.sum((rank.T[:, None, :] < rank.T[:, :, None]).astype(F32), axis=2).T
    named = rank < UNCHOSEN
    kept = named & (earlier < capacity)

    attended = all_to_all(outcome).reshape(MODEL_WIDTH, tile)
    attended, out_ctx, out_other = meet(attended, out_ctx, out_other)
    out_full = spread_end(out_ctx, out_other)
    inputs = tokens.astype(F32)
    inverse_attn = rms_scale(inputs)
    branch = dot(attended, out_full, ((0,), (0,)))
    middle = inputs + RESIDUAL_SCALE * branch
    inverse_ffn = rms_scale(middle)
    normed_ffn = middle * inverse_ffn * gain_ffn[None, :]
    logits = jnp.dot(normed_ffn, router_wide, precision=PRECISE)
    masked_logits = jnp.where(named, logits, MASKED)
    raised = jnp.where(
        named, jnp.exp(masked_logits - jnp.max(masked_logits, axis=1, keepdims=True)), 0.0
    )
    gate_weights = raised / jnp.sum(raised, axis=1, keepdims=True)
    kept_weights = jnp.where(kept, gate_weights, 0.0)
    high = kept_weights.astype(BF16)
    low = (kept_weights - high.astype(F32)).astype(BF16)
    spare = ((0, 0), (0, LANES // 2 - expert_count))
    packet = jnp.concatenate([normed_ffn.astype(BF16), jnp.pad(high, spare), jnp.pad(low, spare)], 1)
    x_parts = from_ctx(packet)
    grouped_rows = tie(grouped.reshape(depth, shards * width), packet)
    own_weights = lax.ppermute(
        lax.dynamic_slice_in_dim(
            grouped_rows, ctx * share_rows, share_rows, 0
        ),
        ("ctx", "shard"),
        [(j * shards + i, ctx_count * i + j) for j in range(ctx_count) for i in range(shards)],
    )
    x_parts, own_weights = meet(x_parts, own_weights)
    carry, grads_first = run_experts(
        x_parts, cot_parts, weights_first, ctx_index, experts, 0, [], False
    )
    gin_parts, mix_parts, grads_last = run_experts(
        x_parts, cot_parts, weights_last, ctx_index, experts, split, carry, True
    )
    back = to_ctx(gin_parts)
    share_first = lax.psum_scatter(grads_first, "shard", scatter_dimension=0, tiled=False)
    share_last = lax.psum_scatter(
        tie(grads_last, share_first, back), "shard", scatter_dimension=0, tiled=False
    )
    upstream = cotangent.astype(F32)
    grad_gates = jnp.where(
        kept,
        back[:, MODEL_WIDTH : MODEL_WIDTH + expert_count]
        + back[:, MODEL_WIDTH + LANES // 2 : MODEL_WIDTH + LANES // 2 + expert_count],
        0.0,
    )
    grad_logits = gate_weights * (
        grad_gates - jnp.sum(gate_weights * grad_gates, axis=1, keepdims=True)
    )
    grad_normed_ffn = back[:, :MODEL_WIDTH] + jnp.einsum(
        "te,de->td", grad_logits, router_wide, precision=PRECISE
    )
    grad_middle = upstream + norm_back(grad_normed_ffn, middle, inverse_ffn, gain_ffn)
    grad_branch = (RESIDUAL_SCALE * grad_middle).astype(BF16)
    grad_attended = dot(out_full, grad_branch, ((1,), (1,))).astype(BF16)
    grad_heads = all_to_all(grad_attended.reshape(shards, q_width, tile))

    grad_router = jnp.einsum("te,td->ed", grad_logits, normed_ffn, precision=PRECISE)
    grad_norm_ffn = jnp.sum(grad_normed_ffn * middle * inverse_ffn, axis=0)[None, :]
    fine = jnp.concatenate([grad_router, grad_norm_ffn], axis=0)
    fine_high = fine.astype(BF16)
    fine_low = (fine - fine_high.astype(F32)).astype(BF16)
    fine_rows = expert_count + 1
    fine = jnp.concatenate(
        [fine_high, fine_low, jnp.zeros((LANES - 2 * fine_rows, MODEL_WIDTH), BF16)], axis=0
    ).T
    block = MODEL_WIDTH // ctx_count
    early_parts = []
    for k in range(ctx_count):
        first = ((ctx - k) % ctx_count) * block
        part = lax.dynamic_slice_in_dim(attended, first, block, 0)
        early_parts.append(dot(part, grad_branch).astype(BF16))
    grad_heads, early_parts = meet(grad_heads, early_parts)
    early_parts = from_later(early_parts)

    out = attend_back(queries, grad_heads, outcome_wide, level, kv_parts, ctx_index)
    early_parts, gq, kv_out = meet(early_parts, out[0], out[1:])
    kv_back = from_later(kv_out)
    early = add_up(early_parts).astype(BF16).reshape(chips, 2, -1, MODEL_WIDTH)
    mine = lax.dynamic_index_in_dim(early, shard % 2, 1, keepdims=False)
    theirs = send_core(lax.dynamic_index_in_dim(early, 1 - shard % 2, 1, keepdims=False))
    out_back, _ = halve_chips((mine.astype(F32) + theirs.astype(F32)).astype(BF16))
    mix_back = from_later(tie(mix_parts, kv_back))
    at = jnp.stack([ctx, shard % 2]).astype(jnp.int32)
    own, other, late_parts = tail(
        gq, cosine, sine, normed, columns, fine, kv_back, at, tile
    )
    chip_sum = (own.astype(F32) + send_core(other).astype(F32)).astype(BF16)
    token_back, _ = halve_chips(chip_sum)
    late = to_ctx(tie(late_parts, chip_sum)).astype(BF16)
    late = all_to_all(late.reshape(shards, share_rows, -1))
    expert_grads = unpack(share_first, share_last, depth, down_depth, MODEL_WIDTH)
    block_out = (middle + RESIDUAL_SCALE * add_up(mix_back)).astype(BF16)
    late, token_back, out_back, block_out, expert_grads = meet(
        late, token_back, out_back, block_out, expert_grads
    )
    first_row = (ctx * shards + shard) * share_rows
    own_gain = lax.dynamic_slice_in_dim(gain_attn, first_row, share_rows, 0)[:, None]
    grad_tokens, grad_query, grad_key, grad_value, grad_out, grad_gain, grad_gain_ffn, grad_router = (
        finish(
            late, own_weights, own_gain, grad_middle, tokens, inverse_attn, gain_attn,
            token_back + out_back,
            q_width, copies, expert_count
        )
    )
    return (
        block_out,
        grad_tokens,
        grad_query,
        grad_key,
        grad_value,
        grad_out,
        grad_gain[0],
        grad_gain_ffn[0],
        grad_router.T,
        *expert_grads,
    )


def solution(mesh):
    placed = (
        P(("ctx", "shard"), None),
        P("shard", None),
        P("shard", None),
        P("shard", None),
        P("shard", None),
        P("shard"),
        P("shard"),
        P("shard", None),
        P("shard", "ctx", None),
        P("shard", "ctx", None),
        P("shard", "ctx", None),
        P(("ctx", "shard"), None),
        P(("ctx", "shard"), None),
        P(("ctx", "shard"), None),
    )
    return jax.shard_map(
        local,
        mesh=mesh,
        in_specs=placed,
        out_specs=(
            P(("ctx", "shard"), None),
            P(("ctx", "shard"), None),
            P(("ctx", "shard"), None),
            P(("ctx", "shard"), None),
            P(("ctx", "shard"), None),
            P(("ctx", "shard"), None),
            P(("ctx", "shard")),
            P(("ctx", "shard")),
            P(("ctx", "shard"), None),
            P("shard", "ctx", None),
            P("shard", "ctx", None),
            P("shard", "ctx", None),
        ),
        check_vma=False,
    )
```
